256 devices in a mesh: pairs: 32 (over x, z), tm: 8 (over y, core).
Axes of the slice: x: 4, y: 4, z: 8, core: 2. Of those that a mesh axis runs over, the one named last changes fastest.
Arguments:
- traces: float32 [16, 2048, 6144], P('tm', 'pairs'), may hold values from -64 to 64
- station_slot: int32 [2048], replicated, may hold values from 0 to 2047, as said below
- pair_stations: int32 [2048, 2], P('pairs'), may hold values from 0 to 2047, as said below
Outputs:
- correlation_stack: float32 [2048, 2048], P('tm', 'pairs')
The draws below stay inside these ranges and needn't reach their ends.
Inputs may be any that keep to these rules, and one draw needn't show every extreme that they name: `station_slot`: A permutation: rows r * 64 to (r + 1) * 64 - 1 of traces are the stations of owner r. `pair_stations`: in each block of 64 pairs (the pairs of one device), at most 8 of the 128 pair ends name stations whose station_slot // 64 is one value, and in every block one value is named by exactly 8 ends. A pair may name one station twice.
All inputs are finite; a program needn't handle non-finite values.
Results may differ from the reference program's by a relative error of at most 0.011.
Values may be sent and summed in bfloat16 or wider, within the bound.
No kernel may reach another device: no remote copies, remote signals or barrier semaphores. Data moves between devices by JAX's collectives and lax.ppermute only.
A program may use at most 64 MiB of HBM per device.

```python
import math
import jax
import jax.numpy as jnp
from jax import lax

NS = 6144
F = 1536
FLO = 32
LAG = 1024
S_DEV = 64
P_DEV = 64
STATIONS = 2048
WINDOWS = 16
CAP = 8


def slot_order(key):
    return jax.random.permutation(jax.random.fold_in(key, 11), STATIONS).astype(jnp.int32)


def draw_station_slot(key, part):
    return slot_order(key)


def draw_pair_stations(key, part):
    permuted = slot_order(key)
    slot_station = jnp.zeros((STATIONS,), jnp.int32).at[permuted].set(jnp.arange(STATIONS, dtype=jnp.int32))
    blocks = STATIONS // S_DEV
    end_total = 2 * P_DEV
    draw_key = jax.random.fold_in(key, 23)
    busiest = jax.random.randint(jax.random.fold_in(draw_key, 1), (blocks,), 0, blocks)

    def one_block(block_index):
        block_key = jax.random.fold_in(draw_key, 100 + block_index)
        picked = jax.random.permutation(jax.random.fold_in(block_key, 1), (blocks - 1) * CAP)[:end_total - CAP]
        others = (picked // CAP).astype(jnp.int32)
        others = others + (others >= busiest[block_index]).astype(jnp.int32)
        owners = jnp.concatenate([jnp.full((CAP,), busiest[block_index], jnp.int32), others])
        owners = jax.random.permutation(jax.random.fold_in(block_key, 2), owners)
        local_rows = jax.random.randint(jax.random.fold_in(block_key, 3), (end_total,), 0, S_DEV)
        return owners * S_DEV + local_rows
    slot_ids = jax.vmap(one_block)(jnp.arange(blocks, dtype=jnp.int32))
    return slot_station[slot_ids.reshape(blocks * P_DEV, 2)]


def draw_traces(key, part):
    full_shape = (WINDOWS, STATIONS, NS)
    amplitude = jnp.exp(jax.random.uniform(jax.random.fold_in(key, 5), (1, STATIONS, 1), minval=0.0, maxval=math.log(10.0)))
    samples = jnp.clip(jax.random.normal(jax.random.fold_in(key, 6), full_shape), -6.0, 6.0)
    return (samples * amplitude).astype(jnp.float32)


def setup_inputs(seed: int = 0) -> dict:
    streams_of = jax.random.split(jax.random.key(seed), 4)
    return {
        "traces": draw_traces(jax.random.fold_in(streams_of[3], 71), 0),
        "station_slot": draw_station_slot(jax.random.fold_in(streams_of[3], 71), 0),
        "pair_stations": draw_pair_stations(jax.random.fold_in(streams_of[3], 71), 0),
    }


two_pi = 6.283185307179586

def tapered_rows(traces):
    length = traces.shape[-1]
    sample_times = lax.iota(jnp.int32, length).astype(jnp.float32)
    hann_window = 0.5 - 0.5 * jnp.cos((sample_times + 0.5) * (two_pi / length))
    centred = traces - lax.optimization_barrier(jnp.mean(traces, axis=-1, keepdims=True))
    return (centred * hann_window).astype(jnp.bfloat16)

def forward_table(first_row, row_count, length, first_bin, bins):
    sample_times = first_row + lax.iota(jnp.int32, row_count)
    frequencies = first_bin + lax.iota(jnp.int32, bins)
    phases = sample_times[:, None] * frequencies[None, :] % length
    angles = phases.astype(jnp.float32) * (two_pi / length)
    return jnp.concatenate([jnp.cos(angles), -jnp.sin(angles)], axis=1).astype(jnp.bfloat16)

def whiten(spectrum, bins):
    real_part = spectrum[..., :bins]
    imag_part = spectrum[..., bins:]
    energy = real_part * real_part + imag_part * imag_part
    water_level = lax.optimization_barrier(jnp.mean(energy, axis=-1, keepdims=True))
    scaling = lax.rsqrt(energy + 0.1 * water_level + 1e-06)
    return jnp.concatenate([real_part * scaling, imag_part * scaling], axis=-1).astype(jnp.bfloat16)

def cross_spectra(left_ends, right_ends, bins):
    left_real = left_ends[..., :bins].astype(jnp.float32)
    left_imag = left_ends[..., bins:].astype(jnp.float32)
    right_real = right_ends[..., :bins].astype(jnp.float32)
    right_imag = right_ends[..., bins:].astype(jnp.float32)
    return jnp.concatenate([left_real * right_real + left_imag * right_imag, left_imag * right_real - left_real * right_imag], axis=-1)

def lag_block(stacked, first_row, row_count, first_bin, bins, length, half_span):
    lag_values = first_row + lax.iota(jnp.int32, row_count) - half_span
    frequencies = first_bin + lax.iota(jnp.int32, bins)
    phases = lag_values[:, None] * frequencies[None, :] % length
    angles = phases.astype(jnp.float32) * (two_pi / length)
    lag_table = jnp.concatenate([jnp.cos(angles), -jnp.sin(angles)], axis=1)
    return lax.dot_general(lag_table, stacked, (((1,), (1,)), ((), ())), precision=lax.Precision.HIGHEST, preferred_element_type=jnp.float32)

def reference(traces, station_slot, pair_stations):
    length = traces.shape[2]
    left_slots = station_slot[pair_stations[:, 0]]
    right_slots = station_slot[pair_stations[:, 1]]
    full_table = forward_table(0, length, length, FLO, F)

    def one_window(running, window):
        tapered = tapered_rows(window)
        spectrum = jnp.dot(tapered, full_table, preferred_element_type=jnp.float32)
        whitened = whiten(spectrum, F)
        return (running + cross_spectra(whitened[left_slots], whitened[right_slots], F), None)
    stacked, unused = lax.scan(one_window, jnp.zeros((pair_stations.shape[0], 2 * F), jnp.float32), traces)
    normalizer = 1.0 / math.sqrt(F * traces.shape[0])
    return lag_block(stacked, 0, 2 * LAG, FLO, F, length, LAG) * normalizer
```

```python
import functools
import math

import jax
import jax.numpy as jnp
import ml_dtypes
import numpy as np
from jax import lax
from jax.experimental import pallas as pl
from jax.experimental.pallas import tpu as pltpu
from jax.sharding import PartitionSpec as P

F = 1536
FLO = 32
LAG = 1024
NS = 6144
RADIX = 12
SUB = NS // RADIX
DBINS = F // RADIX
STEPS = RADIX // 2
CAP = 8
ROOT3_2 = math.sqrt(3.0) / 2.0

TURNS = [0, 6] + [turn for step in range(1, STEPS) for turn in (step, RADIX - step)]
RESIDUES = [(turn - FLO) % RADIX for turn in TURNS]


def spectrum_tables():
    sub_times = np.arange(SUB, dtype=np.int64)[:, None]
    bins = np.arange(DBINS, dtype=np.int64)[None, :]
    tables = np.zeros((STEPS, 2 * SUB, 4 * DBINS), np.float64)
    for position, residue in enumerate(RESIDUES):
        step, half = divmod(position, 2)
        phases = sub_times * (FLO + residue + RADIX * bins) % NS
        angles = phases * (2.0 * np.pi / NS)
        cos_part, sin_part = np.cos(angles), np.sin(angles)
        columns = slice(half * 2 * DBINS, half * 2 * DBINS + DBINS)
        columns_imag = slice(half * 2 * DBINS + DBINS, (half + 1) * 2 * DBINS)
        if step == 0:
            rows = slice(half * SUB, (half + 1) * SUB)
            tables[step, rows, columns] = cos_part
            tables[step, rows, columns_imag] = -sin_part
        else:
            sign = 1.0 if half == 0 else -1.0
            tables[step, :SUB, columns] = cos_part
            tables[step, SUB:, columns] = sign * sin_part
            tables[step, :SUB, columns_imag] = -sin_part
            tables[step, SUB:, columns_imag] = sign * cos_part
    return tables.astype(ml_dtypes.bfloat16)


def hann_window():
    times = np.arange(NS, dtype=np.float64)
    return (0.5 - 0.5 * np.cos((times + 0.5) * (2.0 * np.pi / NS))).astype(np.float32)[None, :]


def lag_tables(normalizer):
    bins = np.arange(DBINS, dtype=np.int64)[:, None]
    sub_lags = np.arange(SUB, dtype=np.int64)[None, :]
    angles = (bins * sub_lags % SUB) * (2.0 * np.pi / SUB)
    cos_part, sin_part = np.cos(angles), np.sin(angles)
    inner = np.block([[cos_part, sin_part], [-sin_part, cos_part]]).astype(ml_dtypes.bfloat16)
    lags = np.arange(2 * LAG, dtype=np.int64)[None, :] - LAG
    first_bins = FLO + np.array(RESIDUES, dtype=np.int64)[:, None]
    outer_angles = (first_bins * lags % NS) * (2.0 * np.pi / NS)
    outer = np.stack([np.cos(outer_angles), -np.sin(outer_angles)], axis=1) * normalizer
    return inner, outer.reshape(2 * RADIX, 2 * LAG).astype(np.float32)


def request_kernel(slots_ref, pairs_ref, wanted_ref, places_ref):
    ends = 2 * pairs_ref.shape[1]
    rows = slots_ref.shape[0]
    windows = wanted_ref.shape[1] // CAP
    stations = wanted_ref.shape[2] // windows
    owners_count = wanted_ref.shape[0]
    sublane = lax.broadcasted_iota(jnp.int32, (ends, ends), 0)
    lane = lax.broadcasted_iota(jnp.int32, (ends, ends), 1)
    end_row = jnp.concatenate([pairs_ref[0:1, :], pairs_ref[1:2, :]], axis=1)
    end_column = jnp.sum(
        jnp.where(sublane == lane, jnp.broadcast_to(end_row, (ends, ends)), 0).astype(jnp.float32),
        axis=1,
        keepdims=True,
    ).astype(jnp.int32)
    lanes = lax.broadcasted_iota(jnp.int32, (ends, 128), 1)
    found = jnp.zeros((ends, 128), jnp.int32)
    for row in range(rows):
        slot_row = slots_ref[row : row + 1, :]
        found = found + jnp.where(end_column == lanes + row * 128, slot_row, 0)
    slot_column = jnp.sum(found.astype(jnp.float32), axis=1, keepdims=True).astype(jnp.int32)
    slot_square = jnp.broadcast_to(slot_column, (ends, ends))
    slot_row = jnp.sum(jnp.where(sublane == lane, slot_square, 0).astype(jnp.float32), axis=0, keepdims=True).astype(
        jnp.int32
    )
    owner_column = slot_column // stations
    owner_row = slot_row // stations
    local_row = slot_row - owner_row * stations
    same_owner = owner_column == owner_row
    rank_row = jnp.sum(
        jnp.where(same_owner & (sublane < lane), 1.0, 0.0), axis=0, keepdims=True
    ).astype(jnp.int32)
    rank_column = jnp.sum(
        jnp.where(same_owner & (lane < sublane), 1.0, 0.0), axis=1, keepdims=True
    ).astype(jnp.int32)
    places_ref[...] = jnp.broadcast_to(owner_column * (windows * CAP) + rank_column, places_ref.shape)
    owner_ids = lax.broadcasted_iota(jnp.int32, (owners_count, ends), 0)
    owned = owner_ids == owner_row
    column_ids = lax.broadcasted_iota(jnp.int32, (owners_count, windows * stations), 1)
    for rank in range(CAP):
        hit = owned & (rank_row == rank)
        row_wanted = jnp.sum(
            jnp.where(hit, local_row, 0).astype(jnp.float32), axis=1, keepdims=True
        ).astype(jnp.int32)
        for window in range(windows):
            picked = jnp.where(column_ids == row_wanted + window * stations, 1.0, 0.0)
            wanted_ref[:, window * CAP + rank, :] = picked


def requests(station_slot, pair_stations, blocks, windows, stations):
    pair_count = pair_stations.shape[0]
    return pl.pallas_call(
        request_kernel,
        out_shape=(
            jax.ShapeDtypeStruct((blocks, windows * CAP, windows * stations), jnp.float32),
            jax.ShapeDtypeStruct((2 * pair_count, 128), jnp.int32),
        ),
        name="requests",
    )(station_slot.reshape(-1, 128), pair_stations.T)


def spectrum_kernel(traces_ref, hann_ref, table_ref, out_ref, parts_ref, spectrum_ref):
    step = pl.program_id(0)
    row_count = traces_ref.shape[0]

    @pl.when(step == 0)
    def _():
        def one_group(group, carry):
            rows = pl.ds(pl.multiple_of(group * 16, 16), 16)
            partial_sum = traces_ref[rows, 0:128]
            for tile in range(1, NS // 128):
                partial_sum = partial_sum + traces_ref[rows, tile * 128 : (tile + 1) * 128]
            mean = jnp.sum(partial_sum, axis=1, keepdims=True) * (1.0 / NS)
            for tile in range(SUB // 128):
                x = []
                for block in range(RADIX):
                    columns = slice(block * SUB + tile * 128, block * SUB + (tile + 1) * 128)
                    x.append((traces_ref[rows, columns] - mean) * hann_ref[:, columns])
                u = [None] + [x[a] + x[RADIX - a] for a in range(1, 6)]
                v = [None] + [x[a] - x[RADIX - a] for a in range(1, 6)]
                e0, o0 = x[0] + x[6], x[0] - x[6]
                p, q = u[1] + u[5], u[2] + u[4]
                pd, qd = u[1] - u[5], u[2] - u[4]
                m, n = v[1] - v[5], v[2] - v[4]
                ms, ns = v[1] + v[5], v[2] + v[4]
                half_pq, half_diff = 0.5 * (p + q), 0.5 * (p - q)
                e_plus, e_minus = e0 + u[3], e0 - u[3]
                base = o0 + 0.5 * qd
                side = ROOT3_2 * pd
                imag_base = 0.5 * ms + v[3]
                imag_side = ROOT3_2 * ns
                parts = [
                    (e_plus + (p + q), e_minus - (p - q)),
                    (base + side, -(imag_base + imag_side)),
                    (e_minus + half_diff, -ROOT3_2 * (m + n)),
                    (o0 - qd, v[3] - ms),
                    (e_plus - half_pq, -ROOT3_2 * (m - n)),
                    (base - side, imag_side - imag_base),
                ]
                for index, (first, second) in enumerate(parts):
                    start = index * 2 * SUB + tile * 128
                    parts_ref[rows, start : start + 128] = first.astype(jnp.bfloat16)
                    parts_ref[rows, start + SUB : start + SUB + 128] = second.astype(jnp.bfloat16)
            return carry

        lax.fori_loop(0, row_count // 16, one_group, 0)

    for index in range(STEPS):

        @pl.when(step == index)
        def _(index=index):
            spectrum_ref[:, index * 512 : (index + 1) * 512] = jnp.dot(
                parts_ref[:, index * 1024 : (index + 1) * 1024],
                table_ref[0],
                preferred_element_type=jnp.float32,
            )

    @pl.when(step == STEPS - 1)
    def _():
        def one_group(group, carry):
            rows = pl.ds(pl.multiple_of(group * 16, 16), 16)
            total = jnp.zeros((16, 128), jnp.float32)
            for residue in range(RADIX):
                real_part = spectrum_ref[rows, residue * 256 : residue * 256 + 128]
                imag_part = spectrum_ref[rows, residue * 256 + 128 : residue * 256 + 256]
                total = total + (real_part * real_part + imag_part * imag_part)
            water_level = jnp.sum(total, axis=1, keepdims=True) * (1.0 / F)
            floor = 0.1 * water_level + 1e-06
            for residue in range(RADIX):
                real_part = spectrum_ref[rows, residue * 256 : residue * 256 + 128]
                imag_part = spectrum_ref[rows, residue * 256 + 128 : residue * 256 + 256]
                energy = real_part * real_part + imag_part * imag_part
                scaling = lax.rsqrt(energy + floor)
                out_ref[rows, residue * 256 : residue * 256 + 128] = (real_part * scaling).astype(jnp.bfloat16)
                out_ref[rows, residue * 256 + 128 : residue * 256 + 256] = (imag_part * scaling).astype(jnp.bfloat16)
            return carry

        lax.fori_loop(0, row_count // 16, one_group, 0)


def whitened_spectra(traces):
    rows = traces.shape[0]
    return pl.pallas_call(
        spectrum_kernel,
        out_shape=jax.ShapeDtypeStruct((rows, 2 * F), jnp.bfloat16),
        grid_spec=pltpu.PrefetchScalarGridSpec(
            num_scalar_prefetch=0,
            grid=(STEPS,),
            in_specs=[
                pl.BlockSpec((rows, NS), lambda s: (0, 0)),
                pl.BlockSpec((1, NS), lambda s: (0, 0)),
                pl.BlockSpec((1, 2 * SUB, 4 * DBINS), lambda s: (s, 0, 0)),
            ],
            out_specs=pl.BlockSpec((rows, 2 * F), lambda s: (0, 0)),
            scratch_shapes=[
                pltpu.VMEM((rows, NS), jnp.bfloat16),
                pltpu.VMEM((rows, 2 * F), jnp.float32),
            ],
        ),
        compiler_params=pltpu.CompilerParams(
            dimension_semantics=("arbitrary",), vmem_limit_bytes=48 << 20
        ),
        cost_estimate=pl.CostEstimate(
            flops=2 * rows * STEPS * 1024 * 512, bytes_accessed=11_000_000, transcendentals=rows * F
        ),
        name="whitened_spectra",
    )(traces, jnp.asarray(hann_window()), jnp.asarray(spectrum_tables()))


C_STEPS = 4
C_RES = RADIX // C_STEPS


def lag_kernel(places_ref, received_ref, inner_ref, outer_ref, out_ref, select_ref, sums_ref):
    step = pl.program_id(0)
    slots = received_ref.shape[0]
    ends = places_ref.shape[0]
    pairs = ends // 2
    windows = select_ref.shape[0] // ends

    @pl.when(step == 0)
    def _():
        lanes = lax.broadcasted_iota(jnp.int32, (ends, 128), 1)
        places = places_ref[...]
        for window in range(windows):
            for tile in range(slots // 128):
                hit = jnp.where(places + window * CAP == lanes + tile * 128, 1.0, 0.0)
                select_ref[window * ends : (window + 1) * ends, tile * 128 : (tile + 1) * 128] = hit.astype(
                    jnp.bfloat16
                )
        sums_ref[...] = jnp.zeros_like(sums_ref)

    picked = jnp.dot(select_ref[...], received_ref[...], preferred_element_type=jnp.float32)
    stacked = []
    for index in range(C_RES):
        real_sum = imag_sum = None
        for window in range(windows):
            left = slice(window * ends, window * ends + pairs)
            right = slice(window * ends + pairs, (window + 1) * ends)
            left_real = picked[left, index * 256 : index * 256 + 128]
            left_imag = picked[left, index * 256 + 128 : index * 256 + 256]
            right_real = picked[right, index * 256 : index * 256 + 128]
            right_imag = picked[right, index * 256 + 128 : index * 256 + 256]
            real_term = left_real * right_real + left_imag * right_imag
            imag_term = left_imag * right_real - left_real * right_imag
            real_sum = real_term if real_sum is None else real_sum + real_term
            imag_sum = imag_term if imag_sum is None else imag_sum + imag_term
        stacked.append(jnp.concatenate([real_sum, imag_sum], axis=1))
    stacked = jnp.concatenate(stacked, axis=0).astype(jnp.bfloat16)
    turned = jnp.dot(stacked, inner_ref[...], preferred_element_type=jnp.float32)
    outer = outer_ref[0]
    for period in range(2 * LAG // SUB):
        for tile in range(SUB // 128):
            lag_columns = slice(period * SUB + tile * 128, period * SUB + (tile + 1) * 128)
            total = sums_ref[:, lag_columns]
            for index in range(C_RES):
                rows = slice(index * pairs, (index + 1) * pairs)
                total = total + outer[2 * index : 2 * index + 1, lag_columns] * turned[rows, tile * 128 : (tile + 1) * 128]
                total = total + outer[2 * index + 1 : 2 * index + 2, lag_columns] * turned[
                    rows, SUB + tile * 128 : SUB + (tile + 1) * 128
                ]
            sums_ref[:, lag_columns] = total

    @pl.when(step == C_STEPS - 1)
    def _():
        share = out_ref.shape[2]
        for part in range(out_ref.shape[0]):
            out_ref[part] = sums_ref[:, part * share : (part + 1) * share].astype(out_ref.dtype)


def lag_sums(places, received, parts, normalizer):
    ends = places.shape[0]
    slots = received.shape[0]
    pairs = ends // 2
    windows = slots // (32 * CAP)
    inner, outer = lag_tables(normalizer)
    return pl.pallas_call(
        lag_kernel,
        out_shape=jax.ShapeDtypeStruct((parts, pairs, 2 * LAG // parts), jnp.bfloat16),
        grid_spec=pltpu.PrefetchScalarGridSpec(
            num_scalar_prefetch=0,
            grid=(C_STEPS,),
            in_specs=[
                pl.BlockSpec((ends, 128), lambda s: (0, 0)),
                pl.BlockSpec((slots, 256 * C_RES), lambda s: (0, s)),
                pl.BlockSpec((2 * DBINS, 2 * SUB), lambda s: (0, 0)),
                pl.BlockSpec((1, 2 * C_RES, 2 * LAG), lambda s: (s, 0, 0)),
            ],
            out_specs=pl.BlockSpec((parts, pairs, 2 * LAG // parts), lambda s: (0, 0, 0)),
            scratch_shapes=[
                pltpu.VMEM((windows * ends, slots), jnp.bfloat16),
                pltpu.VMEM((pairs, 2 * LAG), jnp.float32),
            ],
        ),
        compiler_params=pltpu.CompilerParams(
            dimension_semantics=("arbitrary",), vmem_limit_bytes=48 << 20
        ),
        cost_estimate=pl.CostEstimate(
            flops=2 * windows * ends * slots * 2 * F, bytes_accessed=5_000_000, transcendentals=0
        ),
        name="lag_sums",
    )(places, received, jnp.asarray(inner), jnp.asarray(outer.reshape(C_STEPS, 2 * C_RES, 2 * LAG)))


def total_kernel(parts_ref, out_ref):
    total = parts_ref[0].astype(jnp.float32)
    for part in range(1, parts_ref.shape[0]):
        total = total + parts_ref[part].astype(jnp.float32)
    out_ref[...] = total


def window_total(parts):
    return pl.pallas_call(
        total_kernel,
        out_shape=jax.ShapeDtypeStruct(parts.shape[1:], jnp.float32),
        name="window_total",
    )(parts).T


def on_device(traces, station_slot, pair_stations):
    window_count, station_count, length = traces.shape
    blocks = lax.axis_size("pairs")
    lag_parts = lax.axis_size("tm")
    normalizer = 1.0 / math.sqrt(F * window_count * lag_parts)
    wanted, places = requests(station_slot, pair_stations, blocks, window_count, station_count)
    picks = lax.all_to_all(wanted.astype(jnp.bfloat16), "pairs", split_axis=0, concat_axis=0, tiled=True)
    whitened = whitened_spectra(traces.reshape(window_count * station_count, length))
    rows = jnp.dot(
        picks.reshape(blocks * window_count * CAP, window_count * station_count),
        whitened,
        preferred_element_type=jnp.bfloat16,
    )
    received = lax.all_to_all(
        rows.reshape(blocks, window_count * CAP, 2 * F), "pairs", split_axis=0, concat_axis=0, tiled=True
    )
    sums = lag_sums(places, received.reshape(blocks * window_count * CAP, 2 * F), lag_parts, normalizer)
    parts = lax.all_to_all(sums, "tm", split_axis=0, concat_axis=0, tiled=True)
    return window_total(parts)


def solution(mesh):
    in_specs = (P("tm", "pairs", None), P(), P("pairs", None))
    out_specs = P("tm", "pairs")
    return jax.shard_map(
        on_device, mesh=mesh, in_specs=in_specs, out_specs=out_specs, check_vma=False
    )
```

```python
import math

import jax
import jax.numpy as jnp
import ml_dtypes
import numpy as np
from jax import lax
from jax.experimental import pallas as pl
from jax.experimental.pallas import tpu as pltpu
from jax.sharding import PartitionSpec as P

F = 1536
FLO = 32
LAG = 1024
NS = 6144
RADIX = 12
SUB = NS // RADIX
DBINS = F // RADIX
STEPS = RADIX // 2
CAP = 8
ROOT3_2 = math.sqrt(3.0) / 2.0

TURNS = [0, 6] + [turn for step in range(1, STEPS) for turn in (step, RADIX - step)]
RESIDUES = [(turn - FLO) % RADIX for turn in TURNS]


def spectrum_tables():
    sub_times = np.arange(SUB, dtype=np.int64)[:, None]
    bins = np.arange(DBINS, dtype=np.int64)[None, :]
    angles = (sub_times * bins % SUB) * (2.0 * np.pi / SUB)
    cos_part, sin_part = np.cos(angles), np.sin(angles)
    inner = np.block([[cos_part, -sin_part], [sin_part, cos_part]]).astype(ml_dtypes.bfloat16)
    first_bins = FLO + np.array(RESIDUES, dtype=np.int64)[:, None]
    turn_angles = (first_bins * sub_times[:, 0][None, :] % NS) * (2.0 * np.pi / NS)
    turns = np.stack([np.cos(turn_angles), np.sin(turn_angles)], axis=1)
    return inner, turns.reshape(2 * RADIX, SUB).astype(np.float32)


def hann_window():
    times = np.arange(NS, dtype=np.float64)
    return (0.5 - 0.5 * np.cos((times + 0.5) * (2.0 * np.pi / NS))).astype(np.float32)[None, :]


def lag_tables(normalizer):
    bins = np.arange(DBINS, dtype=np.int64)[:, None]
    sub_lags = np.arange(SUB, dtype=np.int64)[None, :]
    angles = (bins * sub_lags % SUB) * (2.0 * np.pi / SUB)
    cos_part, sin_part = np.cos(angles), np.sin(angles)
    inner = np.block([[cos_part, sin_part], [-sin_part, cos_part]]).astype(ml_dtypes.bfloat16)
    lags = np.arange(2 * LAG, dtype=np.int64)[None, :] - LAG
    first_bins = FLO + np.array(RESIDUES, dtype=np.int64)[:, None]
    outer_angles = (first_bins * lags % NS) * (2.0 * np.pi / NS)
    outer = np.stack([np.cos(outer_angles), -np.sin(outer_angles)], axis=1) * normalizer
    return inner, outer.reshape(2 * RADIX, 2 * LAG).astype(np.float32)


def request_kernel(slots_ref, pairs_ref, wanted_ref, places_ref):
    ends = 2 * pairs_ref.shape[1]
    windows = wanted_ref.shape[1] // CAP
    stations = wanted_ref.shape[2] // windows
    owners_count = wanted_ref.shape[0]
    sublane = lax.broadcasted_iota(jnp.int32, (ends, ends), 0)
    lane = lax.broadcasted_iota(jnp.int32, (ends, ends), 1)

    def to_column(row):
        square = jnp.broadcast_to(row, (ends, ends))
        return jnp.sum(jnp.where(sublane == lane, square, 0).astype(jnp.float32), axis=1, keepdims=True)

    end_row = jnp.concatenate([pairs_ref[0:1, :], pairs_ref[1:2, :]], axis=1)
    end_column = to_column(end_row).astype(jnp.int32)
    lanes = lax.broadcasted_iota(jnp.int32, (ends, 128), 1)
    found = jnp.zeros((ends, 128), jnp.int32)
    for row in range(slots_ref.shape[0]):
        found = found + jnp.where(end_column == lanes + row * 128, slots_ref[row : row + 1, :], 0)
    slot_column = jnp.sum(found.astype(jnp.float32), axis=1, keepdims=True).astype(jnp.int32)
    slot_square = jnp.broadcast_to(slot_column, (ends, ends))
    slot_row = jnp.sum(
        jnp.where(sublane == lane, slot_square, 0).astype(jnp.float32), axis=0, keepdims=True
    ).astype(jnp.int32)
    owner_column = slot_column // stations
    owner_row = slot_row // stations
    local_row = slot_row - owner_row * stations
    same_owner = owner_column == owner_row
    rank_row = jnp.sum(
        jnp.where(same_owner & (sublane < lane), 1.0, 0.0), axis=0, keepdims=True
    ).astype(jnp.int32)
    rank_column = jnp.sum(
        jnp.where(same_owner & (lane < sublane), 1.0, 0.0), axis=1, keepdims=True
    ).astype(jnp.int32)
    places_ref[...] = jnp.broadcast_to(owner_column * (windows * CAP) + rank_column, places_ref.shape)
    owned = lax.broadcasted_iota(jnp.int32, (owners_count, ends), 0) == owner_row
    column_ids = lax.broadcasted_iota(jnp.int32, (owners_count, 1, windows * stations), 2)
    picks = [[] for _ in range(windows)]
    for rank in range(CAP):
        hit = owned & (rank_row == rank)
        row_wanted = jnp.sum(
            jnp.where(hit, local_row, 0).astype(jnp.float32), axis=1, keepdims=True
        ).astype(jnp.int32)
        for window in range(windows):
            column = (row_wanted + window * stations)[:, :, None]
            picks[window].append(jnp.where(column_ids == column, 1.0, 0.0))
    wanted_ref[...] = jnp.concatenate(sum(picks, []), axis=1).astype(jnp.bfloat16)


def requests(station_slot, pair_stations, blocks, windows, stations):
    pair_count = pair_stations.shape[0]
    return pl.pallas_call(
        request_kernel,
        out_shape=(
            jax.ShapeDtypeStruct((blocks, windows * CAP, windows * stations), jnp.bfloat16),
            jax.ShapeDtypeStruct((2 * pair_count, 128), jnp.int32),
        ),
        name="requests",
    )(station_slot.reshape(-1, 128), pair_stations.T)


def spectrum_kernel(traces_ref, hann_ref, turns_ref, table_ref, out_ref, *scratch):
    count = len(scratch) // 2
    row_count = traces_ref.shape[0] // count
    tables = (hann_ref, turns_ref, table_ref)
    for part in range(count):
        transform_rows(part * row_count, row_count, traces_ref, *tables, out_ref, *scratch[2 * part : 2 * part + 2])


def transform_rows(
    base_row, row_count, traces_ref, hann_ref, turns_ref, table_ref, out_ref, parts_ref, spectrum_ref
):

    def one_group(group):
        first = group * 16
        rows = pl.ds(base_row + first, 16)
        partial_sum = traces_ref[rows, 0:128]
        for tile in range(1, NS // 128):
            partial_sum = partial_sum + traces_ref[rows, tile * 128 : (tile + 1) * 128]
        mean = jnp.sum(partial_sum, axis=1, keepdims=True) * (1.0 / NS)
        for tile in range(SUB // 128):
            x = []
            for block in range(RADIX):
                columns = slice(block * SUB + tile * 128, block * SUB + (tile + 1) * 128)
                x.append((traces_ref[rows, columns] - mean) * hann_ref[:, columns])
            u = [None] + [x[a] + x[RADIX - a] for a in range(1, 6)]
            v = [None] + [x[a] - x[RADIX - a] for a in range(1, 6)]
            e0, o0 = x[0] + x[6], x[0] - x[6]
            p, q = u[1] + u[5], u[2] + u[4]
            pd, qd = u[1] - u[5], u[2] - u[4]
            m, n = v[1] - v[5], v[2] - v[4]
            ms, ns = v[1] + v[5], v[2] + v[4]
            half_pq, half_diff = 0.5 * (p + q), 0.5 * (p - q)
            e_plus, e_minus = e0 + u[3], e0 - u[3]
            base = o0 + 0.5 * qd
            side = ROOT3_2 * pd
            imag_base = 0.5 * ms + v[3]
            imag_side = ROOT3_2 * ns
            real_parts = [
                e_plus + (p + q),
                base + side,
                e_minus + half_diff,
                o0 - qd,
                e_plus - half_pq,
                base - side,
                e_minus - (p - q),
            ]
            imag_parts = [
                None,
                -(imag_base + imag_side),
                -ROOT3_2 * (m + n),
                v[3] - ms,
                -ROOT3_2 * (m - n),
                imag_side - imag_base,
                None,
            ]
            lanes = slice(tile * 128, (tile + 1) * 128)
            imag_lanes = slice(SUB + tile * 128, SUB + (tile + 1) * 128)
            for position, turn in enumerate(TURNS):
                index = min(turn, RADIX - turn)
                real_part, imag_part = real_parts[index], imag_parts[index]
                cos_turn = turns_ref[2 * position : 2 * position + 1, lanes]
                sin_turn = turns_ref[2 * position + 1 : 2 * position + 2, lanes]
                if imag_part is None:
                    turned_real = real_part * cos_turn
                    turned_imag = -(real_part * sin_turn)
                elif index == turn:
                    turned_real = real_part * cos_turn + imag_part * sin_turn
                    turned_imag = imag_part * cos_turn - real_part * sin_turn
                else:
                    turned_real = real_part * cos_turn - imag_part * sin_turn
                    turned_imag = -(imag_part * cos_turn + real_part * sin_turn)
                target = pl.ds(position * row_count + first, 16)
                parts_ref[target, lanes] = turned_real.astype(jnp.bfloat16)
                parts_ref[target, imag_lanes] = turned_imag.astype(jnp.bfloat16)

    for group in range(row_count // 16):
        one_group(group)
    spectrum_ref[...] = jnp.dot(parts_ref[...], table_ref[...], preferred_element_type=jnp.float32)

    def whiten_group(group):
        first = group * 16
        rows = pl.ds(base_row + first, 16)
        total = jnp.zeros((16, DBINS), jnp.float32)
        for position in range(RADIX):
            source = pl.ds(position * row_count + first, 16)
            real_part, imag_part = spectrum_ref[source, :DBINS], spectrum_ref[source, DBINS:]
            total = total + (real_part * real_part + imag_part * imag_part)
        water_level = jnp.sum(total, axis=1, keepdims=True) * (1.0 / F)
        floor = 0.1 * water_level + 1e-06
        for position in range(RADIX):
            source = pl.ds(position * row_count + first, 16)
            real_part, imag_part = spectrum_ref[source, :DBINS], spectrum_ref[source, DBINS:]
            scaling = lax.rsqrt(real_part * real_part + imag_part * imag_part + floor)
            start = position * 2 * DBINS
            out_ref[rows, start : start + DBINS] = (real_part * scaling).astype(jnp.bfloat16)
            out_ref[rows, start + DBINS : start + 2 * DBINS] = (imag_part * scaling).astype(jnp.bfloat16)

    for group in range(row_count // 16):
        whiten_group(group)


PART_ROWS = 32
STEP_PARTS = 2


def whitened_spectra(traces):
    total = traces.shape[0]
    rows = PART_ROWS * STEP_PARTS
    table, turns = spectrum_tables()
    scratch = [
        pltpu.VMEM((RADIX * PART_ROWS, 2 * SUB), jnp.bfloat16),
        pltpu.VMEM((RADIX * PART_ROWS, 2 * DBINS), jnp.float32),
    ]
    return pl.pallas_call(
        spectrum_kernel,
        out_shape=jax.ShapeDtypeStruct((total, 2 * F), jnp.bfloat16),
        grid_spec=pltpu.PrefetchScalarGridSpec(
            num_scalar_prefetch=0,
            grid=(total // rows,),
            in_specs=[
                pl.BlockSpec((rows, NS), lambda s: (s, 0)),
                pl.BlockSpec((1, NS), lambda s: (0, 0)),
                pl.BlockSpec((2 * RADIX, SUB), lambda s: (0, 0)),
                pl.BlockSpec((2 * SUB, 2 * DBINS), lambda s: (0, 0)),
            ],
            out_specs=pl.BlockSpec((rows, 2 * F), lambda s: (s, 0)),
            scratch_shapes=scratch * STEP_PARTS,
        ),
        compiler_params=pltpu.CompilerParams(dimension_semantics=("arbitrary",)),
        cost_estimate=pl.CostEstimate(
            flops=2 * total * RADIX * 2 * SUB * 2 * DBINS,
            bytes_accessed=5_000_000,
            transcendentals=total * F,
        ),
        name="whitened_spectra",
    )(traces, jnp.asarray(hann_window()), jnp.asarray(turns), jnp.asarray(table))


C_STEPS = 4
C_RES = RADIX // C_STEPS


def lag_kernel(places_ref, received_ref, inner_ref, outer_ref, out_ref, select_ref, sums_ref):
    step = pl.program_id(0)
    slots = received_ref.shape[0]
    ends = places_ref.shape[0]
    pairs = ends // 2
    windows = select_ref.shape[0] // ends

    @pl.when(step == 0)
    def _():
        lanes = lax.broadcasted_iota(jnp.int32, (ends, 128), 1)
        places = places_ref[...]
        for window in range(windows):
            for tile in range(slots // 128):
                hit = jnp.where(places + window * CAP == lanes + tile * 128, 1.0, 0.0)
                select_ref[window * ends : (window + 1) * ends, tile * 128 : (tile + 1) * 128] = hit.astype(
                    jnp.bfloat16
                )
        sums_ref[...] = jnp.zeros_like(sums_ref)

    picked = jnp.dot(select_ref[...], received_ref[...], preferred_element_type=jnp.float32)
    stacked = []
    for index in range(C_RES):
        real_sum = imag_sum = None
        for window in range(windows):
            left = slice(window * ends, window * ends + pairs)
            right = slice(window * ends + pairs, (window + 1) * ends)
            left_real = picked[left, index * 256 : index * 256 + 128]
            left_imag = picked[left, index * 256 + 128 : index * 256 + 256]
            right_real = picked[right, index * 256 : index * 256 + 128]
            right_imag = picked[right, index * 256 + 128 : index * 256 + 256]
            real_term = left_real * right_real + left_imag * right_imag
            imag_term = left_imag * right_real - left_real * right_imag
            real_sum = real_term if real_sum is None else real_sum + real_term
            imag_sum = imag_term if imag_sum is None else imag_sum + imag_term
        stacked.append(jnp.concatenate([real_sum, imag_sum], axis=1))
    stacked = jnp.concatenate(stacked, axis=0).astype(jnp.bfloat16)
    turned = jnp.dot(stacked, inner_ref[...], preferred_element_type=jnp.float32)
    outer = outer_ref[0]
    for period in range(2 * LAG // SUB):
        for tile in range(SUB // 128):
            lag_columns = slice(period * SUB + tile * 128, period * SUB + (tile + 1) * 128)
            total = sums_ref[:, lag_columns]
            for index in range(C_RES):
                rows = slice(index * pairs, (index + 1) * pairs)
                total = total + outer[2 * index : 2 * index + 1, lag_columns] * turned[rows, tile * 128 : (tile + 1) * 128]
                total = total + outer[2 * index + 1 : 2 * index + 2, lag_columns] * turned[
                    rows, SUB + tile * 128 : SUB + (tile + 1) * 128
                ]
            sums_ref[:, lag_columns] = total

    @pl.when(step == C_STEPS - 1)
    def _():
        share = out_ref.shape[2]
        for part in range(out_ref.shape[0]):
            out_ref[part] = sums_ref[:, part * share : (part + 1) * share].astype(out_ref.dtype)


def lag_sums(places, received, parts, normalizer):
    ends = places.shape[0]
    slots = received.shape[0]
    pairs = ends // 2
    windows = slots // (32 * CAP)
    inner, outer = lag_tables(normalizer)
    return pl.pallas_call(
        lag_kernel,
        out_shape=jax.ShapeDtypeStruct((parts, pairs, 2 * LAG // parts), jnp.bfloat16),
        grid_spec=pltpu.PrefetchScalarGridSpec(
            num_scalar_prefetch=0,
            grid=(C_STEPS,),
            in_specs=[
                pl.BlockSpec((ends, 128), lambda s: (0, 0)),
                pl.BlockSpec((slots, 256 * C_RES), lambda s: (0, s)),
                pl.BlockSpec((2 * DBINS, 2 * SUB), lambda s: (0, 0)),
                pl.BlockSpec((1, 2 * C_RES, 2 * LAG), lambda s: (s, 0, 0)),
            ],
            out_specs=pl.BlockSpec((parts, pairs, 2 * LAG // parts), lambda s: (0, 0, 0)),
            scratch_shapes=[
                pltpu.VMEM((windows * ends, slots), jnp.bfloat16),
                pltpu.VMEM((pairs, 2 * LAG), jnp.float32),
            ],
        ),
        compiler_params=pltpu.CompilerParams(
            dimension_semantics=("arbitrary",), vmem_limit_bytes=32 << 20
        ),
        cost_estimate=pl.CostEstimate(
            flops=2 * windows * ends * slots * 2 * F, bytes_accessed=5_000_000, transcendentals=0
        ),
        name="lag_sums",
    )(places, received, jnp.asarray(inner), jnp.asarray(outer.reshape(C_STEPS, 2 * C_RES, 2 * LAG)))


def total_kernel(parts_ref, out_ref):
    total = parts_ref[0].astype(jnp.float32)
    for part in range(1, parts_ref.shape[0]):
        total = total + parts_ref[part].astype(jnp.float32)
    out_ref[...] = total


def window_total(parts):
    return pl.pallas_call(
        total_kernel,
        out_shape=jax.ShapeDtypeStruct(parts.shape[1:], jnp.float32),
        name="window_total",
    )(parts).T


def on_device(traces, station_slot, pair_stations):
    window_count, station_count, length = traces.shape
    blocks = lax.axis_size("pairs")
    lag_parts = lax.axis_size("tm")
    normalizer = 1.0 / math.sqrt(F * window_count * lag_parts)
    wanted, places = requests(station_slot, pair_stations, blocks, window_count, station_count)
    picks = lax.all_to_all(wanted, "pairs", split_axis=0, concat_axis=0, tiled=True)
    whitened = whitened_spectra(traces.reshape(window_count * station_count, length))
    rows = jnp.dot(
        picks.reshape(blocks * window_count * CAP, window_count * station_count),
        whitened,
        preferred_element_type=jnp.bfloat16,
    )
    received = lax.all_to_all(
        rows.reshape(blocks, window_count * CAP, 2 * F), "pairs", split_axis=0, concat_axis=0, tiled=True
    )
    sums = lag_sums(places, received.reshape(blocks * window_count * CAP, 2 * F), lag_parts, normalizer)
    parts = lax.all_to_all(sums, "tm", split_axis=0, concat_axis=0, tiled=True)
    return window_total(parts)


def solution(mesh):
    in_specs = (P("tm", "pairs", None), P(), P("pairs", None))
    out_specs = P("tm", "pairs")
    return jax.shard_map(
        on_device, mesh=mesh, in_specs=in_specs, out_specs=out_specs, check_vma=False
    )
```

```python
import math

import jax
import jax.numpy as jnp
import ml_dtypes
import numpy as np
from jax import lax
from jax.experimental import pallas as pl
from jax.experimental.pallas import tpu as pltpu
from jax.sharding import PartitionSpec as P

F = 1536
FLO = 32
LAG = 1024
NS = 6144
RADIX = 12
SUB = NS // RADIX
DBINS = F // RADIX
STEPS = RADIX // 2
CAP = 8
ROOT3_2 = math.sqrt(3.0) / 2.0

TURNS = [0, 6] + [turn for step in range(1, STEPS) for turn in (step, RADIX - step)]
RESIDUES = [(turn - FLO) % RADIX for turn in TURNS]


def spectrum_tables():
    sub_times = np.arange(SUB, dtype=np.int64)[:, None]
    bins = np.arange(DBINS, dtype=np.int64)[None, :]
    angles = (sub_times * bins % SUB) * (2.0 * np.pi / SUB)
    cos_part, sin_part = np.cos(angles), np.sin(angles)
    inner = np.block([[cos_part, -sin_part], [sin_part, cos_part]]).astype(ml_dtypes.bfloat16)
    first_bins = FLO + np.array(RESIDUES, dtype=np.int64)[:, None]
    turn_angles = (first_bins * sub_times[:, 0][None, :] % NS) * (2.0 * np.pi / NS)
    turns = np.stack([np.cos(turn_angles), np.sin(turn_angles)], axis=1)
    return inner, turns.reshape(2 * RADIX, SUB).astype(np.float32)


def hann_window():
    times = np.arange(NS, dtype=np.float64)
    return (0.5 - 0.5 * np.cos((times + 0.5) * (2.0 * np.pi / NS))).astype(np.float32)[None, :]


def lag_tables(normalizer):
    bins = np.arange(DBINS, dtype=np.int64)[:, None]
    sub_lags = np.arange(SUB, dtype=np.int64)[None, :]
    angles = (bins * sub_lags % SUB) * (2.0 * np.pi / SUB)
    cos_part, sin_part = np.cos(angles), np.sin(angles)
    inner = np.block([[cos_part, sin_part], [-sin_part, cos_part]]).astype(ml_dtypes.bfloat16)
    first_bins = FLO + np.array(RESIDUES, dtype=np.int64)[:, None]
    outer_angles = (first_bins * sub_lags % NS) * (2.0 * np.pi / NS)
    outer = np.stack([np.cos(outer_angles), np.sin(outer_angles)], axis=1) * normalizer
    return inner, outer.reshape(2 * RADIX, SUB).astype(np.float32)


def request_kernel(slots_ref, pairs_ref, wanted_ref, places_ref):
    ends = 2 * pairs_ref.shape[1]
    windows = wanted_ref.shape[1] // CAP
    stations = wanted_ref.shape[2] // windows
    owners_count = wanted_ref.shape[0]
    sublane = lax.broadcasted_iota(jnp.int32, (ends, ends), 0)
    lane = lax.broadcasted_iota(jnp.int32, (ends, ends), 1)

    def to_column(row):
        square = jnp.broadcast_to(row, (ends, ends))
        return jnp.sum(jnp.where(sublane == lane, square, 0).astype(jnp.float32), axis=1, keepdims=True)

    end_row = jnp.concatenate([pairs_ref[0:1, :], pairs_ref[1:2, :]], axis=1)
    end_column = to_column(end_row).astype(jnp.int32)
    lanes = lax.broadcasted_iota(jnp.int32, (ends, 128), 1)
    found = jnp.zeros((ends, 128), jnp.int32)
    for row in range(slots_ref.shape[0]):
        found = found + jnp.where(end_column == lanes + row * 128, slots_ref[row : row + 1, :], 0)
    slot_column = jnp.sum(found.astype(jnp.float32), axis=1, keepdims=True).astype(jnp.int32)
    slot_square = jnp.broadcast_to(slot_column, (ends, ends))
    slot_row = jnp.sum(
        jnp.where(sublane == lane, slot_square, 0).astype(jnp.float32), axis=0, keepdims=True
    ).astype(jnp.int32)
    owner_column = slot_column // stations
    owner_row = slot_row // stations
    local_row = slot_row - owner_row * stations
    same_owner = owner_column == owner_row
    rank_row = jnp.sum(
        jnp.where(same_owner & (sublane < lane), 1.0, 0.0), axis=0, keepdims=True
    ).astype(jnp.int32)
    rank_column = jnp.sum(
        jnp.where(same_owner & (lane < sublane), 1.0, 0.0), axis=1, keepdims=True
    ).astype(jnp.int32)
    places_ref[...] = jnp.broadcast_to(owner_column * (windows * CAP) + rank_column, places_ref.shape)
    owned = lax.broadcasted_iota(jnp.int32, (owners_count, ends), 0) == owner_row
    column_ids = lax.broadcasted_iota(jnp.int32, (owners_count, 1, windows * stations), 2)
    picks = [[] for _ in range(windows)]
    for rank in range(CAP):
        hit = owned & (rank_row == rank)
        row_wanted = jnp.sum(
            jnp.where(hit, local_row, 0).astype(jnp.float32), axis=1, keepdims=True
        ).astype(jnp.int32)
        for window in range(windows):
            column = (row_wanted + window * stations)[:, :, None]
            picks[window].append(jnp.where(column_ids == column, 1.0, 0.0))
    wanted_ref[...] = jnp.concatenate(sum(picks, []), axis=1).astype(jnp.bfloat16)


def requests(station_slot, pair_stations, blocks, windows, stations):
    pair_count = pair_stations.shape[0]
    return pl.pallas_call(
        request_kernel,
        out_shape=(
            jax.ShapeDtypeStruct((blocks, windows * CAP, windows * stations), jnp.bfloat16),
            jax.ShapeDtypeStruct((2 * pair_count, 128), jnp.int32),
        ),
        name="requests",
    )(station_slot.reshape(-1, 128), pair_stations.T)


def spectrum_kernel(traces_ref, hann_ref, turns_ref, table_ref, out_ref, *scratch):
    count = len(scratch) // 2
    row_count = traces_ref.shape[0] // count
    tables = (hann_ref, turns_ref, table_ref)
    for part in range(count):
        transform_rows(part * row_count, row_count, traces_ref, *tables, out_ref, *scratch[2 * part : 2 * part + 2])


def transform_rows(
    base_row, row_count, traces_ref, hann_ref, turns_ref, table_ref, out_ref, parts_ref, spectrum_ref
):

    def one_group(group):
        first = group * 16
        rows = pl.ds(base_row + first, 16)
        partial_sum = traces_ref[rows, 0:128]
        for tile in range(1, NS // 128):
            partial_sum = partial_sum + traces_ref[rows, tile * 128 : (tile + 1) * 128]
        mean = jnp.sum(partial_sum, axis=1, keepdims=True) * (1.0 / NS)
        for tile in range(SUB // 128):
            x = []
            for block in range(RADIX):
                columns = slice(block * SUB + tile * 128, block * SUB + (tile + 1) * 128)
                x.append((traces_ref[rows, columns] - mean) * hann_ref[:, columns])
            u = [None] + [x[a] + x[RADIX - a] for a in range(1, 6)]
            v = [None] + [x[a] - x[RADIX - a] for a in range(1, 6)]
            e0, o0 = x[0] + x[6], x[0] - x[6]
            p, q = u[1] + u[5], u[2] + u[4]
            pd, qd = u[1] - u[5], u[2] - u[4]
            m, n = v[1] - v[5], v[2] - v[4]
            ms, ns = v[1] + v[5], v[2] + v[4]
            half_pq, half_diff = 0.5 * (p + q), 0.5 * (p - q)
            e_plus, e_minus = e0 + u[3], e0 - u[3]
            base = o0 + 0.5 * qd
            side = ROOT3_2 * pd
            imag_base = 0.5 * ms + v[3]
            imag_side = ROOT3_2 * ns
            real_parts = [
                e_plus + (p + q),
                base + side,
                e_minus + half_diff,
                o0 - qd,
                e_plus - half_pq,
                base - side,
                e_minus - (p - q),
            ]
            imag_parts = [
                None,
                -(imag_base + imag_side),
                -ROOT3_2 * (m + n),
                v[3] - ms,
                -ROOT3_2 * (m - n),
                imag_side - imag_base,
                None,
            ]
            lanes = slice(tile * 128, (tile + 1) * 128)
            imag_lanes = slice(SUB + tile * 128, SUB + (tile + 1) * 128)
            for position, turn in enumerate(TURNS):
                index = min(turn, RADIX - turn)
                real_part, imag_part = real_parts[index], imag_parts[index]
                cos_turn = turns_ref[2 * position : 2 * position + 1, lanes]
                sin_turn = turns_ref[2 * position + 1 : 2 * position + 2, lanes]
                if imag_part is None:
                    turned_real = real_part * cos_turn
                    turned_imag = -(real_part * sin_turn)
                elif index == turn:
                    turned_real = real_part * cos_turn + imag_part * sin_turn
                    turned_imag = imag_part * cos_turn - real_part * sin_turn
                else:
                    turned_real = real_part * cos_turn - imag_part * sin_turn
                    turned_imag = -(imag_part * cos_turn + real_part * sin_turn)
                target = pl.ds(position * row_count + first, 16)
                parts_ref[target, lanes] = turned_real.astype(jnp.bfloat16)
                parts_ref[target, imag_lanes] = turned_imag.astype(jnp.bfloat16)

    for group in range(row_count // 16):
        one_group(group)
    spectrum_ref[...] = jnp.dot(parts_ref[...], table_ref[...], preferred_element_type=jnp.float32)

    def whiten_group(group):
        first = group * 16
        rows = pl.ds(base_row + first, 16)
        total = jnp.zeros((16, DBINS), jnp.float32)
        for position in range(RADIX):
            source = pl.ds(position * row_count + first, 16)
            real_part, imag_part = spectrum_ref[source, :DBINS], spectrum_ref[source, DBINS:]
            total = total + (real_part * real_part + imag_part * imag_part)
        water_level = jnp.sum(total, axis=1, keepdims=True) * (1.0 / F)
        floor = 0.1 * water_level + 1e-06
        for position in range(RADIX):
            source = pl.ds(position * row_count + first, 16)
            real_part, imag_part = spectrum_ref[source, :DBINS], spectrum_ref[source, DBINS:]
            scaling = lax.rsqrt(real_part * real_part + imag_part * imag_part + floor)
            start = position * 2 * DBINS
            out_ref[rows, start : start + DBINS] = (real_part * scaling).astype(jnp.bfloat16)
            out_ref[rows, start + DBINS : start + 2 * DBINS] = (imag_part * scaling).astype(jnp.bfloat16)

    for group in range(row_count // 16):
        whiten_group(group)


PART_ROWS = 32
STEP_PARTS = 2


def whitened_spectra(traces):
    total = traces.shape[0]
    rows = PART_ROWS * STEP_PARTS
    table, turns = spectrum_tables()
    scratch = [
        pltpu.VMEM((RADIX * PART_ROWS, 2 * SUB), jnp.bfloat16),
        pltpu.VMEM((RADIX * PART_ROWS, 2 * DBINS), jnp.float32),
    ]
    return pl.pallas_call(
        spectrum_kernel,
        out_shape=jax.ShapeDtypeStruct((total, 2 * F), jnp.bfloat16),
        grid_spec=pltpu.PrefetchScalarGridSpec(
            num_scalar_prefetch=0,
            grid=(total // rows,),
            in_specs=[
                pl.BlockSpec((rows, NS), lambda s: (s, 0)),
                pl.BlockSpec((1, NS), lambda s: (0, 0)),
                pl.BlockSpec((2 * RADIX, SUB), lambda s: (0, 0)),
                pl.BlockSpec((2 * SUB, 2 * DBINS), lambda s: (0, 0)),
            ],
            out_specs=pl.BlockSpec((rows, 2 * F), lambda s: (s, 0)),
            scratch_shapes=scratch * STEP_PARTS,
        ),
        compiler_params=pltpu.CompilerParams(dimension_semantics=("arbitrary",)),
        cost_estimate=pl.CostEstimate(
            flops=2 * total * RADIX * 2 * SUB * 2 * DBINS,
            bytes_accessed=5_000_000,
            transcendentals=total * F,
        ),
        name="whitened_spectra",
    )(traces, jnp.asarray(hann_window()), jnp.asarray(turns), jnp.asarray(table))


def lag_kernel(
    place_ref, places_ref, received_ref, inner_ref, outer_ref, kept_ref, sent_ref,
    select_ref, stacked_ref, turned_ref, sums_ref,
):
    slots = received_ref.shape[0]
    ends = places_ref.shape[0]
    pairs = ends // 2
    windows = select_ref.shape[0] // ends
    lanes = lax.broadcasted_iota(jnp.int32, (ends, 128), 1)
    places = places_ref[...]
    for window in range(windows):
        for tile in range(slots // 128):
            hit = jnp.where(places + window * CAP == lanes + tile * 128, 1.0, 0.0)
            rows = slice(window * ends, (window + 1) * ends)
            select_ref[rows, tile * 128 : (tile + 1) * 128] = hit.astype(jnp.bfloat16)

    for step in range(STEPS):
        columns = slice(step * 4 * DBINS, (step + 1) * 4 * DBINS)
        picked = jnp.dot(select_ref[...], received_ref[:, columns], preferred_element_type=jnp.float32)
        for half in range(2):
            real_columns = slice(half * 2 * DBINS, half * 2 * DBINS + DBINS)
            imag_columns = slice(half * 2 * DBINS + DBINS, (half + 1) * 2 * DBINS)
            real_sum = imag_sum = None
            for window in range(windows):
                left = slice(window * ends, window * ends + pairs)
                right = slice(window * ends + pairs, (window + 1) * ends)
                left_real, left_imag = picked[left, real_columns], picked[left, imag_columns]
                right_real, right_imag = picked[right, real_columns], picked[right, imag_columns]
                real_term = left_real * right_real + left_imag * right_imag
                imag_term = left_imag * right_real - left_real * right_imag
                real_sum = real_term if real_sum is None else real_sum + real_term
                imag_sum = imag_term if imag_sum is None else imag_sum + imag_term
            position = 2 * step + half
            rows = slice(position * pairs, (position + 1) * pairs)
            stacked_ref[rows, :DBINS] = real_sum.astype(jnp.bfloat16)
            stacked_ref[rows, DBINS:] = imag_sum.astype(jnp.bfloat16)

    turned_ref[...] = jnp.dot(stacked_ref[...], inner_ref[...], preferred_element_type=jnp.float32)

    for tile in range(SUB // 128):
        columns = slice(tile * 128, (tile + 1) * 128)
        imag_columns = slice(SUB + tile * 128, SUB + (tile + 1) * 128)
        for group in range(pairs // 8):
            real_of, imag_of = {}, {}
            for position, turn in enumerate(TURNS):
                rows = slice(position * pairs + group * 8, position * pairs + group * 8 + 8)
                real_part, imag_part = turned_ref[rows, columns], turned_ref[rows, imag_columns]
                cos_turn = outer_ref[2 * position : 2 * position + 1, columns]
                sin_turn = outer_ref[2 * position + 1 : 2 * position + 2, columns]
                real_of[turn] = real_part * cos_turn - imag_part * sin_turn
                if turn % STEPS:
                    imag_of[turn] = real_part * sin_turn + imag_part * cos_turn
            r0, r6 = real_of[0], real_of[6]
            re = [None] + [real_of[r] + real_of[RADIX - r] for r in range(1, STEPS)]
            im = [None] + [imag_of[r] - imag_of[RADIX - r] for r in range(1, STEPS)]
            even, odd = re[2] + re[4], re[1] + re[5]
            q_zero = (r0 + r6) + (even + odd + re[3])
            q_one_real = (r0 - r6) + 0.5 * (re[2] - re[4]) + ROOT3_2 * (re[1] - re[5])
            q_one_imag = 0.5 * (im[1] + im[5]) + ROOT3_2 * (im[2] + im[4]) + im[3]
            q_two_real = (r0 + r6) + 0.5 * (re[1] + re[5] - even) - re[3]
            q_two_imag = ROOT3_2 * (im[1] + im[2] - im[4] - im[5])
            periods = [q_two_real + q_two_imag, q_one_real + q_one_imag, q_zero, q_one_real - q_one_imag]
            for period, values in enumerate(periods):
                sums_ref[group * 8 : group * 8 + 8, period * SUB + tile * 128 : period * SUB + (tile + 1) * 128] = values

    rings = kept_ref.shape[0]
    share = kept_ref.shape[2]
    for offset in range(rings):
        ring = lax.rem(place_ref[0] + offset, rings)
        kept = pl.multiple_of((2 * ring + place_ref[1]) * share, share)
        sent = pl.multiple_of((2 * ring + 1 - place_ref[1]) * share, share)
        kept_ref[offset] = sums_ref[:, pl.ds(kept, share)]
        sent_ref[offset] = sums_ref[:, pl.ds(sent, share)].astype(sent_ref.dtype)


def lag_sums(place, places, received, parts, normalizer):
    ends = places.shape[0]
    slots = received.shape[0]
    pairs = ends // 2
    windows = slots // (32 * CAP)
    inner, outer = lag_tables(normalizer)
    share = 2 * LAG // parts
    vmem = pl.BlockSpec(memory_space=pltpu.VMEM)
    return pl.pallas_call(
        lag_kernel,
        out_shape=(
            jax.ShapeDtypeStruct((parts // 2, pairs, share), jnp.float32),
            jax.ShapeDtypeStruct((parts // 2, pairs, share), jnp.bfloat16),
        ),
        in_specs=[pl.BlockSpec(memory_space=pltpu.SMEM)] + [vmem] * 4,
        out_specs=(vmem, vmem),
        scratch_shapes=[
            pltpu.VMEM((windows * ends, slots), jnp.bfloat16),
            pltpu.VMEM((RADIX * pairs, 2 * DBINS), jnp.bfloat16),
            pltpu.VMEM((RADIX * pairs, 2 * SUB), jnp.float32),
            pltpu.VMEM((pairs, 2 * LAG), jnp.float32),
        ],
        compiler_params=pltpu.CompilerParams(vmem_limit_bytes=32 << 20),
        cost_estimate=pl.CostEstimate(
            flops=2 * windows * ends * slots * 2 * F, bytes_accessed=5_000_000, transcendentals=0
        ),
        name="lag_sums",
    )(place, places, received, jnp.asarray(inner), jnp.asarray(outer))


def add_kernel(kept_ref, got_ref, own_ref, *sent_refs):
    own_ref[...] = kept_ref[0] + got_ref[0].astype(jnp.float32)
    for offset, sent_ref in enumerate(sent_refs, 1):
        sent_ref[...] = (kept_ref[offset] + got_ref[offset].astype(jnp.float32)).astype(sent_ref.dtype)


def total_kernel(own_ref, *rest):
    total = own_ref[...]
    for got_ref in rest[:-1]:
        total = total + got_ref[...].astype(jnp.float32)
    rest[-1][...] = total


def window_total(kept, sent):
    rings, pairs, share = kept.shape
    devices = range(2 * rings)
    got = lax.ppermute(sent, "tm", [(source, source ^ 1) for source in devices])
    params = pltpu.CompilerParams(vmem_limit_bytes=16 << 20)
    own, *onward = pl.pallas_call(
        add_kernel,
        out_shape=[jax.ShapeDtypeStruct((pairs, share), jnp.float32)]
        + [jax.ShapeDtypeStruct((pairs, share), jnp.bfloat16)] * (rings - 1),
        compiler_params=params,
        name="core_total",
    )(kept, got)
    arrived = []
    for offset, values in enumerate(onward, 1):
        targets = [(source, (source // 2 + offset) % rings * 2 + source % 2) for source in devices]
        arrived.append(lax.ppermute(values, "tm", targets))
    return pl.pallas_call(
        total_kernel,
        out_shape=jax.ShapeDtypeStruct((pairs, share), jnp.float32),
        compiler_params=params,
        name="window_total",
    )(own, *arrived).T


def on_device(traces, station_slot, pair_stations):
    window_count, station_count, length = traces.shape
    blocks = lax.axis_size("pairs")
    lag_parts = lax.axis_size("tm")
    slots = blocks * window_count * CAP
    normalizer = 1.0 / math.sqrt(F * window_count * lag_parts)
    own = lax.axis_index("tm")
    place = jnp.stack([own // 2, own % 2]).astype(jnp.int32)
    wanted, places = requests(station_slot, pair_stations, blocks, window_count, station_count)
    picks = lax.all_to_all(wanted, "pairs", split_axis=0, concat_axis=0, tiled=True)
    whitened = whitened_spectra(traces.reshape(window_count * station_count, length))
    rows = jnp.dot(
        picks.reshape(slots, window_count * station_count), whitened, preferred_element_type=jnp.bfloat16
    )
    received = lax.all_to_all(
        rows.reshape(blocks, window_count * CAP, 2 * F), "pairs", split_axis=0, concat_axis=0, tiled=True
    )
    kept, sent = lag_sums(place, places, received.reshape(slots, 2 * F), lag_parts, normalizer)
    return window_total(kept, sent)


def solution(mesh):
    in_specs = (P("tm", "pairs", None), P(), P("pairs", None))
    out_specs = P("tm", "pairs")
    return jax.shard_map(
        on_device, mesh=mesh, in_specs=in_specs, out_specs=out_specs, check_vma=False
    )
```

```python
import math

import jax
import jax.numpy as jnp
import ml_dtypes
import numpy as np
from jax import lax
from jax.experimental import pallas as pl
from jax.experimental.pallas import tpu as pltpu
from jax.sharding import PartitionSpec as P

F = 1536
FLO = 32
LAG = 1024
NS = 6144
RADIX = 12
SUB = NS // RADIX
DBINS = F // RADIX
STEPS = RADIX // 2
CAP = 8
ROOT3_2 = math.sqrt(3.0) / 2.0

TURNS = [0, 6] + [turn for step in range(1, STEPS) for turn in (step, RADIX - step)]
RESIDUES = [(turn - FLO) % RADIX for turn in TURNS]


def spectrum_tables():
    sub_times = np.arange(SUB, dtype=np.int64)[:, None]
    bins = np.arange(DBINS, dtype=np.int64)[None, :]
    angles = (sub_times * bins % SUB) * (2.0 * np.pi / SUB)
    cos_part, sin_part = np.cos(angles), np.sin(angles)
    inner = np.block([[cos_part, -sin_part], [sin_part, cos_part]]).astype(ml_dtypes.bfloat16)
    first_bins = FLO + np.array(RESIDUES, dtype=np.int64)[:, None]
    turn_angles = (first_bins * sub_times[:, 0][None, :] % NS) * (2.0 * np.pi / NS)
    turns = np.stack([np.cos(turn_angles), np.sin(turn_angles)], axis=1)
    return inner, turns.reshape(2 * RADIX, SUB).astype(np.float32)


def hann_window():
    times = np.arange(NS, dtype=np.float64)
    return (0.5 - 0.5 * np.cos((times + 0.5) * (2.0 * np.pi / NS))).astype(np.float32)[None, :]


def lag_tables(normalizer):
    bins = np.arange(DBINS, dtype=np.int64)[:, None]
    sub_lags = np.arange(SUB, dtype=np.int64)[None, :]
    angles = (bins * sub_lags % SUB)[:, :DBINS] * (2.0 * np.pi / SUB)
    cos_part, sin_part = np.cos(angles), np.sin(angles)
    inner = np.block([[cos_part, sin_part], [-sin_part, cos_part]]).astype(ml_dtypes.bfloat16)
    first_bins = FLO + np.array(RESIDUES, dtype=np.int64)[:, None]
    outer_angles = (first_bins * sub_lags % NS) * (2.0 * np.pi / NS)
    outer = np.stack([np.cos(outer_angles), np.sin(outer_angles)], axis=1) * normalizer
    return inner, outer.reshape(2 * RADIX, SUB).astype(np.float32)


def request_kernel(slots_ref, pairs_ref, wanted_ref, places_ref):
    ends = 2 * pairs_ref.shape[1]
    windows = wanted_ref.shape[1] // CAP
    stations = wanted_ref.shape[2] // windows
    owners_count = wanted_ref.shape[0]
    sublane = lax.broadcasted_iota(jnp.int32, (ends, ends), 0)
    lane = lax.broadcasted_iota(jnp.int32, (ends, ends), 1)

    def to_column(row):
        square = jnp.broadcast_to(row, (ends, ends))
        return jnp.sum(jnp.where(sublane == lane, square, 0).astype(jnp.float32), axis=1, keepdims=True)

    end_row = jnp.concatenate([pairs_ref[0:1, :], pairs_ref[1:2, :]], axis=1)
    end_column = to_column(end_row).astype(jnp.int32)
    lanes = lax.broadcasted_iota(jnp.int32, (ends, 128), 1)
    found = jnp.zeros((ends, 128), jnp.int32)
    for row in range(slots_ref.shape[0]):
        found = found + jnp.where(end_column == lanes + row * 128, slots_ref[row : row + 1, :], 0)
    slot_column = jnp.sum(found.astype(jnp.float32), axis=1, keepdims=True).astype(jnp.int32)
    slot_square = jnp.broadcast_to(slot_column, (ends, ends))
    slot_row = jnp.sum(
        jnp.where(sublane == lane, slot_square, 0).astype(jnp.float32), axis=0, keepdims=True
    ).astype(jnp.int32)
    owner_column = slot_column // stations
    owner_row = slot_row // stations
    same_owner = owner_column == owner_row
    rank_row = jnp.sum(
        jnp.where(same_owner & (sublane < lane), 1.0, 0.0), axis=0, keepdims=True
    ).astype(jnp.int32)
    rank_column = jnp.sum(
        jnp.where(same_owner & (lane < sublane), 1.0, 0.0), axis=1, keepdims=True
    ).astype(jnp.int32)
    places_ref[...] = jnp.broadcast_to(owner_column * (windows * CAP) + rank_column, places_ref.shape)
    row_keys = owner_row * (windows * CAP) + rank_row
    slots = owners_count * windows * CAP
    slot_ids = lax.broadcasted_iota(jnp.int32, (slots, ends), 0)
    slot_windows = slot_ids // CAP % windows
    local_column = slot_column - owner_column * stations
    picks = None
    for window in range(windows):
        hit = (slot_ids == row_keys + window * CAP) & (slot_windows == window)
        columns = lax.broadcasted_iota(jnp.int32, (ends, windows * stations), 1)
        rows = jnp.where(columns == local_column + window * stations, 1.0, 0.0).astype(jnp.bfloat16)
        term = jnp.dot(jnp.where(hit, 1.0, 0.0).astype(jnp.bfloat16), rows, preferred_element_type=jnp.float32)
        picks = term if picks is None else picks + term
    wanted_ref[...] = picks.astype(jnp.bfloat16).reshape(wanted_ref.shape)


def requests(station_slot, pair_stations, blocks, windows, stations):
    pair_count = pair_stations.shape[0]
    return pl.pallas_call(
        request_kernel,
        out_shape=(
            jax.ShapeDtypeStruct((blocks, windows * CAP, windows * stations), jnp.bfloat16),
            jax.ShapeDtypeStruct((2 * pair_count, 128), jnp.int32),
        ),
        name="requests",
    )(station_slot.reshape(-1, 128), pair_stations.T)


def spectrum_kernel(traces_ref, hann_ref, turns_ref, table_ref, out_ref, *scratch):
    count = len(scratch) // 2
    row_count = traces_ref.shape[0] // count
    tables = (hann_ref, turns_ref, table_ref)
    for part in range(count):
        transform_rows(part * row_count, row_count, traces_ref, *tables, out_ref, *scratch[2 * part : 2 * part + 2])


def transform_rows(
    base_row, row_count, traces_ref, hann_ref, turns_ref, table_ref, out_ref, parts_ref, spectrum_ref
):

    def one_group(group):
        first = group * 16
        rows = pl.ds(base_row + first, 16)
        partial_sum = traces_ref[rows, 0:128]
        for tile in range(1, NS // 128):
            partial_sum = partial_sum + traces_ref[rows, tile * 128 : (tile + 1) * 128]
        mean = jnp.sum(partial_sum, axis=1, keepdims=True) * (1.0 / NS)
        for tile in range(SUB // 128):
            x = []
            for block in range(RADIX):
                columns = slice(block * SUB + tile * 128, block * SUB + (tile + 1) * 128)
                x.append((traces_ref[rows, columns] - mean) * hann_ref[:, columns])
            u = [None] + [x[a] + x[RADIX - a] for a in range(1, 6)]
            v = [None] + [x[a] - x[RADIX - a] for a in range(1, 6)]
            e0, o0 = x[0] + x[6], x[0] - x[6]
            p, q = u[1] + u[5], u[2] + u[4]
            pd, qd = u[1] - u[5], u[2] - u[4]
            m, n = v[1] - v[5], v[2] - v[4]
            ms, ns = v[1] + v[5], v[2] + v[4]
            half_pq, half_diff = 0.5 * (p + q), 0.5 * (p - q)
            e_plus, e_minus = e0 + u[3], e0 - u[3]
            base = o0 + 0.5 * qd
            side = ROOT3_2 * pd
            imag_base = 0.5 * ms + v[3]
            imag_side = ROOT3_2 * ns
            real_parts = [
                e_plus + (p + q),
                base + side,
                e_minus + half_diff,
                o0 - qd,
                e_plus - half_pq,
                base - side,
                e_minus - (p - q),
            ]
            imag_parts = [
                None,
                -(imag_base + imag_side),
                -ROOT3_2 * (m + n),
                v[3] - ms,
                -ROOT3_2 * (m - n),
                imag_side - imag_base,
                None,
            ]
            lanes = slice(tile * 128, (tile + 1) * 128)
            imag_lanes = slice(SUB + tile * 128, SUB + (tile + 1) * 128)
            for position, turn in enumerate(TURNS):
                index = min(turn, RADIX - turn)
                real_part, imag_part = real_parts[index], imag_parts[index]
                cos_turn = turns_ref[2 * position : 2 * position + 1, lanes]
                sin_turn = turns_ref[2 * position + 1 : 2 * position + 2, lanes]
                if imag_part is None:
                    turned_real = real_part * cos_turn
                    turned_imag = -(real_part * sin_turn)
                elif index == turn:
                    turned_real = real_part * cos_turn + imag_part * sin_turn
                    turned_imag = imag_part * cos_turn - real_part * sin_turn
                else:
                    turned_real = real_part * cos_turn - imag_part * sin_turn
                    turned_imag = -(imag_part * cos_turn + real_part * sin_turn)
                target = pl.ds(position * row_count + first, 16)
                parts_ref[target, lanes] = turned_real.astype(jnp.bfloat16)
                parts_ref[target, imag_lanes] = turned_imag.astype(jnp.bfloat16)

    for group in range(row_count // 16):
        one_group(group)
    spectrum_ref[...] = jnp.dot(parts_ref[...], table_ref[...], preferred_element_type=jnp.float32)

    def whiten_group(group):
        first = group * 16
        rows = pl.ds(base_row + first, 16)
        total = jnp.zeros((16, DBINS), jnp.float32)
        for position in range(RADIX):
            source = pl.ds(position * row_count + first, 16)
            real_part, imag_part = spectrum_ref[source, :DBINS], spectrum_ref[source, DBINS:]
            total = total + (real_part * real_part + imag_part * imag_part)
        water_level = jnp.sum(total, axis=1, keepdims=True) * (1.0 / F)
        floor = 0.1 * water_level + 1e-06
        for position in range(RADIX):
            source = pl.ds(position * row_count + first, 16)
            real_part, imag_part = spectrum_ref[source, :DBINS], spectrum_ref[source, DBINS:]
            scaling = lax.rsqrt(real_part * real_part + imag_part * imag_part + floor)
            start = position * 2 * DBINS
            out_ref[rows, start : start + DBINS] = (real_part * scaling).astype(jnp.bfloat16)
            out_ref[rows, start + DBINS : start + 2 * DBINS] = (imag_part * scaling).astype(jnp.bfloat16)

    for group in range(row_count // 16):
        whiten_group(group)


def in_hbm(*arrays):
    return [pltpu.with_memory_space_constraint(array, pltpu.HBM) for array in arrays]


def gather_kernel(picks_ref, whitened_ref, rows_ref):
    rows_ref[...] = jnp.dot(picks_ref[...], whitened_ref[...], preferred_element_type=jnp.float32).astype(
        rows_ref.dtype
    )


def gathered(picks, whitened):
    slots, rows = picks.shape
    return pl.pallas_call(
        gather_kernel,
        out_shape=pltpu.HBM((slots, whitened.shape[1]), whitened.dtype),
        grid=(slots // 128,),
        in_specs=[
            pl.BlockSpec((128, rows), lambda s: (s, 0)),
            pl.BlockSpec(whitened.shape, lambda s: (0, 0)),
        ],
        out_specs=pl.BlockSpec((128, whitened.shape[1]), lambda s: (s, 0)),
        compiler_params=pltpu.CompilerParams(
            dimension_semantics=("arbitrary",), vmem_limit_bytes=16 << 20
        ),
        name="gathered",
    )(picks, whitened)


PART_ROWS = 32
STEP_PARTS = 2


def whitened_spectra(traces):
    total = traces.shape[0]
    rows = PART_ROWS * STEP_PARTS
    table, turns = spectrum_tables()
    scratch = [
        pltpu.VMEM((RADIX * PART_ROWS, 2 * SUB), jnp.bfloat16),
        pltpu.VMEM((RADIX * PART_ROWS, 2 * DBINS), jnp.float32),
    ]
    return pl.pallas_call(
        spectrum_kernel,
        out_shape=jax.ShapeDtypeStruct((total, 2 * F), jnp.bfloat16),
        grid_spec=pltpu.PrefetchScalarGridSpec(
            num_scalar_prefetch=0,
            grid=(total // rows,),
            in_specs=[
                pl.BlockSpec((rows, NS), lambda s: (s, 0)),
                pl.BlockSpec((1, NS), lambda s: (0, 0)),
                pl.BlockSpec((2 * RADIX, SUB), lambda s: (0, 0)),
                pl.BlockSpec((2 * SUB, 2 * DBINS), lambda s: (0, 0)),
            ],
            out_specs=pl.BlockSpec((rows, 2 * F), lambda s: (s, 0)),
            scratch_shapes=scratch * STEP_PARTS,
        ),
        compiler_params=pltpu.CompilerParams(
            dimension_semantics=("arbitrary",), vmem_limit_bytes=24 << 20
        ),
        cost_estimate=pl.CostEstimate(
            flops=2 * total * RADIX * 2 * SUB * 2 * DBINS,
            bytes_accessed=5_000_000,
            transcendentals=total * F,
        ),
        name="whitened_spectra",
    )(*in_hbm(traces, jnp.asarray(hann_window()), jnp.asarray(turns), jnp.asarray(table)))


def lag_kernel(
    place_ref, places_ref, received_ref, inner_ref, outer_ref, kept_ref, sent_ref,
    select_ref, stacked_ref, turned_ref, sums_ref,
):
    slots = received_ref.shape[0]
    ends = places_ref.shape[0]
    pairs = ends // 2
    windows = select_ref.shape[0] // ends
    lanes = lax.broadcasted_iota(jnp.int32, (ends, 128), 1)
    places = places_ref[...]
    for window in range(windows):
        for tile in range(slots // 128):
            hit = jnp.where(places + window * CAP == lanes + tile * 128, 1.0, 0.0)
            rows = slice(window * ends, (window + 1) * ends)
            select_ref[rows, tile * 128 : (tile + 1) * 128] = hit.astype(jnp.bfloat16)

    bins = lax.broadcasted_iota(jnp.int32, (1, DBINS), 1)
    even = bins % 2 == 0
    flip_odd = jnp.where(even, 1.0, -1.0)
    flip_upper = jnp.where(bins % 4 < 2, 1.0, -1.0)
    residue_rows = RADIX * pairs
    for step in range(STEPS):
        columns = slice(step * 4 * DBINS, (step + 1) * 4 * DBINS)
        picked = jnp.dot(select_ref[...], received_ref[:, columns], preferred_element_type=jnp.float32)
        for half in range(2):
            real_columns = slice(half * 2 * DBINS, half * 2 * DBINS + DBINS)
            imag_columns = slice(half * 2 * DBINS + DBINS, (half + 1) * 2 * DBINS)
            real_sum = imag_sum = None
            for window in range(windows):
                left = slice(window * ends, window * ends + pairs)
                right = slice(window * ends + pairs, (window + 1) * ends)
                left_real, left_imag = picked[left, real_columns], picked[left, imag_columns]
                right_real, right_imag = picked[right, real_columns], picked[right, imag_columns]
                real_term = left_real * right_real + left_imag * right_imag
                imag_term = left_imag * right_real - left_real * right_imag
                real_sum = real_term if real_sum is None else real_sum + real_term
                imag_sum = imag_term if imag_sum is None else imag_sum + imag_term
            quarter_real = jnp.where(even, real_sum, -imag_sum) * flip_upper
            quarter_imag = jnp.where(even, imag_sum, real_sum) * flip_upper
            quarters = [
                (real_sum, imag_sum),
                (quarter_real, quarter_imag),
                (real_sum * flip_odd, imag_sum * flip_odd),
                (quarter_real * flip_odd, quarter_imag * flip_odd),
            ]
            position = 2 * step + half
            for quarter, (real_part, imag_part) in enumerate(quarters):
                first = quarter * residue_rows + position * pairs
                stacked_ref[first : first + pairs, :DBINS] = real_part.astype(jnp.bfloat16)
                stacked_ref[first : first + pairs, DBINS:] = imag_part.astype(jnp.bfloat16)

    turned_ref[...] = jnp.dot(stacked_ref[...], inner_ref[...], preferred_element_type=jnp.float32)

    for tile in range(SUB // 128):
        columns = slice(tile * 128, (tile + 1) * 128)
        for group in range(pairs // 8):
            real_of, imag_of = {}, {}
            for position, turn in enumerate(TURNS):
                first = tile * residue_rows + position * pairs + group * 8
                real_part, imag_part = turned_ref[first : first + 8, :DBINS], turned_ref[first : first + 8, DBINS:]
                cos_turn = outer_ref[2 * position : 2 * position + 1, columns]
                sin_turn = outer_ref[2 * position + 1 : 2 * position + 2, columns]
                real_of[turn] = real_part * cos_turn - imag_part * sin_turn
                if turn % STEPS:
                    imag_of[turn] = real_part * sin_turn + imag_part * cos_turn
            r0, r6 = real_of[0], real_of[6]
            re = [None] + [real_of[r] + real_of[RADIX - r] for r in range(1, STEPS)]
            im = [None] + [imag_of[r] - imag_of[RADIX - r] for r in range(1, STEPS)]
            even, odd = re[2] + re[4], re[1] + re[5]
            q_zero = (r0 + r6) + (even + odd + re[3])
            q_one_real = (r0 - r6) + 0.5 * (re[2] - re[4]) + ROOT3_2 * (re[1] - re[5])
            q_one_imag = 0.5 * (im[1] + im[5]) + ROOT3_2 * (im[2] + im[4]) + im[3]
            q_two_real = (r0 + r6) + 0.5 * (re[1] + re[5] - even) - re[3]
            q_two_imag = ROOT3_2 * (im[1] + im[2] - im[4] - im[5])
            periods = [q_two_real + q_two_imag, q_one_real + q_one_imag, q_zero, q_one_real - q_one_imag]
            for period, values in enumerate(periods):
                sums_ref[group * 8 : group * 8 + 8, period * SUB + tile * 128 : period * SUB + (tile + 1) * 128] = values

    rings = kept_ref.shape[0]
    share = kept_ref.shape[2]
    for offset in range(rings):
        ring = lax.rem(place_ref[0] + offset, rings)
        kept = pl.multiple_of((2 * ring + place_ref[1]) * share, share)
        sent = pl.multiple_of((2 * ring + 1 - place_ref[1]) * share, share)
        kept_ref[offset] = sums_ref[:, pl.ds(kept, share)]
        sent_ref[offset] = sums_ref[:, pl.ds(sent, share)].astype(sent_ref.dtype)


def lag_sums(place, places, received, parts, normalizer):
    ends = places.shape[0]
    slots = received.shape[0]
    pairs = ends // 2
    windows = slots // (32 * CAP)
    inner, outer = lag_tables(normalizer)
    share = 2 * LAG // parts
    vmem = pl.BlockSpec(memory_space=pltpu.VMEM)
    return pl.pallas_call(
        lag_kernel,
        out_shape=(
            jax.ShapeDtypeStruct((parts // 2, pairs, share), jnp.float32),
            jax.ShapeDtypeStruct((parts // 2, pairs, share), jnp.bfloat16),
        ),
        in_specs=[pl.BlockSpec(memory_space=pltpu.SMEM)] + [vmem] * 4,
        out_specs=(vmem, vmem),
        scratch_shapes=[
            pltpu.VMEM((windows * ends, slots), jnp.bfloat16),
            pltpu.VMEM((SUB // DBINS * RADIX * pairs, 2 * DBINS), jnp.bfloat16),
            pltpu.VMEM((SUB // DBINS * RADIX * pairs, 2 * DBINS), jnp.float32),
            pltpu.VMEM((pairs, 2 * LAG), jnp.float32),
        ],
        compiler_params=pltpu.CompilerParams(vmem_limit_bytes=32 << 20),
        cost_estimate=pl.CostEstimate(
            flops=2 * windows * ends * slots * 2 * F, bytes_accessed=5_000_000, transcendentals=0
        ),
        name="lag_sums",
    )(place, places, received, jnp.asarray(inner), jnp.asarray(outer))


def add_kernel(kept_ref, got_ref, own_ref, *sent_refs):
    own_ref[...] = kept_ref[0] + got_ref[0].astype(jnp.float32)
    for offset, sent_ref in enumerate(sent_refs, 1):
        sent_ref[...] = (kept_ref[offset] + got_ref[offset].astype(jnp.float32)).astype(sent_ref.dtype)


def total_kernel(own_ref, *rest):
    total = own_ref[...]
    for got_ref in rest[:-1]:
        total = total + got_ref[...].astype(jnp.float32)
    rest[-1][...] = total


def window_total(kept, sent):
    rings, pairs, share = kept.shape
    devices = range(2 * rings)
    got = lax.ppermute(sent, "tm", [(source, source ^ 1) for source in devices])
    params = pltpu.CompilerParams(vmem_limit_bytes=16 << 20)
    own, *onward = pl.pallas_call(
        add_kernel,
        out_shape=[jax.ShapeDtypeStruct((pairs, share), jnp.float32)]
        + [jax.ShapeDtypeStruct((pairs, share), jnp.bfloat16)] * (rings - 1),
        compiler_params=params,
        name="core_total",
    )(kept, got)
    arrived = []
    for offset, values in enumerate(onward, 1):
        targets = [(source, (source // 2 + offset) % rings * 2 + source % 2) for source in devices]
        arrived.append(lax.ppermute(values, "tm", targets))
    return pl.pallas_call(
        total_kernel,
        out_shape=jax.ShapeDtypeStruct((pairs, share), jnp.float32),
        compiler_params=params,
        name="window_total",
    )(own, *arrived).T


def on_device(traces, station_slot, pair_stations):
    window_count, station_count, length = traces.shape
    blocks = lax.axis_size("pairs")
    lag_parts = lax.axis_size("tm")
    slots = blocks * window_count * CAP
    normalizer = 1.0 / math.sqrt(F * window_count * lag_parts)
    own = lax.axis_index("tm")
    place = jnp.stack([own // 2, own % 2]).astype(jnp.int32)
    wanted, places = requests(station_slot, pair_stations, blocks, window_count, station_count)
    picks = lax.all_to_all(wanted, "pairs", split_axis=0, concat_axis=0, tiled=True)
    whitened = whitened_spectra(traces.reshape(window_count * station_count, length))
    rows = gathered(picks.reshape(slots, window_count * station_count), whitened)
    received = lax.all_to_all(
        rows.reshape(blocks, window_count * CAP, 2 * F), "pairs", split_axis=0, concat_axis=0, tiled=True
    )
    kept, sent = lag_sums(place, places, received.reshape(slots, 2 * F), lag_parts, normalizer)
    return window_total(kept, sent)


def solution(mesh):
    in_specs = (P("tm", "pairs", None), P(), P("pairs", None))
    out_specs = P("tm", "pairs")
    return jax.shard_map(
        on_device, mesh=mesh, in_specs=in_specs, out_specs=out_specs, check_vma=False
    )
```

```python
import functools
import math

import jax
import jax.numpy as jnp
import ml_dtypes
import numpy as np
from jax import lax
from jax.experimental import pallas as pl
from jax.experimental.pallas import tpu as pltpu
from jax.sharding import PartitionSpec as P

F = 1536
FLO = 32
LAG = 1024
NS = 6144
RADIX = 12
SUB = NS // RADIX
DBINS = F // RADIX
STEPS = RADIX // 2
CAP = 8
ROOT3_2 = math.sqrt(3.0) / 2.0

TURNS = [0, 6] + [turn for step in range(1, STEPS) for turn in (step, RADIX - step)]
RESIDUES = [(turn - FLO) % RADIX for turn in TURNS]


def spectrum_tables():
    sub_times = np.arange(SUB, dtype=np.int64)[:, None]
    bins = np.arange(DBINS, dtype=np.int64)[None, :]
    angles = (sub_times * bins % SUB) * (2.0 * np.pi / SUB)
    cos_part, sin_part = np.cos(angles), np.sin(angles)
    inner = np.block([[cos_part, -sin_part], [sin_part, cos_part]]).astype(ml_dtypes.bfloat16)
    first_bins = FLO + np.array(RESIDUES, dtype=np.int64)[:, None]
    turn_angles = (first_bins * sub_times[:, 0][None, :] % NS) * (2.0 * np.pi / NS)
    turns = np.stack([np.cos(turn_angles), np.sin(turn_angles)], axis=1)
    return inner, turns.reshape(2 * RADIX, SUB).astype(np.float32)


def hann_window():
    times = np.arange(NS, dtype=np.float64)
    return (0.5 - 0.5 * np.cos((times + 0.5) * (2.0 * np.pi / NS))).astype(np.float32)[None, :]


def lag_tables(normalizer):
    bins = np.arange(DBINS, dtype=np.int64)[:, None]
    sub_lags = np.arange(SUB, dtype=np.int64)[None, :]
    angles = (bins * sub_lags % SUB)[:, :DBINS] * (2.0 * np.pi / SUB)
    cos_part, sin_part = np.cos(angles), np.sin(angles)
    inner = np.block([[cos_part, sin_part], [-sin_part, cos_part]]).astype(ml_dtypes.bfloat16)
    first_bins = FLO + np.array(RESIDUES, dtype=np.int64)[:, None]
    outer_angles = (first_bins * sub_lags % NS) * (2.0 * np.pi / NS)
    outer = np.stack([np.cos(outer_angles), np.sin(outer_angles)], axis=1) * normalizer
    return inner, outer.reshape(2 * RADIX, SUB).astype(np.float32)


def request_kernel(windows, stations, slots_ref, pairs_ref, wanted_ref, places_ref):
    ends = 2 * pairs_ref.shape[1]
    owners_count = wanted_ref.shape[0]
    sublane = lax.broadcasted_iota(jnp.int32, (ends, ends), 0)
    lane = lax.broadcasted_iota(jnp.int32, (ends, ends), 1)

    def to_column(row):
        square = jnp.broadcast_to(row, (ends, ends))
        return jnp.sum(jnp.where(sublane == lane, square, 0).astype(jnp.float32), axis=1, keepdims=True)

    end_row = jnp.concatenate([pairs_ref[0:1, :], pairs_ref[1:2, :]], axis=1)
    end_column = to_column(end_row).astype(jnp.int32)
    lanes = lax.broadcasted_iota(jnp.int32, (ends, 128), 1)
    found = jnp.zeros((ends, 128), jnp.int32)
    for row in range(slots_ref.shape[0]):
        found = found + jnp.where(end_column == lanes + row * 128, slots_ref[row : row + 1, :], 0)
    slot_column = jnp.sum(found.astype(jnp.float32), axis=1, keepdims=True).astype(jnp.int32)
    slot_square = jnp.broadcast_to(slot_column, (ends, ends))
    slot_row = jnp.sum(
        jnp.where(sublane == lane, slot_square, 0).astype(jnp.float32), axis=0, keepdims=True
    ).astype(jnp.int32)
    owner_column = slot_column // stations
    owner_row = slot_row // stations
    same_owner = owner_column == owner_row
    rank_column = jnp.sum(
        jnp.where(same_owner & (lane < sublane), 1.0, 0.0), axis=1, keepdims=True
    ).astype(jnp.int32)
    places_ref[...] = jnp.broadcast_to(owner_column * (windows * CAP) + rank_column, places_ref.shape)
    local_column = (slot_column - owner_column * stations).astype(jnp.float32)
    owned = lax.broadcasted_iota(jnp.int32, (owners_count, ends), 0) == owner_row
    ranked = jnp.where(lane == rank_column, jnp.broadcast_to(local_column, (ends, ends)), 0.0)
    wanted_ref[...] = jnp.dot(
        jnp.where(owned, 1.0, 0.0).astype(jnp.bfloat16),
        ranked.astype(jnp.bfloat16),
        preferred_element_type=jnp.float32,
    )


def requests(station_slot, pair_stations, blocks, windows, stations):
    pair_count = pair_stations.shape[0]
    return pl.pallas_call(
        functools.partial(request_kernel, windows, stations),
        out_shape=(
            jax.ShapeDtypeStruct((blocks, 128), jnp.float32),
            jax.ShapeDtypeStruct((2 * pair_count, 128), jnp.int32),
        ),
        name="requests",
    )(station_slot.reshape(-1, 128), pair_stations.T)


def spectrum_kernel(traces_ref, hann_ref, turns_ref, table_ref, out_ref, *scratch):
    count = len(scratch) // 2
    row_count = traces_ref.shape[0] // count
    tables = (hann_ref, turns_ref, table_ref)
    for part in range(count):
        transform_rows(part * row_count, row_count, traces_ref, *tables, out_ref, *scratch[2 * part : 2 * part + 2])


def transform_rows(
    base_row, row_count, traces_ref, hann_ref, turns_ref, table_ref, out_ref, parts_ref, spectrum_ref
):

    def one_group(group):
        first = group * 16
        rows = pl.ds(base_row + first, 16)
        partial_sum = traces_ref[rows, 0:128]
        for tile in range(1, NS // 128):
            partial_sum = partial_sum + traces_ref[rows, tile * 128 : (tile + 1) * 128]
        mean = jnp.sum(partial_sum, axis=1, keepdims=True) * (1.0 / NS)
        for tile in range(SUB // 128):
            x = []
            for block in range(RADIX):
                columns = slice(block * SUB + tile * 128, block * SUB + (tile + 1) * 128)
                x.append((traces_ref[rows, columns] - mean) * hann_ref[:, columns])
            u = [None] + [x[a] + x[RADIX - a] for a in range(1, 6)]
            v = [None] + [x[a] - x[RADIX - a] for a in range(1, 6)]
            e0, o0 = x[0] + x[6], x[0] - x[6]
            p, q = u[1] + u[5], u[2] + u[4]
            pd, qd = u[1] - u[5], u[2] - u[4]
            m, n = v[1] - v[5], v[2] - v[4]
            ms, ns = v[1] + v[5], v[2] + v[4]
            half_pq, half_diff = 0.5 * (p + q), 0.5 * (p - q)
            e_plus, e_minus = e0 + u[3], e0 - u[3]
            base = o0 + 0.5 * qd
            side = ROOT3_2 * pd
            imag_base = 0.5 * ms + v[3]
            imag_side = ROOT3_2 * ns
            real_parts = [
                e_plus + (p + q),
                base + side,
                e_minus + half_diff,
                o0 - qd,
                e_plus - half_pq,
                base - side,
                e_minus - (p - q),
            ]
            imag_parts = [
                None,
                -(imag_base + imag_side),
                -ROOT3_2 * (m + n),
                v[3] - ms,
                -ROOT3_2 * (m - n),
                imag_side - imag_base,
                None,
            ]
            lanes = slice(tile * 128, (tile + 1) * 128)
            imag_lanes = slice(SUB + tile * 128, SUB + (tile + 1) * 128)
            for position, turn in enumerate(TURNS):
                index = min(turn, RADIX - turn)
                real_part, imag_part = real_parts[index], imag_parts[index]
                cos_turn = turns_ref[2 * position : 2 * position + 1, lanes]
                sin_turn = turns_ref[2 * position + 1 : 2 * position + 2, lanes]
                if imag_part is None:
                    turned_real = real_part * cos_turn
                    turned_imag = -(real_part * sin_turn)
                elif index == turn:
                    turned_real = real_part * cos_turn + imag_part * sin_turn
                    turned_imag = imag_part * cos_turn - real_part * sin_turn
                else:
                    turned_real = real_part * cos_turn - imag_part * sin_turn
                    turned_imag = -(imag_part * cos_turn + real_part * sin_turn)
                target = pl.ds(position * row_count + first, 16)
                parts_ref[target, lanes] = turned_real.astype(jnp.bfloat16)
                parts_ref[target, imag_lanes] = turned_imag.astype(jnp.bfloat16)

    for group in range(row_count // 16):
        one_group(group)
    spectrum_ref[...] = jnp.dot(parts_ref[...], table_ref[...], preferred_element_type=jnp.float32)

    def whiten_group(group):
        first = group * 16
        rows = pl.ds(base_row + first, 16)
        total = jnp.zeros((16, DBINS), jnp.float32)
        for position in range(RADIX):
            source = pl.ds(position * row_count + first, 16)
            real_part, imag_part = spectrum_ref[source, :DBINS], spectrum_ref[source, DBINS:]
            total = total + (real_part * real_part + imag_part * imag_part)
        water_level = jnp.sum(total, axis=1, keepdims=True) * (1.0 / F)
        floor = 0.1 * water_level + 1e-06
        for position in range(RADIX):
            source = pl.ds(position * row_count + first, 16)
            real_part, imag_part = spectrum_ref[source, :DBINS], spectrum_ref[source, DBINS:]
            scaling = lax.rsqrt(real_part * real_part + imag_part * imag_part + floor)
            start = position * 2 * DBINS
            out_ref[rows, start : start + DBINS] = (real_part * scaling).astype(jnp.bfloat16)
            out_ref[rows, start + DBINS : start + 2 * DBINS] = (imag_part * scaling).astype(jnp.bfloat16)

    for group in range(row_count // 16):
        whiten_group(group)


def in_hbm(*arrays):
    return [pltpu.with_memory_space_constraint(array, pltpu.HBM) for array in arrays]


def gather_kernel(windows, wanted_ref, whitened_ref, rows_hbm, picks_ref, rows_ref, semaphores):
    slots = rows_ref.shape[0]
    owners, lanes_count = wanted_ref.shape
    stations = whitened_ref.shape[0] // windows
    owner_of = lax.broadcasted_iota(jnp.int32, (slots, owners), 0) // (windows * CAP)
    spread = jnp.where(owner_of == lax.broadcasted_iota(jnp.int32, (slots, owners), 1), 1.0, 0.0)
    lists = jnp.dot(
        spread.astype(jnp.bfloat16), wanted_ref[...].astype(jnp.bfloat16), preferred_element_type=jnp.float32
    )
    slot_ids = lax.broadcasted_iota(jnp.int32, (slots, lanes_count), 0)
    lanes = lax.broadcasted_iota(jnp.int32, (slots, lanes_count), 1)
    row_wanted = jnp.sum(jnp.where(lanes == slot_ids % CAP, lists, 0.0), axis=1, keepdims=True)
    source = row_wanted.astype(jnp.int32) + slot_ids // CAP % windows * stations
    picks_ref[...] = jnp.where(lanes == source, 1.0, 0.0).astype(picks_ref.dtype)
    chunk = slots // GATHER_CHUNKS
    copies = []
    for index in range(GATHER_CHUNKS):
        rows = pl.ds(index * chunk, chunk)
        rows_ref[rows] = jnp.dot(
            picks_ref[rows], whitened_ref[...], preferred_element_type=jnp.float32
        ).astype(rows_ref.dtype)
        copies.append(pltpu.make_async_copy(rows_ref.at[rows], rows_hbm.at[rows], semaphores.at[index]))
        copies[-1].start()
    for copy in copies:
        copy.wait()


GATHER_CHUNKS = 8


def gathered(wanted, whitened, windows):
    slots = wanted.shape[0] * windows * CAP
    shape = (slots, whitened.shape[1])
    vmem = pl.BlockSpec(memory_space=pltpu.VMEM)
    return pl.pallas_call(
        functools.partial(gather_kernel, windows),
        out_shape=pltpu.HBM(shape, whitened.dtype),
        in_specs=[vmem, vmem],
        out_specs=pl.BlockSpec(memory_space=pltpu.HBM),
        scratch_shapes=[
            pltpu.VMEM((slots, whitened.shape[0]), whitened.dtype),
            pltpu.VMEM(shape, whitened.dtype),
            pltpu.SemaphoreType.DMA((GATHER_CHUNKS,)),
        ],
        compiler_params=pltpu.CompilerParams(vmem_limit_bytes=16 << 20),
        name="gathered",
    )(wanted, whitened)


PART_ROWS = 32
STEP_PARTS = 2


def whitened_spectra(traces):
    total = traces.shape[0]
    rows = PART_ROWS * STEP_PARTS
    table, turns = spectrum_tables()
    scratch = [
        pltpu.VMEM((RADIX * PART_ROWS, 2 * SUB), jnp.bfloat16),
        pltpu.VMEM((RADIX * PART_ROWS, 2 * DBINS), jnp.float32),
    ]
    return pl.pallas_call(
        spectrum_kernel,
        out_shape=jax.ShapeDtypeStruct((total, 2 * F), jnp.bfloat16),
        grid_spec=pltpu.PrefetchScalarGridSpec(
            num_scalar_prefetch=0,
            grid=(total // rows,),
            in_specs=[
                pl.BlockSpec((rows, NS), lambda s: (s, 0)),
                pl.BlockSpec((1, NS), lambda s: (0, 0)),
                pl.BlockSpec((2 * RADIX, SUB), lambda s: (0, 0)),
                pl.BlockSpec((2 * SUB, 2 * DBINS), lambda s: (0, 0)),
            ],
            out_specs=pl.BlockSpec((rows, 2 * F), lambda s: (s, 0)),
            scratch_shapes=scratch * STEP_PARTS,
        ),
        compiler_params=pltpu.CompilerParams(
            dimension_semantics=("arbitrary",), vmem_limit_bytes=24 << 20
        ),
        cost_estimate=pl.CostEstimate(
            flops=2 * total * RADIX * 2 * SUB * 2 * DBINS,
            bytes_accessed=5_000_000,
            transcendentals=total * F,
        ),
        name="whitened_spectra",
    )(*in_hbm(traces, jnp.asarray(hann_window()), jnp.asarray(turns), jnp.asarray(table)))


def lag_kernel(
    place_ref, places_ref, received_ref, inner_ref, outer_ref, kept_ref, sent_ref,
    select_ref, stacked_ref, turned_ref, sums_ref,
):
    slots = received_ref.shape[0]
    ends = places_ref.shape[0]
    pairs = ends // 2
    windows = select_ref.shape[0] // ends
    lanes = lax.broadcasted_iota(jnp.int32, (ends, 128), 1)
    places = places_ref[...]
    for window in range(windows):
        for tile in range(slots // 128):
            hit = jnp.where(places + window * CAP == lanes + tile * 128, 1.0, 0.0)
            rows = slice(window * ends, (window + 1) * ends)
            select_ref[rows, tile * 128 : (tile + 1) * 128] = hit.astype(jnp.bfloat16)

    bins = lax.broadcasted_iota(jnp.int32, (1, DBINS), 1)
    even = bins % 2 == 0
    flip_odd = jnp.where(even, 1.0, -1.0)
    flip_upper = jnp.where(bins % 4 < 2, 1.0, -1.0)
    residue_rows = RADIX * pairs
    for step in range(STEPS):
        columns = slice(step * 4 * DBINS, (step + 1) * 4 * DBINS)
        picked = jnp.dot(select_ref[...], received_ref[:, columns], preferred_element_type=jnp.float32)
        for half in range(2):
            real_columns = slice(half * 2 * DBINS, half * 2 * DBINS + DBINS)
            imag_columns = slice(half * 2 * DBINS + DBINS, (half + 1) * 2 * DBINS)
            real_sum = imag_sum = None
            for window in range(windows):
                left = slice(window * ends, window * ends + pairs)
                right = slice(window * ends + pairs, (window + 1) * ends)
                left_real, left_imag = picked[left, real_columns], picked[left, imag_columns]
                right_real, right_imag = picked[right, real_columns], picked[right, imag_columns]
                real_term = left_real * right_real + left_imag * right_imag
                imag_term = left_imag * right_real - left_real * right_imag
                real_sum = real_term if real_sum is None else real_sum + real_term
                imag_sum = imag_term if imag_sum is None else imag_sum + imag_term
            quarter_real = jnp.where(even, real_sum, -imag_sum) * flip_upper
            quarter_imag = jnp.where(even, imag_sum, real_sum) * flip_upper
            quarters = [
                (real_sum, imag_sum),
                (quarter_real, quarter_imag),
                (real_sum * flip_odd, imag_sum * flip_odd),
                (quarter_real * flip_odd, quarter_imag * flip_odd),
            ]
            position = 2 * step + half
            for quarter, (real_part, imag_part) in enumerate(quarters):
                first = quarter * residue_rows + position * pairs
                stacked_ref[first : first + pairs, :DBINS] = real_part.astype(jnp.bfloat16)
                stacked_ref[first : first + pairs, DBINS:] = imag_part.astype(jnp.bfloat16)

    turned_ref[...] = jnp.dot(stacked_ref[...], inner_ref[...], preferred_element_type=jnp.float32)

    for tile in range(SUB // 128):
        columns = slice(tile * 128, (tile + 1) * 128)
        for group in range(pairs // 8):
            real_of, imag_of = {}, {}
            for position, turn in enumerate(TURNS):
                first = tile * residue_rows + position * pairs + group * 8
                real_part, imag_part = turned_ref[first : first + 8, :DBINS], turned_ref[first : first + 8, DBINS:]
                cos_turn = outer_ref[2 * position : 2 * position + 1, columns]
                sin_turn = outer_ref[2 * position + 1 : 2 * position + 2, columns]
                real_of[turn] = real_part * cos_turn - imag_part * sin_turn
                if turn % STEPS:
                    imag_of[turn] = real_part * sin_turn + imag_part * cos_turn
            r0, r6 = real_of[0], real_of[6]
            re = [None] + [real_of[r] + real_of[RADIX - r] for r in range(1, STEPS)]
            im = [None] + [imag_of[r] - imag_of[RADIX - r] for r in range(1, STEPS)]
            even, odd = re[2] + re[4], re[1] + re[5]
            q_zero = (r0 + r6) + (even + odd + re[3])
            q_one_real = (r0 - r6) + 0.5 * (re[2] - re[4]) + ROOT3_2 * (re[1] - re[5])
            q_one_imag = 0.5 * (im[1] + im[5]) + ROOT3_2 * (im[2] + im[4]) + im[3]
            q_two_real = (r0 + r6) + 0.5 * (re[1] + re[5] - even) - re[3]
            q_two_imag = ROOT3_2 * (im[1] + im[2] - im[4] - im[5])
            periods = [q_two_real + q_two_imag, q_one_real + q_one_imag, q_zero, q_one_real - q_one_imag]
            for period, values in enumerate(periods):
                sums_ref[group * 8 : group * 8 + 8, period * SUB + tile * 128 : period * SUB + (tile + 1) * 128] = values

    rings = kept_ref.shape[0]
    share = kept_ref.shape[2]
    for offset in range(rings):
        ring = lax.rem(place_ref[0] + offset, rings)
        kept = pl.multiple_of((2 * ring + place_ref[1]) * share, share)
        sent = pl.multiple_of((2 * ring + 1 - place_ref[1]) * share, share)
        kept_ref[offset] = sums_ref[:, pl.ds(kept, share)]
        sent_ref[offset] = sums_ref[:, pl.ds(sent, share)].astype(sent_ref.dtype)


def lag_sums(place, places, received, parts, normalizer):
    ends = places.shape[0]
    slots = received.shape[0]
    pairs = ends // 2
    windows = slots // (32 * CAP)
    inner, outer = lag_tables(normalizer)
    share = 2 * LAG // parts
    vmem = pl.BlockSpec(memory_space=pltpu.VMEM)
    return pl.pallas_call(
        lag_kernel,
        out_shape=(
            jax.ShapeDtypeStruct((parts // 2, pairs, share), jnp.float32),
            jax.ShapeDtypeStruct((parts // 2, pairs, share), jnp.bfloat16),
        ),
        in_specs=[pl.BlockSpec(memory_space=pltpu.SMEM)] + [vmem] * 4,
        out_specs=(vmem, vmem),
        scratch_shapes=[
            pltpu.VMEM((windows * ends, slots), jnp.bfloat16),
            pltpu.VMEM((SUB // DBINS * RADIX * pairs, 2 * DBINS), jnp.bfloat16),
            pltpu.VMEM((SUB // DBINS * RADIX * pairs, 2 * DBINS), jnp.float32),
            pltpu.VMEM((pairs, 2 * LAG), jnp.float32),
        ],
        compiler_params=pltpu.CompilerParams(vmem_limit_bytes=32 << 20),
        cost_estimate=pl.CostEstimate(
            flops=2 * windows * ends * slots * 2 * F, bytes_accessed=5_000_000, transcendentals=0
        ),
        name="lag_sums",
    )(place, places, received, jnp.asarray(inner), jnp.asarray(outer))


def add_kernel(kept_ref, got_ref, own_ref, *sent_refs):
    own_ref[...] = kept_ref[0] + got_ref[0].astype(jnp.float32)
    for offset, sent_ref in enumerate(sent_refs, 1):
        sent_ref[...] = (kept_ref[offset] + got_ref[offset].astype(jnp.float32)).astype(sent_ref.dtype)


def total_kernel(own_ref, *rest):
    total = own_ref[...]
    for got_ref in rest[:-1]:
        total = total + got_ref[...].astype(jnp.float32)
    rest[-1][...] = total


def window_total(kept, sent):
    rings, pairs, share = kept.shape
    devices = range(2 * rings)
    got = lax.ppermute(sent, "tm", [(source, source ^ 1) for source in devices])
    params = pltpu.CompilerParams(vmem_limit_bytes=16 << 20)
    own, *onward = pl.pallas_call(
        add_kernel,
        out_shape=[jax.ShapeDtypeStruct((pairs, share), jnp.float32)]
        + [jax.ShapeDtypeStruct((pairs, share), jnp.bfloat16)] * (rings - 1),
        compiler_params=params,
        name="core_total",
    )(kept, got)
    arrived = []
    for offset, values in enumerate(onward, 1):
        targets = [(source, (source // 2 + offset) % rings * 2 + source % 2) for source in devices]
        arrived.append(lax.ppermute(values, "tm", targets))
    return pl.pallas_call(
        total_kernel,
        out_shape=jax.ShapeDtypeStruct((pairs, share), jnp.float32),
        compiler_params=params,
        name="window_total",
    )(own, *arrived).T


def on_device(traces, station_slot, pair_stations):
    window_count, station_count, length = traces.shape
    blocks = lax.axis_size("pairs")
    lag_parts = lax.axis_size("tm")
    slots = blocks * window_count * CAP
    normalizer = 1.0 / math.sqrt(F * window_count * lag_parts)
    own = lax.axis_index("tm")
    place = jnp.stack([own // 2, own % 2]).astype(jnp.int32)
    wanted, places = requests(station_slot, pair_stations, blocks, window_count, station_count)
    lists = lax.all_to_all(wanted[:, None, :], "pairs", split_axis=0, concat_axis=0, tiled=True)
    whitened = whitened_spectra(traces.reshape(window_count * station_count, length))
    rows = gathered(lists.reshape(wanted.shape), whitened, window_count)
    received = lax.all_to_all(
        rows.reshape(blocks, window_count * CAP, 2 * F), "pairs", split_axis=0, concat_axis=0, tiled=True
    )
    kept, sent = lag_sums(place, places, received.reshape(slots, 2 * F), lag_parts, normalizer)
    return window_total(kept, sent)


def solution(mesh):
    in_specs = (P("tm", "pairs", None), P(), P("pairs", None))
    out_specs = P("tm", "pairs")
    return jax.shard_map(
        on_device, mesh=mesh, in_specs=in_specs, out_specs=out_specs, check_vma=False
    )
```

```python
import functools
import math

import jax
import jax.numpy as jnp
import ml_dtypes
import numpy as np
from jax import lax
from jax.experimental import pallas as pl
from jax.experimental.pallas import tpu as pltpu
from jax.sharding import PartitionSpec as P

F = 1536
FLO = 32
LAG = 1024
NS = 6144
RADIX = 12
SUB = NS // RADIX
DBINS = F // RADIX
STEPS = RADIX // 2
CAP = 8
ROOT3_2 = math.sqrt(3.0) / 2.0

TURNS = [0, 6] + [turn for step in range(1, STEPS) for turn in (step, RADIX - step)]
RESIDUES = [(turn - FLO) % RADIX for turn in TURNS]


def spectrum_tables():
    sub_times = np.arange(SUB, dtype=np.int64)[:, None]
    bins = np.arange(DBINS, dtype=np.int64)[None, :]
    angles = (sub_times * bins % SUB) * (2.0 * np.pi / SUB)
    cos_part, sin_part = np.cos(angles), np.sin(angles)
    inner = np.block([[cos_part, -sin_part], [sin_part, cos_part]]).astype(ml_dtypes.bfloat16)
    first_bins = FLO + np.array(RESIDUES, dtype=np.int64)[:, None]
    turn_angles = (first_bins * sub_times[:, 0][None, :] % NS) * (2.0 * np.pi / NS)
    turns = np.stack([np.cos(turn_angles), np.sin(turn_angles)], axis=1)
    return inner, turns.reshape(2 * RADIX, SUB).astype(np.float32)


def hann_window():
    times = np.arange(NS, dtype=np.float64)
    return (0.5 - 0.5 * np.cos((times + 0.5) * (2.0 * np.pi / NS))).astype(np.float32)[None, :]


def lag_tables(normalizer):
    bins = np.arange(DBINS, dtype=np.int64)[:, None]
    sub_lags = np.arange(SUB, dtype=np.int64)[None, :]
    angles = (bins * sub_lags % SUB)[:, :DBINS] * (2.0 * np.pi / SUB)
    cos_part, sin_part = np.cos(angles), np.sin(angles)
    inner = np.block([[cos_part, sin_part], [-sin_part, cos_part]]).astype(ml_dtypes.bfloat16)
    first_bins = FLO + np.array(RESIDUES, dtype=np.int64)[:, None]
    outer_angles = (first_bins * sub_lags % NS) * (2.0 * np.pi / NS)
    outer = np.stack([np.cos(outer_angles), np.sin(outer_angles)], axis=1) * normalizer
    return inner, outer.reshape(2 * RADIX, SUB).astype(np.float32)


def request_kernel(windows, stations, slots_ref, pairs_ref, wanted_ref, places_ref):
    ends = 2 * pairs_ref.shape[1]
    owners_count = wanted_ref.shape[0]
    sublane = lax.broadcasted_iota(jnp.int32, (ends, ends), 0)
    lane = lax.broadcasted_iota(jnp.int32, (ends, ends), 1)

    def to_column(row):
        square = jnp.broadcast_to(row, (ends, ends))
        return jnp.sum(jnp.where(sublane == lane, square, 0).astype(jnp.float32), axis=1, keepdims=True)

    end_row = jnp.concatenate([pairs_ref[0:1, :], pairs_ref[1:2, :]], axis=1)
    end_column = to_column(end_row).astype(jnp.int32)
    lanes = lax.broadcasted_iota(jnp.int32, (ends, 128), 1)
    found = jnp.zeros((ends, 128), jnp.int32)
    for row in range(slots_ref.shape[0]):
        found = found + jnp.where(end_column == lanes + row * 128, slots_ref[row : row + 1, :], 0)
    slot_column = jnp.sum(found.astype(jnp.float32), axis=1, keepdims=True).astype(jnp.int32)
    slot_square = jnp.broadcast_to(slot_column, (ends, ends))
    slot_row = jnp.sum(
        jnp.where(sublane == lane, slot_square, 0).astype(jnp.float32), axis=0, keepdims=True
    ).astype(jnp.int32)
    owner_column = slot_column // stations
    owner_row = slot_row // stations
    same_owner = owner_column == owner_row
    rank_column = jnp.sum(
        jnp.where(same_owner & (lane < sublane), 1.0, 0.0), axis=1, keepdims=True
    ).astype(jnp.int32)
    places_ref[...] = jnp.broadcast_to(owner_column * (windows * CAP) + rank_column, places_ref.shape)
    local_column = (slot_column - owner_column * stations).astype(jnp.float32)
    owned = lax.broadcasted_iota(jnp.int32, (owners_count, ends), 0) == owner_row
    ranked = jnp.where(lane == rank_column, jnp.broadcast_to(local_column, (ends, ends)), 0.0)
    wanted_ref[...] = jnp.dot(
        jnp.where(owned, 1.0, 0.0).astype(jnp.bfloat16),
        ranked.astype(jnp.bfloat16),
        preferred_element_type=jnp.float32,
    )


def requests(station_slot, pair_stations, blocks, windows, stations):
    pair_count = pair_stations.shape[0]
    return pl.pallas_call(
        functools.partial(request_kernel, windows, stations),
        out_shape=(
            jax.ShapeDtypeStruct((blocks, 128), jnp.float32),
            jax.ShapeDtypeStruct((2 * pair_count, 128), jnp.int32),
        ),
        name="requests",
    )(station_slot.reshape(-1, 128), pair_stations.T)


def spectrum_kernel(traces_ref, hann_ref, turns_ref, table_ref, out_ref, *scratch):
    count = len(scratch) // 2
    row_count = traces_ref.shape[0] // count
    tables = (hann_ref, turns_ref, table_ref)
    for part in range(count):
        transform_rows(part * row_count, row_count, traces_ref, *tables, out_ref, *scratch[2 * part : 2 * part + 2])


def transform_rows(
    base_row, row_count, traces_ref, hann_ref, turns_ref, table_ref, out_ref, parts_ref, spectrum_ref
):

    def one_group(group):
        first = group * 16
        rows = pl.ds(base_row + first, 16)
        partial_sum = traces_ref[rows, 0:128]
        for tile in range(1, NS // 128):
            partial_sum = partial_sum + traces_ref[rows, tile * 128 : (tile + 1) * 128]
        mean = jnp.sum(partial_sum, axis=1, keepdims=True) * (1.0 / NS)
        for tile in range(SUB // 128):
            x = []
            for block in range(RADIX):
                columns = slice(block * SUB + tile * 128, block * SUB + (tile + 1) * 128)
                x.append((traces_ref[rows, columns] - mean) * hann_ref[:, columns])
            u = [None] + [x[a] + x[RADIX - a] for a in range(1, 6)]
            v = [None] + [x[a] - x[RADIX - a] for a in range(1, 6)]
            e0, o0 = x[0] + x[6], x[0] - x[6]
            p, q = u[1] + u[5], u[2] + u[4]
            pd, qd = u[1] - u[5], u[2] - u[4]
            m, n = v[1] - v[5], v[2] - v[4]
            ms, ns = v[1] + v[5], v[2] + v[4]
            half_pq, half_diff = 0.5 * (p + q), 0.5 * (p - q)
            e_plus, e_minus = e0 + u[3], e0 - u[3]
            base = o0 + 0.5 * qd
            side = ROOT3_2 * pd
            imag_base = 0.5 * ms + v[3]
            imag_side = ROOT3_2 * ns
            real_parts = [
                e_plus + (p + q),
                base + side,
                e_minus + half_diff,
                o0 - qd,
                e_plus - half_pq,
                base - side,
                e_minus - (p - q),
            ]
            imag_parts = [
                None,
                -(imag_base + imag_side),
                -ROOT3_2 * (m + n),
                v[3] - ms,
                -ROOT3_2 * (m - n),
                imag_side - imag_base,
                None,
            ]
            lanes = slice(tile * 128, (tile + 1) * 128)
            imag_lanes = slice(SUB + tile * 128, SUB + (tile + 1) * 128)
            for position, turn in enumerate(TURNS):
                index = min(turn, RADIX - turn)
                real_part, imag_part = real_parts[index], imag_parts[index]
                cos_turn = turns_ref[2 * position : 2 * position + 1, lanes]
                sin_turn = turns_ref[2 * position + 1 : 2 * position + 2, lanes]
                if imag_part is None:
                    turned_real = real_part * cos_turn
                    turned_imag = -(real_part * sin_turn)
                elif index == turn:
                    turned_real = real_part * cos_turn + imag_part * sin_turn
                    turned_imag = imag_part * cos_turn - real_part * sin_turn
                else:
                    turned_real = real_part * cos_turn - imag_part * sin_turn
                    turned_imag = -(imag_part * cos_turn + real_part * sin_turn)
                target = pl.ds(position * row_count + first, 16)
                parts_ref[target, lanes] = turned_real.astype(jnp.bfloat16)
                parts_ref[target, imag_lanes] = turned_imag.astype(jnp.bfloat16)

    for group in range(row_count // 16):
        one_group(group)
    spectrum_ref[...] = jnp.dot(parts_ref[...], table_ref[...], preferred_element_type=jnp.float32)

    def whiten_group(group):
        first = group * 16
        rows = pl.ds(base_row + first, 16)
        total = jnp.zeros((16, DBINS), jnp.float32)
        for position in range(RADIX):
            source = pl.ds(position * row_count + first, 16)
            real_part, imag_part = spectrum_ref[source, :DBINS], spectrum_ref[source, DBINS:]
            total = total + (real_part * real_part + imag_part * imag_part)
        water_level = jnp.sum(total, axis=1, keepdims=True) * (1.0 / F)
        floor = 0.1 * water_level + 1e-06
        for position in range(RADIX):
            source = pl.ds(position * row_count + first, 16)
            real_part, imag_part = spectrum_ref[source, :DBINS], spectrum_ref[source, DBINS:]
            scaling = lax.rsqrt(real_part * real_part + imag_part * imag_part + floor)
            start = position * 2 * DBINS
            out_ref[rows, start : start + DBINS] = (real_part * scaling).astype(jnp.bfloat16)
            out_ref[rows, start + DBINS : start + 2 * DBINS] = (imag_part * scaling).astype(jnp.bfloat16)

    for group in range(row_count // 16):
        whiten_group(group)


def in_hbm(*arrays):
    return [pltpu.with_memory_space_constraint(array, pltpu.HBM) for array in arrays]


def gather_kernel(windows, wanted_ref, whitened_ref, rows_hbm, picks_ref, rows_ref, semaphores):
    slots = rows_ref.shape[0]
    owners, lanes_count = wanted_ref.shape
    stations = whitened_ref.shape[0] // windows
    owner_of = lax.broadcasted_iota(jnp.int32, (slots, owners), 0) // (windows * CAP)
    spread = jnp.where(owner_of == lax.broadcasted_iota(jnp.int32, (slots, owners), 1), 1.0, 0.0)
    lists = jnp.dot(
        spread.astype(jnp.bfloat16), wanted_ref[...].astype(jnp.bfloat16), preferred_element_type=jnp.float32
    )
    slot_ids = lax.broadcasted_iota(jnp.int32, (slots, lanes_count), 0)
    lanes = lax.broadcasted_iota(jnp.int32, (slots, lanes_count), 1)
    row_wanted = jnp.sum(jnp.where(lanes == slot_ids % CAP, lists, 0.0), axis=1, keepdims=True)
    source = row_wanted.astype(jnp.int32) + slot_ids // CAP % windows * stations
    picks_ref[...] = jnp.where(lanes == source, 1.0, 0.0).astype(picks_ref.dtype)
    chunk = slots // GATHER_CHUNKS
    copies = []
    for index in range(GATHER_CHUNKS):
        rows = pl.ds(index * chunk, chunk)
        rows_ref[rows] = jnp.dot(
            picks_ref[rows], whitened_ref[...], preferred_element_type=jnp.float32
        ).astype(rows_ref.dtype)
        copies.append(pltpu.make_async_copy(rows_ref.at[rows], rows_hbm.at[rows], semaphores.at[index]))
        copies[-1].start()
    for copy in copies:
        copy.wait()


GATHER_CHUNKS = 8


def gathered(wanted, whitened, windows):
    slots = wanted.shape[0] * windows * CAP
    shape = (slots, whitened.shape[1])
    vmem = pl.BlockSpec(memory_space=pltpu.VMEM)
    return pl.pallas_call(
        functools.partial(gather_kernel, windows),
        out_shape=pltpu.HBM(shape, whitened.dtype),
        in_specs=[vmem, vmem],
        out_specs=pl.BlockSpec(memory_space=pltpu.HBM),
        scratch_shapes=[
            pltpu.VMEM((slots, whitened.shape[0]), whitened.dtype),
            pltpu.VMEM(shape, whitened.dtype),
            pltpu.SemaphoreType.DMA((GATHER_CHUNKS,)),
        ],
        compiler_params=pltpu.CompilerParams(vmem_limit_bytes=16 << 20),
        name="gathered",
    )(wanted, whitened)


PART_ROWS = 32
STEP_PARTS = 2


def whitened_spectra(traces):
    total = traces.shape[0]
    rows = PART_ROWS * STEP_PARTS
    table, turns = spectrum_tables()
    scratch = [
        pltpu.VMEM((RADIX * PART_ROWS, 2 * SUB), jnp.bfloat16),
        pltpu.VMEM((RADIX * PART_ROWS, 2 * DBINS), jnp.float32),
    ]
    return pl.pallas_call(
        spectrum_kernel,
        out_shape=jax.ShapeDtypeStruct((total, 2 * F), jnp.bfloat16),
        grid_spec=pltpu.PrefetchScalarGridSpec(
            num_scalar_prefetch=0,
            grid=(total // rows,),
            in_specs=[
                pl.BlockSpec((rows, NS), lambda s: (s, 0)),
                pl.BlockSpec((1, NS), lambda s: (0, 0)),
                pl.BlockSpec((2 * RADIX, SUB), lambda s: (0, 0)),
                pl.BlockSpec((2 * SUB, 2 * DBINS), lambda s: (0, 0)),
            ],
            out_specs=pl.BlockSpec((rows, 2 * F), lambda s: (s, 0)),
            scratch_shapes=scratch * STEP_PARTS,
        ),
        compiler_params=pltpu.CompilerParams(
            dimension_semantics=("arbitrary",), vmem_limit_bytes=24 << 20
        ),
        cost_estimate=pl.CostEstimate(
            flops=2 * total * RADIX * 2 * SUB * 2 * DBINS,
            bytes_accessed=5_000_000,
            transcendentals=total * F,
        ),
        name="whitened_spectra",
    )(*in_hbm(traces, jnp.asarray(hann_window()), jnp.asarray(turns), jnp.asarray(table)))


def lag_kernel(
    place_ref, places_ref, received_ref, inner_ref, outer_ref, kept_ref, sent_ref,
    select_ref, stacked_ref, turned_ref, sums_ref,
):
    slots = received_ref.shape[0]
    ends = places_ref.shape[0]
    pairs = ends // 2
    windows = select_ref.shape[0] // ends
    lanes = lax.broadcasted_iota(jnp.int32, (ends, 128), 1)
    places = places_ref[...]
    for window in range(windows):
        for tile in range(slots // 128):
            hit = jnp.where(places + window * CAP == lanes + tile * 128, 1.0, 0.0)
            rows = slice(window * ends, (window + 1) * ends)
            select_ref[rows, tile * 128 : (tile + 1) * 128] = hit.astype(jnp.bfloat16)

    bins = lax.broadcasted_iota(jnp.int32, (1, DBINS), 1)
    even = bins % 2 == 0
    flip_odd = jnp.where(even, 1.0, -1.0)
    flip_upper = jnp.where(bins % 4 < 2, 1.0, -1.0)
    residue_rows = RADIX * pairs
    for step in range(STEPS):
        columns = slice(step * 4 * DBINS, (step + 1) * 4 * DBINS)
        picked = jnp.dot(select_ref[...], received_ref[:, columns], preferred_element_type=jnp.float32)
        for half in range(2):
            real_columns = slice(half * 2 * DBINS, half * 2 * DBINS + DBINS)
            imag_columns = slice(half * 2 * DBINS + DBINS, (half + 1) * 2 * DBINS)
            real_sum = imag_sum = None
            for window in range(windows):
                left = slice(window * ends, window * ends + pairs)
                right = slice(window * ends + pairs, (window + 1) * ends)
                left_real, left_imag = picked[left, real_columns], picked[left, imag_columns]
                right_real, right_imag = picked[right, real_columns], picked[right, imag_columns]
                real_term = left_real * right_real + left_imag * right_imag
                imag_term = left_imag * right_real - left_real * right_imag
                real_sum = real_term if real_sum is None else real_sum + real_term
                imag_sum = imag_term if imag_sum is None else imag_sum + imag_term
            quarter_real = jnp.where(even, real_sum, -imag_sum) * flip_upper
            quarter_imag = jnp.where(even, imag_sum, real_sum) * flip_upper
            quarters = [
                (real_sum, imag_sum),
                (quarter_real, quarter_imag),
                (real_sum * flip_odd, imag_sum * flip_odd),
                (quarter_real * flip_odd, quarter_imag * flip_odd),
            ]
            position = 2 * step + half
            for quarter, (real_part, imag_part) in enumerate(quarters):
                first = quarter * residue_rows + position * pairs
                stacked_ref[first : first + pairs, :DBINS] = real_part.astype(jnp.bfloat16)
                stacked_ref[first : first + pairs, DBINS:] = imag_part.astype(jnp.bfloat16)

    turned_ref[...] = jnp.dot(stacked_ref[...], inner_ref[...], preferred_element_type=jnp.float32)

    for tile in range(SUB // 128):
        columns = slice(tile * 128, (tile + 1) * 128)
        for group in range(pairs // 8):
            real_of, imag_of = {}, {}
            for position, turn in enumerate(TURNS):
                first = tile * residue_rows + position * pairs + group * 8
                real_part, imag_part = turned_ref[first : first + 8, :DBINS], turned_ref[first : first + 8, DBINS:]
                cos_turn = outer_ref[2 * position : 2 * position + 1, columns]
                sin_turn = outer_ref[2 * position + 1 : 2 * position + 2, columns]
                real_of[turn] = real_part * cos_turn - imag_part * sin_turn
                if turn % STEPS:
                    imag_of[turn] = real_part * sin_turn + imag_part * cos_turn
            r0, r6 = real_of[0], real_of[6]
            re = [None] + [real_of[r] + real_of[RADIX - r] for r in range(1, STEPS)]
            im = [None] + [imag_of[r] - imag_of[RADIX - r] for r in range(1, STEPS)]
            even, odd = re[2] + re[4], re[1] + re[5]
            q_zero = (r0 + r6) + (even + odd + re[3])
            q_one_real = (r0 - r6) + 0.5 * (re[2] - re[4]) + ROOT3_2 * (re[1] - re[5])
            q_one_imag = 0.5 * (im[1] + im[5]) + ROOT3_2 * (im[2] + im[4]) + im[3]
            q_two_real = (r0 + r6) + 0.5 * (re[1] + re[5] - even) - re[3]
            q_two_imag = ROOT3_2 * (im[1] + im[2] - im[4] - im[5])
            periods = [q_two_real + q_two_imag, q_one_real + q_one_imag, q_zero, q_one_real - q_one_imag]
            for period, values in enumerate(periods):
                sums_ref[group * 8 : group * 8 + 8, period * SUB + tile * 128 : period * SUB + (tile + 1) * 128] = values

    rings = kept_ref.shape[0]
    share = kept_ref.shape[2]
    for offset in range(rings):
        ring = lax.rem(place_ref[0] + offset, rings)
        kept = pl.multiple_of((2 * ring + place_ref[1]) * share, share)
        sent = pl.multiple_of((2 * ring + 1 - place_ref[1]) * share, share)
        kept_ref[offset] = sums_ref[:, pl.ds(kept, share)]
        sent_ref[offset] = sums_ref[:, pl.ds(sent, share)].astype(sent_ref.dtype)


def lag_sums(place, places, received, parts, normalizer):
    ends = places.shape[0]
    slots = received.shape[0]
    pairs = ends // 2
    windows = slots // (32 * CAP)
    inner, outer = lag_tables(normalizer)
    share = 2 * LAG // parts
    vmem = pl.BlockSpec(memory_space=pltpu.VMEM)
    return pl.pallas_call(
        lag_kernel,
        out_shape=(
            jax.ShapeDtypeStruct((parts // 2, pairs, share), jnp.float32),
            jax.ShapeDtypeStruct((parts // 2, pairs, share), jnp.bfloat16),
        ),
        in_specs=[pl.BlockSpec(memory_space=pltpu.SMEM)] + [vmem] * 4,
        out_specs=(vmem, vmem),
        scratch_shapes=[
            pltpu.VMEM((windows * ends, slots), jnp.bfloat16),
            pltpu.VMEM((SUB // DBINS * RADIX * pairs, 2 * DBINS), jnp.bfloat16),
            pltpu.VMEM((SUB // DBINS * RADIX * pairs, 2 * DBINS), jnp.float32),
            pltpu.VMEM((pairs, 2 * LAG), jnp.float32),
        ],
        compiler_params=pltpu.CompilerParams(vmem_limit_bytes=32 << 20),
        cost_estimate=pl.CostEstimate(
            flops=2 * windows * ends * slots * 2 * F, bytes_accessed=5_000_000, transcendentals=0
        ),
        name="lag_sums",
    )(place, places, received, jnp.asarray(inner), jnp.asarray(outer))


def add_kernel(kept_ref, got_ref, own_ref, *sent_refs):
    own_ref[...] = kept_ref[0] + got_ref[0].astype(jnp.float32)
    for offset, sent_ref in enumerate(sent_refs, 1):
        sent_ref[...] = (kept_ref[offset] + got_ref[offset].astype(jnp.float32)).astype(sent_ref.dtype)


def total_kernel(own_ref, *rest):
    total = own_ref[...]
    for got_ref in rest[:-1]:
        total = total + got_ref[...].astype(jnp.float32)
    rest[-1][...] = total


def window_total(kept, sent):
    rings, pairs, share = kept.shape
    devices = range(2 * rings)
    got = lax.ppermute(sent, "tm", [(source, source ^ 1) for source in devices])
    params = pltpu.CompilerParams(vmem_limit_bytes=16 << 20)
    own, *onward = pl.pallas_call(
        add_kernel,
        out_shape=[jax.ShapeDtypeStruct((pairs, share), jnp.float32)]
        + [jax.ShapeDtypeStruct((pairs, share), jnp.bfloat16)] * (rings - 1),
        compiler_params=params,
        name="core_total",
    )(kept, got)
    arrived = []
    for offset, values in enumerate(onward, 1):
        targets = [(source, (source // 2 + offset) % rings * 2 + source % 2) for source in devices]
        arrived.append(lax.ppermute(values, "tm", targets))
    return pl.pallas_call(
        total_kernel,
        out_shape=jax.ShapeDtypeStruct((pairs, share), jnp.float32),
        compiler_params=params,
        name="window_total",
    )(own, *arrived).T


def on_device(traces, station_slot, pair_stations):
    window_count, station_count, length = traces.shape
    blocks = lax.axis_size("pairs")
    lag_parts = lax.axis_size("tm")
    slots = blocks * window_count * CAP
    normalizer = 1.0 / math.sqrt(F * window_count * lag_parts)
    own = lax.axis_index("tm")
    place = jnp.stack([own // 2, own % 2]).astype(jnp.int32)
    wanted, places = requests(station_slot, pair_stations, blocks, window_count, station_count)
    lists = lax.all_to_all(wanted[:, None, :], "pairs", split_axis=0, concat_axis=0, tiled=True)
    traces, lists = lax.optimization_barrier((traces, lists))
    whitened = whitened_spectra(traces.reshape(window_count * station_count, length))
    rows = gathered(lists.reshape(wanted.shape), whitened, window_count)
    received = lax.all_to_all(
        rows.reshape(blocks, window_count * CAP, 2 * F), "pairs", split_axis=0, concat_axis=0, tiled=True
    )
    kept, sent = lag_sums(place, places, received.reshape(slots, 2 * F), lag_parts, normalizer)
    return window_total(kept, sent)


def solution(mesh):
    in_specs = (P("tm", "pairs", None), P(), P("pairs", None))
    out_specs = P("tm", "pairs")
    return jax.shard_map(
        on_device, mesh=mesh, in_specs=in_specs, out_specs=out_specs, check_vma=False
    )
```

```python
import functools
import math

import jax
import jax.numpy as jnp
import ml_dtypes
import numpy as np
from jax import lax
from jax.experimental import pallas as pl
from jax.experimental.pallas import tpu as pltpu
from jax.sharding import PartitionSpec as P

F = 1536
FLO = 32
LAG = 1024
NS = 6144
RADIX = 12
SUB = NS // RADIX
DBINS = F // RADIX
STEPS = RADIX // 2
CAP = 8
ROOT3_2 = math.sqrt(3.0) / 2.0

TURNS = [0, 6] + [turn for step in range(1, STEPS) for turn in (step, RADIX - step)]
RESIDUES = [(turn - FLO) % RADIX for turn in TURNS]


def spectrum_tables():
    sub_times = np.arange(SUB, dtype=np.int64)[:, None]
    bins = np.arange(DBINS, dtype=np.int64)[None, :]
    angles = (sub_times * bins % SUB) * (2.0 * np.pi / SUB)
    cos_part, sin_part = np.cos(angles), np.sin(angles)
    inner = np.block([[cos_part, -sin_part], [sin_part, cos_part]]).astype(ml_dtypes.bfloat16)
    first_bins = FLO + np.array(RESIDUES, dtype=np.int64)[:, None]
    turn_angles = (first_bins * sub_times[:, 0][None, :] % NS) * (2.0 * np.pi / NS)
    turns = np.stack([np.cos(turn_angles), np.sin(turn_angles)], axis=1)
    return inner, turns.reshape(2 * RADIX, SUB).astype(np.float32)


def hann_window():
    times = np.arange(NS, dtype=np.float64)
    return (0.5 - 0.5 * np.cos((times + 0.5) * (2.0 * np.pi / NS))).astype(np.float32)[None, :]


def lag_tables(normalizer):
    bins = np.arange(DBINS, dtype=np.int64)[:, None]
    sub_lags = np.arange(SUB, dtype=np.int64)[None, :]
    angles = (bins * sub_lags % SUB)[:, :DBINS] * (2.0 * np.pi / SUB)
    cos_part, sin_part = np.cos(angles), np.sin(angles)
    inner = np.block([[cos_part, sin_part], [-sin_part, cos_part]]).astype(ml_dtypes.bfloat16)
    first_bins = FLO + np.array(RESIDUES, dtype=np.int64)[:, None]
    outer_angles = (first_bins * sub_lags % NS) * (2.0 * np.pi / NS)
    outer = np.stack([np.cos(outer_angles), np.sin(outer_angles)], axis=1) * normalizer
    return inner, outer.reshape(2 * RADIX, SUB).astype(np.float32)


def request_kernel(windows, stations, slots_ref, pairs_ref, wanted_ref, places_ref):
    ends = 2 * pairs_ref.shape[1]
    owners_count = wanted_ref.shape[0]
    sublane = lax.broadcasted_iota(jnp.int32, (ends, ends), 0)
    lane = lax.broadcasted_iota(jnp.int32, (ends, ends), 1)

    def to_column(row):
        square = jnp.broadcast_to(row, (ends, ends))
        return jnp.sum(jnp.where(sublane == lane, square, 0).astype(jnp.float32), axis=1, keepdims=True)

    end_row = jnp.concatenate([pairs_ref[0:1, :], pairs_ref[1:2, :]], axis=1)
    end_column = to_column(end_row).astype(jnp.int32)
    lanes = lax.broadcasted_iota(jnp.int32, (ends, 128), 1)
    found = jnp.zeros((ends, 128), jnp.int32)
    for row in range(slots_ref.shape[0]):
        found = found + jnp.where(end_column == lanes + row * 128, slots_ref[row : row + 1, :], 0)
    slot_column = jnp.sum(found.astype(jnp.float32), axis=1, keepdims=True).astype(jnp.int32)
    slot_square = jnp.broadcast_to(slot_column, (ends, ends))
    slot_row = jnp.sum(
        jnp.where(sublane == lane, slot_square, 0).astype(jnp.float32), axis=0, keepdims=True
    ).astype(jnp.int32)
    owner_column = slot_column // stations
    owner_row = slot_row // stations
    same_owner = owner_column == owner_row
    rank_column = jnp.sum(
        jnp.where(same_owner & (lane < sublane), 1.0, 0.0), axis=1, keepdims=True
    ).astype(jnp.int32)
    places_ref[...] = jnp.broadcast_to(owner_column * (windows * CAP) + rank_column, places_ref.shape)
    local_column = (slot_column - owner_column * stations).astype(jnp.float32)
    owned = lax.broadcasted_iota(jnp.int32, (owners_count, ends), 0) == owner_row
    ranked = jnp.where(lane == rank_column, jnp.broadcast_to(local_column, (ends, ends)), 0.0)
    wanted_ref[...] = jnp.dot(
        jnp.where(owned, 1.0, 0.0).astype(jnp.bfloat16),
        ranked.astype(jnp.bfloat16),
        preferred_element_type=jnp.float32,
    )


def requests(station_slot, pair_stations, blocks, windows, stations):
    pair_count = pair_stations.shape[0]
    return pl.pallas_call(
        functools.partial(request_kernel, windows, stations),
        out_shape=(
            jax.ShapeDtypeStruct((blocks, 128), jnp.float32),
            jax.ShapeDtypeStruct((2 * pair_count, 128), jnp.int32),
        ),
        name="requests",
    )(station_slot.reshape(-1, 128), pair_stations.T)


def spectrum_kernel(traces_ref, hann_ref, turns_ref, table_ref, out_ref, *scratch):
    count = len(scratch) // 2
    row_count = traces_ref.shape[0] // count
    tables = (hann_ref, turns_ref, table_ref)
    for part in range(count):
        transform_rows(part * row_count, row_count, traces_ref, *tables, out_ref, *scratch[2 * part : 2 * part + 2])


def transform_rows(
    base_row, row_count, traces_ref, hann_ref, turns_ref, table_ref, out_ref, parts_ref, spectrum_ref
):

    def one_group(group):
        first = group * 16
        rows = pl.ds(base_row + first, 16)
        partial_sum = traces_ref[rows, 0:128]
        for tile in range(1, NS // 128):
            partial_sum = partial_sum + traces_ref[rows, tile * 128 : (tile + 1) * 128]
        mean = jnp.sum(partial_sum, axis=1, keepdims=True) * (1.0 / NS)
        for tile in range(SUB // 128):
            x = []
            for block in range(RADIX):
                columns = slice(block * SUB + tile * 128, block * SUB + (tile + 1) * 128)
                x.append((traces_ref[rows, columns] - mean) * hann_ref[:, columns])
            u = [None] + [x[a] + x[RADIX - a] for a in range(1, 6)]
            v = [None] + [x[a] - x[RADIX - a] for a in range(1, 6)]
            e0, o0 = x[0] + x[6], x[0] - x[6]
            p, q = u[1] + u[5], u[2] + u[4]
            pd, qd = u[1] - u[5], u[2] - u[4]
            m, n = v[1] - v[5], v[2] - v[4]
            ms, ns = v[1] + v[5], v[2] + v[4]
            half_pq, half_diff = 0.5 * (p + q), 0.5 * (p - q)
            e_plus, e_minus = e0 + u[3], e0 - u[3]
            base = o0 + 0.5 * qd
            side = ROOT3_2 * pd
            imag_base = 0.5 * ms + v[3]
            imag_side = ROOT3_2 * ns
            real_parts = [
                e_plus + (p + q),
                base + side,
                e_minus + half_diff,
                o0 - qd,
                e_plus - half_pq,
                base - side,
                e_minus - (p - q),
            ]
            imag_parts = [
                None,
                -(imag_base + imag_side),
                -ROOT3_2 * (m + n),
                v[3] - ms,
                -ROOT3_2 * (m - n),
                imag_side - imag_base,
                None,
            ]
            lanes = slice(tile * 128, (tile + 1) * 128)
            imag_lanes = slice(SUB + tile * 128, SUB + (tile + 1) * 128)
            for position, turn in enumerate(TURNS):
                index = min(turn, RADIX - turn)
                real_part, imag_part = real_parts[index], imag_parts[index]
                cos_turn = turns_ref[2 * position : 2 * position + 1, lanes]
                sin_turn = turns_ref[2 * position + 1 : 2 * position + 2, lanes]
                if imag_part is None:
                    turned_real = real_part * cos_turn
                    turned_imag = -(real_part * sin_turn)
                elif index == turn:
                    turned_real = real_part * cos_turn + imag_part * sin_turn
                    turned_imag = imag_part * cos_turn - real_part * sin_turn
                else:
                    turned_real = real_part * cos_turn - imag_part * sin_turn
                    turned_imag = -(imag_part * cos_turn + real_part * sin_turn)
                target = pl.ds(position * row_count + first, 16)
                parts_ref[target, lanes] = turned_real.astype(jnp.bfloat16)
                parts_ref[target, imag_lanes] = turned_imag.astype(jnp.bfloat16)

    for group in range(row_count // 16):
        one_group(group)
    spectrum_ref[...] = jnp.dot(parts_ref[...], table_ref[...], preferred_element_type=jnp.float32)

    def whiten_group(group):
        first = group * 16
        rows = pl.ds(base_row + first, 16)
        total = jnp.zeros((16, DBINS), jnp.float32)
        for position in range(RADIX):
            source = pl.ds(position * row_count + first, 16)
            real_part, imag_part = spectrum_ref[source, :DBINS], spectrum_ref[source, DBINS:]
            total = total + (real_part * real_part + imag_part * imag_part)
        water_level = jnp.sum(total, axis=1, keepdims=True) * (1.0 / F)
        floor = 0.1 * water_level + 1e-06
        for position in range(RADIX):
            source = pl.ds(position * row_count + first, 16)
            real_part, imag_part = spectrum_ref[source, :DBINS], spectrum_ref[source, DBINS:]
            scaling = lax.rsqrt(real_part * real_part + imag_part * imag_part + floor)
            start = position * 2 * DBINS
            out_ref[rows, start : start + DBINS] = (real_part * scaling).astype(jnp.bfloat16)
            out_ref[rows, start + DBINS : start + 2 * DBINS] = (imag_part * scaling).astype(jnp.bfloat16)

    for group in range(row_count // 16):
        whiten_group(group)


def in_hbm(*arrays):
    return [pltpu.with_memory_space_constraint(array, pltpu.HBM) for array in arrays]


def gather_kernel(windows, wanted_ref, whitened_ref, rows_ref):
    slots = rows_ref.shape[0]
    owners, lanes_count = wanted_ref.shape
    stations = whitened_ref.shape[0] // windows
    owner_of = lax.broadcasted_iota(jnp.int32, (slots, owners), 0) // (windows * CAP)
    spread = jnp.where(owner_of == lax.broadcasted_iota(jnp.int32, (slots, owners), 1), 1.0, 0.0)
    lists = jnp.dot(
        spread.astype(jnp.bfloat16), wanted_ref[...].astype(jnp.bfloat16), preferred_element_type=jnp.float32
    )
    slot_ids = lax.broadcasted_iota(jnp.int32, (slots, lanes_count), 0)
    lanes = lax.broadcasted_iota(jnp.int32, (slots, lanes_count), 1)
    row_wanted = jnp.sum(jnp.where(lanes == slot_ids % CAP, lists, 0.0), axis=1, keepdims=True)
    source = row_wanted.astype(jnp.int32) + slot_ids // CAP % windows * stations
    picks = jnp.where(lanes == source, 1.0, 0.0).astype(whitened_ref.dtype)
    for start in range(0, rows_ref.shape[1], GATHER_COLUMNS):
        columns = slice(start, start + GATHER_COLUMNS)
        rows_ref[:, columns] = jnp.dot(
            picks, whitened_ref[:, columns], preferred_element_type=jnp.float32
        ).astype(rows_ref.dtype)


GATHER_COLUMNS = 512


def gathered(wanted, whitened, windows):
    slots = wanted.shape[0] * windows * CAP
    shape = (slots, whitened.shape[1])
    vmem = pl.BlockSpec(memory_space=pltpu.VMEM)
    return pl.pallas_call(
        functools.partial(gather_kernel, windows),
        out_shape=jax.ShapeDtypeStruct(shape, whitened.dtype),
        in_specs=[vmem, vmem],
        out_specs=vmem,
        compiler_params=pltpu.CompilerParams(vmem_limit_bytes=16 << 20),
        name="gathered",
    )(wanted, whitened)


PART_ROWS = 32
STEP_PARTS = 2


def whitened_spectra(traces):
    total = traces.shape[0]
    rows = PART_ROWS * STEP_PARTS
    table, turns = spectrum_tables()
    scratch = [
        pltpu.VMEM((RADIX * PART_ROWS, 2 * SUB), jnp.bfloat16),
        pltpu.VMEM((RADIX * PART_ROWS, 2 * DBINS), jnp.float32),
    ]
    return pl.pallas_call(
        spectrum_kernel,
        out_shape=jax.ShapeDtypeStruct((total, 2 * F), jnp.bfloat16),
        grid_spec=pltpu.PrefetchScalarGridSpec(
            num_scalar_prefetch=0,
            grid=(total // rows,),
            in_specs=[
                pl.BlockSpec((rows, NS), lambda s: (s, 0)),
                pl.BlockSpec((1, NS), lambda s: (0, 0)),
                pl.BlockSpec((2 * RADIX, SUB), lambda s: (0, 0)),
                pl.BlockSpec((2 * SUB, 2 * DBINS), lambda s: (0, 0)),
            ],
            out_specs=pl.BlockSpec((rows, 2 * F), lambda s: (s, 0)),
            scratch_shapes=scratch * STEP_PARTS,
        ),
        compiler_params=pltpu.CompilerParams(
            dimension_semantics=("arbitrary",), vmem_limit_bytes=24 << 20
        ),
        cost_estimate=pl.CostEstimate(
            flops=2 * total * RADIX * 2 * SUB * 2 * DBINS,
            bytes_accessed=5_000_000,
            transcendentals=total * F,
        ),
        name="whitened_spectra",
    )(*in_hbm(traces, jnp.asarray(hann_window()), jnp.asarray(turns), jnp.asarray(table)))


def lag_kernel(
    place_ref, places_ref, received_ref, inner_ref, outer_ref, kept_ref, sent_ref,
    select_ref, stacked_ref, turned_ref, sums_ref,
):
    slots = received_ref.shape[0]
    ends = places_ref.shape[0]
    pairs = ends // 2
    windows = select_ref.shape[0] // ends
    lanes = lax.broadcasted_iota(jnp.int32, (ends, 128), 1)
    places = places_ref[...]
    for window in range(windows):
        for tile in range(slots // 128):
            hit = jnp.where(places + window * CAP == lanes + tile * 128, 1.0, 0.0)
            rows = slice(window * ends, (window + 1) * ends)
            select_ref[rows, tile * 128 : (tile + 1) * 128] = hit.astype(jnp.bfloat16)

    bins = lax.broadcasted_iota(jnp.int32, (1, DBINS), 1)
    even = bins % 2 == 0
    flip_odd = jnp.where(even, 1.0, -1.0)
    flip_upper = jnp.where(bins % 4 < 2, 1.0, -1.0)
    residue_rows = RADIX * pairs
    for step in range(STEPS):
        columns = slice(step * 4 * DBINS, (step + 1) * 4 * DBINS)
        picked = jnp.dot(select_ref[...], received_ref[:, columns], preferred_element_type=jnp.float32)
        for half in range(2):
            real_columns = slice(half * 2 * DBINS, half * 2 * DBINS + DBINS)
            imag_columns = slice(half * 2 * DBINS + DBINS, (half + 1) * 2 * DBINS)
            real_sum = imag_sum = None
            for window in range(windows):
                left = slice(window * ends, window * ends + pairs)
                right = slice(window * ends + pairs, (window + 1) * ends)
                left_real, left_imag = picked[left, real_columns], picked[left, imag_columns]
                right_real, right_imag = picked[right, real_columns], picked[right, imag_columns]
                real_term = left_real * right_real + left_imag * right_imag
                imag_term = left_imag * right_real - left_real * right_imag
                real_sum = real_term if real_sum is None else real_sum + real_term
                imag_sum = imag_term if imag_sum is None else imag_sum + imag_term
            quarter_real = jnp.where(even, real_sum, -imag_sum) * flip_upper
            quarter_imag = jnp.where(even, imag_sum, real_sum) * flip_upper
            quarters = [
                (real_sum, imag_sum),
                (quarter_real, quarter_imag),
                (real_sum * flip_odd, imag_sum * flip_odd),
                (quarter_real * flip_odd, quarter_imag * flip_odd),
            ]
            position = 2 * step + half
            for quarter, (real_part, imag_part) in enumerate(quarters):
                first = quarter * residue_rows + position * pairs
                stacked_ref[first : first + pairs, :DBINS] = real_part.astype(jnp.bfloat16)
                stacked_ref[first : first + pairs, DBINS:] = imag_part.astype(jnp.bfloat16)

    turned_ref[...] = jnp.dot(stacked_ref[...], inner_ref[...], preferred_element_type=jnp.float32)

    for tile in range(SUB // 128):
        columns = slice(tile * 128, (tile + 1) * 128)
        for group in range(pairs // 8):
            real_of, imag_of = {}, {}
            for position, turn in enumerate(TURNS):
                first = tile * residue_rows + position * pairs + group * 8
                real_part, imag_part = turned_ref[first : first + 8, :DBINS], turned_ref[first : first + 8, DBINS:]
                cos_turn = outer_ref[2 * position : 2 * position + 1, columns]
                sin_turn = outer_ref[2 * position + 1 : 2 * position + 2, columns]
                real_of[turn] = real_part * cos_turn - imag_part * sin_turn
                if turn % STEPS:
                    imag_of[turn] = real_part * sin_turn + imag_part * cos_turn
            r0, r6 = real_of[0], real_of[6]
            re = [None] + [real_of[r] + real_of[RADIX - r] for r in range(1, STEPS)]
            im = [None] + [imag_of[r] - imag_of[RADIX - r] for r in range(1, STEPS)]
            even, odd = re[2] + re[4], re[1] + re[5]
            q_zero = (r0 + r6) + (even + odd + re[3])
            q_one_real = (r0 - r6) + 0.5 * (re[2] - re[4]) + ROOT3_2 * (re[1] - re[5])
            q_one_imag = 0.5 * (im[1] + im[5]) + ROOT3_2 * (im[2] + im[4]) + im[3]
            q_two_real = (r0 + r6) + 0.5 * (re[1] + re[5] - even) - re[3]
            q_two_imag = ROOT3_2 * (im[1] + im[2] - im[4] - im[5])
            periods = [q_two_real + q_two_imag, q_one_real + q_one_imag, q_zero, q_one_real - q_one_imag]
            for period, values in enumerate(periods):
                sums_ref[group * 8 : group * 8 + 8, period * SUB + tile * 128 : period * SUB + (tile + 1) * 128] = values

    rings = kept_ref.shape[0]
    share = kept_ref.shape[2]
    for offset in range(rings):
        ring = lax.rem(place_ref[0] + offset, rings)
        kept = pl.multiple_of((2 * ring + place_ref[1]) * share, share)
        sent = pl.multiple_of((2 * ring + 1 - place_ref[1]) * share, share)
        kept_ref[offset] = sums_ref[:, pl.ds(kept, share)]
        sent_ref[offset] = sums_ref[:, pl.ds(sent, share)].astype(sent_ref.dtype)


def lag_sums(place, places, received, parts, normalizer):
    ends = places.shape[0]
    slots = received.shape[0]
    pairs = ends // 2
    windows = slots // (32 * CAP)
    inner, outer = lag_tables(normalizer)
    share = 2 * LAG // parts
    vmem = pl.BlockSpec(memory_space=pltpu.VMEM)
    return pl.pallas_call(
        lag_kernel,
        out_shape=(
            jax.ShapeDtypeStruct((parts // 2, pairs, share), jnp.float32),
            jax.ShapeDtypeStruct((parts // 2, pairs, share), jnp.bfloat16),
        ),
        in_specs=[pl.BlockSpec(memory_space=pltpu.SMEM)] + [vmem] * 4,
        out_specs=(vmem, vmem),
        scratch_shapes=[
            pltpu.VMEM((windows * ends, slots), jnp.bfloat16),
            pltpu.VMEM((SUB // DBINS * RADIX * pairs, 2 * DBINS), jnp.bfloat16),
            pltpu.VMEM((SUB // DBINS * RADIX * pairs, 2 * DBINS), jnp.float32),
            pltpu.VMEM((pairs, 2 * LAG), jnp.float32),
        ],
        compiler_params=pltpu.CompilerParams(vmem_limit_bytes=32 << 20),
        cost_estimate=pl.CostEstimate(
            flops=2 * windows * ends * slots * 2 * F, bytes_accessed=5_000_000, transcendentals=0
        ),
        name="lag_sums",
    )(place, places, received, jnp.asarray(inner), jnp.asarray(outer))


def add_kernel(kept_ref, got_ref, own_ref, *sent_refs):
    own_ref[...] = kept_ref[0] + got_ref[0].astype(jnp.float32)
    for offset, sent_ref in enumerate(sent_refs, 1):
        sent_ref[...] = (kept_ref[offset] + got_ref[offset].astype(jnp.float32)).astype(sent_ref.dtype)


def total_kernel(own_ref, *rest):
    total = own_ref[...]
    for got_ref in rest[:-1]:
        total = total + got_ref[...].astype(jnp.float32)
    rest[-1][...] = total


def window_total(kept, sent):
    rings, pairs, share = kept.shape
    devices = range(2 * rings)
    got = lax.ppermute(sent, "tm", [(source, source ^ 1) for source in devices])
    params = pltpu.CompilerParams(vmem_limit_bytes=16 << 20)
    own, *onward = pl.pallas_call(
        add_kernel,
        out_shape=[jax.ShapeDtypeStruct((pairs, share), jnp.float32)]
        + [jax.ShapeDtypeStruct((pairs, share), jnp.bfloat16)] * (rings - 1),
        compiler_params=params,
        name="core_total",
    )(kept, got)
    arrived = []
    for offset, values in enumerate(onward, 1):
        targets = [(source, (source // 2 + offset) % rings * 2 + source % 2) for source in devices]
        arrived.append(lax.ppermute(values, "tm", targets))
    return pl.pallas_call(
        total_kernel,
        out_shape=jax.ShapeDtypeStruct((pairs, share), jnp.float32),
        compiler_params=params,
        name="window_total",
    )(own, *arrived).T


def on_device(traces, station_slot, pair_stations):
    window_count, station_count, length = traces.shape
    blocks = lax.axis_size("pairs")
    lag_parts = lax.axis_size("tm")
    slots = blocks * window_count * CAP
    normalizer = 1.0 / math.sqrt(F * window_count * lag_parts)
    own = lax.axis_index("tm")
    wanted, places = requests(station_slot, pair_stations, blocks, window_count, station_count)
    wanted, own = lax.optimization_barrier((wanted, own))
    lists = lax.all_to_all(wanted[:, None, :], "pairs", split_axis=0, concat_axis=0, tiled=True)
    place = jnp.stack([own // 2, own % 2]).astype(jnp.int32)
    lists, place = lax.optimization_barrier((lists, place))
    whitened = whitened_spectra(traces.reshape(window_count * station_count, length))
    rows = gathered(lists.reshape(wanted.shape), whitened, window_count)
    received = lax.all_to_all(
        rows.reshape(blocks, window_count * CAP, 2 * F), "pairs", split_axis=0, concat_axis=0, tiled=True
    )
    kept, sent = lag_sums(place, places, received.reshape(slots, 2 * F), lag_parts, normalizer)
    return window_total(kept, sent)


def solution(mesh):
    in_specs = (P("tm", "pairs", None), P(), P("pairs", None))
    out_specs = P("tm", "pairs")
    return jax.shard_map(
        on_device, mesh=mesh, in_specs=in_specs, out_specs=out_specs, check_vma=False
    )
```

```python
import functools
import math

import jax
import jax.numpy as jnp
import ml_dtypes
import numpy as np
from jax import lax
from jax.experimental import pallas as pl
from jax.experimental.pallas import tpu as pltpu
from jax.sharding import PartitionSpec as P

F = 1536
FLO = 32
LAG = 1024
NS = 6144
RADIX = 12
SUB = NS // RADIX
DBINS = F // RADIX
STEPS = RADIX // 2
CAP = 8
ROOT3_2 = math.sqrt(3.0) / 2.0

TURNS = [0, 6] + [turn for step in range(1, STEPS) for turn in (step, RADIX - step)]
RESIDUES = [(turn - FLO) % RADIX for turn in TURNS]


def spectrum_tables():
    sub_times = np.arange(SUB, dtype=np.int64)[:, None]
    bins = np.arange(DBINS, dtype=np.int64)[None, :]
    angles = (sub_times * bins % SUB) * (2.0 * np.pi / SUB)
    cos_part, sin_part = np.cos(angles), np.sin(angles)
    inner = np.block([[cos_part, -sin_part], [sin_part, cos_part]]).astype(ml_dtypes.bfloat16)
    first_bins = FLO + np.array(RESIDUES, dtype=np.int64)[:, None]
    turn_angles = (first_bins * sub_times[:, 0][None, :] % NS) * (2.0 * np.pi / NS)
    turns = np.stack([np.cos(turn_angles), np.sin(turn_angles)], axis=1)
    return inner, turns.reshape(2 * RADIX, SUB).astype(np.float32)


def hann_window():
    times = np.arange(NS, dtype=np.float64)
    return (0.5 - 0.5 * np.cos((times + 0.5) * (2.0 * np.pi / NS))).astype(np.float32)[None, :]


def lag_tables(normalizer):
    bins = np.arange(DBINS, dtype=np.int64)[:, None]
    sub_lags = np.arange(SUB, dtype=np.int64)[None, :]
    angles = (bins * sub_lags % SUB)[:, :DBINS] * (2.0 * np.pi / SUB)
    cos_part, sin_part = np.cos(angles), np.sin(angles)
    inner = np.block([[cos_part, sin_part], [-sin_part, cos_part]]).astype(ml_dtypes.bfloat16)
    first_bins = FLO + np.array(RESIDUES, dtype=np.int64)[:, None]
    outer_angles = (first_bins * sub_lags % NS) * (2.0 * np.pi / NS)
    outer = np.stack([np.cos(outer_angles), np.sin(outer_angles)], axis=1) * normalizer
    return inner, outer.reshape(2 * RADIX, SUB).astype(np.float32)


def request_kernel(windows, stations, slots_ref, pairs_ref, wanted_ref, places_ref):
    ends = 2 * pairs_ref.shape[1]
    owners_count = wanted_ref.shape[0]
    sublane = lax.broadcasted_iota(jnp.int32, (ends, ends), 0)
    lane = lax.broadcasted_iota(jnp.int32, (ends, ends), 1)

    def to_column(row):
        square = jnp.broadcast_to(row, (ends, ends))
        return jnp.sum(jnp.where(sublane == lane, square, 0).astype(jnp.float32), axis=1, keepdims=True)

    end_row = jnp.concatenate([pairs_ref[0:1, :], pairs_ref[1:2, :]], axis=1)
    end_column = to_column(end_row).astype(jnp.int32)
    lanes = lax.broadcasted_iota(jnp.int32, (ends, 128), 1)
    found = jnp.zeros((ends, 128), jnp.int32)
    for row in range(slots_ref.shape[0]):
        found = found + jnp.where(end_column == lanes + row * 128, slots_ref[row : row + 1, :], 0)
    slot_column = jnp.sum(found.astype(jnp.float32), axis=1, keepdims=True).astype(jnp.int32)
    slot_square = jnp.broadcast_to(slot_column, (ends, ends))
    slot_row = jnp.sum(
        jnp.where(sublane == lane, slot_square, 0).astype(jnp.float32), axis=0, keepdims=True
    ).astype(jnp.int32)
    owner_column = slot_column // stations
    owner_row = slot_row // stations
    same_owner = owner_column == owner_row
    rank_column = jnp.sum(
        jnp.where(same_owner & (lane < sublane), 1.0, 0.0), axis=1, keepdims=True
    ).astype(jnp.int32)
    places_ref[...] = jnp.broadcast_to(owner_column * (windows * CAP) + rank_column, places_ref.shape)
    local_column = (slot_column - owner_column * stations).astype(jnp.float32)
    owned = lax.broadcasted_iota(jnp.int32, (owners_count, ends), 0) == owner_row
    ranked = jnp.where(lane == rank_column, jnp.broadcast_to(local_column, (ends, ends)), 0.0)
    wanted_ref[...] = jnp.dot(
        jnp.where(owned, 1.0, 0.0).astype(jnp.bfloat16),
        ranked.astype(jnp.bfloat16),
        preferred_element_type=jnp.float32,
    )


def requests(station_slot, pair_stations, blocks, windows, stations):
    pair_count = pair_stations.shape[0]
    return pl.pallas_call(
        functools.partial(request_kernel, windows, stations),
        out_shape=(
            jax.ShapeDtypeStruct((blocks, 128), jnp.float32),
            jax.ShapeDtypeStruct((2 * pair_count, 128), jnp.int32),
        ),
        name="requests",
    )(station_slot.reshape(-1, 128), pair_stations.T)


def spectrum_kernel(traces_ref, hann_ref, turns_ref, table_ref, out_ref, *scratch):
    count = len(scratch) // 2
    row_count = traces_ref.shape[0] // count
    tables = (hann_ref, turns_ref, table_ref)
    for part in range(count):
        transform_rows(part * row_count, row_count, traces_ref, *tables, out_ref, *scratch[2 * part : 2 * part + 2])


def transform_rows(
    base_row, row_count, traces_ref, hann_ref, turns_ref, table_ref, out_ref, parts_ref, spectrum_ref
):

    def one_group(group):
        first = group * 16
        rows = pl.ds(base_row + first, 16)
        partial_sum = traces_ref[rows, 0:128]
        for tile in range(1, NS // 128):
            partial_sum = partial_sum + traces_ref[rows, tile * 128 : (tile + 1) * 128]
        mean = jnp.sum(partial_sum, axis=1, keepdims=True) * (1.0 / NS)
        for tile in range(SUB // 128):
            x = []
            for block in range(RADIX):
                columns = slice(block * SUB + tile * 128, block * SUB + (tile + 1) * 128)
                x.append((traces_ref[rows, columns] - mean) * hann_ref[:, columns])
            u = [None] + [x[a] + x[RADIX - a] for a in range(1, 6)]
            v = [None] + [x[a] - x[RADIX - a] for a in range(1, 6)]
            e0, o0 = x[0] + x[6], x[0] - x[6]
            p, q = u[1] + u[5], u[2] + u[4]
            pd, qd = u[1] - u[5], u[2] - u[4]
            m, n = v[1] - v[5], v[2] - v[4]
            ms, ns = v[1] + v[5], v[2] + v[4]
            half_pq, half_diff = 0.5 * (p + q), 0.5 * (p - q)
            e_plus, e_minus = e0 + u[3], e0 - u[3]
            base = o0 + 0.5 * qd
            side = ROOT3_2 * pd
            imag_base = 0.5 * ms + v[3]
            imag_side = ROOT3_2 * ns
            real_parts = [
                e_plus + (p + q),
                base + side,
                e_minus + half_diff,
                o0 - qd,
                e_plus - half_pq,
                base - side,
                e_minus - (p - q),
            ]
            imag_parts = [
                None,
                -(imag_base + imag_side),
                -ROOT3_2 * (m + n),
                v[3] - ms,
                -ROOT3_2 * (m - n),
                imag_side - imag_base,
                None,
            ]
            lanes = slice(tile * 128, (tile + 1) * 128)
            imag_lanes = slice(SUB + tile * 128, SUB + (tile + 1) * 128)
            for position, turn in enumerate(TURNS):
                index = min(turn, RADIX - turn)
                real_part, imag_part = real_parts[index], imag_parts[index]
                cos_turn = turns_ref[2 * position : 2 * position + 1, lanes]
                sin_turn = turns_ref[2 * position + 1 : 2 * position + 2, lanes]
                if imag_part is None:
                    turned_real = real_part * cos_turn
                    turned_imag = -(real_part * sin_turn)
                elif index == turn:
                    turned_real = real_part * cos_turn + imag_part * sin_turn
                    turned_imag = imag_part * cos_turn - real_part * sin_turn
                else:
                    turned_real = real_part * cos_turn - imag_part * sin_turn
                    turned_imag = -(imag_part * cos_turn + real_part * sin_turn)
                target = pl.ds(position * row_count + first, 16)
                parts_ref[target, lanes] = turned_real.astype(jnp.bfloat16)
                parts_ref[target, imag_lanes] = turned_imag.astype(jnp.bfloat16)

    for group in range(row_count // 16):
        one_group(group)
    spectrum_ref[...] = jnp.dot(parts_ref[...], table_ref[...], preferred_element_type=jnp.float32)

    def whiten_group(group):
        first = group * 16
        rows = pl.ds(base_row + first, 16)
        total = jnp.zeros((16, DBINS), jnp.float32)
        for position in range(RADIX):
            source = pl.ds(position * row_count + first, 16)
            real_part, imag_part = spectrum_ref[source, :DBINS], spectrum_ref[source, DBINS:]
            total = total + (real_part * real_part + imag_part * imag_part)
        water_level = jnp.sum(total, axis=1, keepdims=True) * (1.0 / F)
        floor = 0.1 * water_level + 1e-06
        for position in range(RADIX):
            source = pl.ds(position * row_count + first, 16)
            real_part, imag_part = spectrum_ref[source, :DBINS], spectrum_ref[source, DBINS:]
            scaling = lax.rsqrt(real_part * real_part + imag_part * imag_part + floor)
            start = position * 2 * DBINS
            out_ref[rows, start : start + DBINS] = (real_part * scaling).astype(jnp.bfloat16)
            out_ref[rows, start + DBINS : start + 2 * DBINS] = (imag_part * scaling).astype(jnp.bfloat16)

    for group in range(row_count // 16):
        whiten_group(group)


def in_hbm(*arrays):
    return [pltpu.with_memory_space_constraint(array, pltpu.HBM) for array in arrays]


def gather_kernel(windows, wanted_ref, whitened_ref, rows_ref):
    slots = rows_ref.shape[0]
    owners, lanes_count = wanted_ref.shape
    stations = whitened_ref.shape[0] // windows
    owner_of = lax.broadcasted_iota(jnp.int32, (slots, owners), 0) // (windows * CAP)
    spread = jnp.where(owner_of == lax.broadcasted_iota(jnp.int32, (slots, owners), 1), 1.0, 0.0)
    lists = jnp.dot(
        spread.astype(jnp.bfloat16), wanted_ref[...].astype(jnp.bfloat16), preferred_element_type=jnp.float32
    )
    slot_ids = lax.broadcasted_iota(jnp.int32, (slots, lanes_count), 0)
    lanes = lax.broadcasted_iota(jnp.int32, (slots, lanes_count), 1)
    row_wanted = jnp.sum(jnp.where(lanes == slot_ids % CAP, lists, 0.0), axis=1, keepdims=True)
    source = row_wanted.astype(jnp.int32) + slot_ids // CAP % windows * stations
    picks = jnp.where(lanes == source, 1.0, 0.0).astype(whitened_ref.dtype)
    for start in range(0, rows_ref.shape[1], GATHER_COLUMNS):
        columns = slice(start, start + GATHER_COLUMNS)
        rows_ref[:, columns] = jnp.dot(
            picks, whitened_ref[:, columns], preferred_element_type=jnp.float32
        ).astype(rows_ref.dtype)


GATHER_COLUMNS = 512


def gathered(wanted, whitened, windows):
    slots = wanted.shape[0] * windows * CAP
    shape = (slots, whitened.shape[1])
    vmem = pl.BlockSpec(memory_space=pltpu.VMEM)
    return pl.pallas_call(
        functools.partial(gather_kernel, windows),
        out_shape=jax.ShapeDtypeStruct(shape, whitened.dtype),
        in_specs=[vmem, vmem],
        out_specs=vmem,
        compiler_params=pltpu.CompilerParams(vmem_limit_bytes=16 << 20),
        name="gathered",
    )(wanted, whitened)


PART_ROWS = 32
STEP_PARTS = 2


def whitened_spectra(traces):
    total = traces.shape[0]
    rows = PART_ROWS * STEP_PARTS
    table, turns = spectrum_tables()
    scratch = [
        pltpu.VMEM((RADIX * PART_ROWS, 2 * SUB), jnp.bfloat16),
        pltpu.VMEM((RADIX * PART_ROWS, 2 * DBINS), jnp.float32),
    ]
    return pl.pallas_call(
        spectrum_kernel,
        out_shape=jax.ShapeDtypeStruct((total, 2 * F), jnp.bfloat16),
        grid_spec=pltpu.PrefetchScalarGridSpec(
            num_scalar_prefetch=0,
            grid=(total // rows,),
            in_specs=[
                pl.BlockSpec((rows, NS), lambda s: (s, 0)),
                pl.BlockSpec((1, NS), lambda s: (0, 0)),
                pl.BlockSpec((2 * RADIX, SUB), lambda s: (0, 0)),
                pl.BlockSpec((2 * SUB, 2 * DBINS), lambda s: (0, 0)),
            ],
            out_specs=pl.BlockSpec((rows, 2 * F), lambda s: (s, 0)),
            scratch_shapes=scratch * STEP_PARTS,
        ),
        compiler_params=pltpu.CompilerParams(
            dimension_semantics=("arbitrary",), vmem_limit_bytes=24 << 20
        ),
        cost_estimate=pl.CostEstimate(
            flops=2 * total * RADIX * 2 * SUB * 2 * DBINS,
            bytes_accessed=5_000_000,
            transcendentals=total * F,
        ),
        name="whitened_spectra",
    )(*in_hbm(traces, jnp.asarray(hann_window()), jnp.asarray(turns), jnp.asarray(table)))


def lag_kernel(
    place_ref, places_ref, received_ref, inner_ref, outer_ref, kept_ref, sent_ref,
    select_ref, stacked_ref, turned_ref, sums_ref,
):
    slots = received_ref.shape[0]
    ends = places_ref.shape[0]
    pairs = ends // 2
    windows = select_ref.shape[0] // ends
    lanes = lax.broadcasted_iota(jnp.int32, (ends, 128), 1)
    places = places_ref[...]
    for window in range(windows):
        for tile in range(slots // 128):
            hit = jnp.where(places + window * CAP == lanes + tile * 128, 1.0, 0.0)
            rows = slice(window * ends, (window + 1) * ends)
            select_ref[rows, tile * 128 : (tile + 1) * 128] = hit.astype(jnp.bfloat16)

    bins = lax.broadcasted_iota(jnp.int32, (1, DBINS), 1)
    even = bins % 2 == 0
    flip_odd = jnp.where(even, 1.0, -1.0)
    flip_upper = jnp.where(bins % 4 < 2, 1.0, -1.0)
    residue_rows = RADIX * pairs
    for step in range(STEPS):
        columns = slice(step * 4 * DBINS, (step + 1) * 4 * DBINS)
        picked = jnp.dot(select_ref[...], received_ref[:, columns], preferred_element_type=jnp.float32)
        for half in range(2):
            real_columns = slice(half * 2 * DBINS, half * 2 * DBINS + DBINS)
            imag_columns = slice(half * 2 * DBINS + DBINS, (half + 1) * 2 * DBINS)
            real_sum = imag_sum = None
            for window in range(windows):
                left = slice(window * ends, window * ends + pairs)
                right = slice(window * ends + pairs, (window + 1) * ends)
                left_real, left_imag = picked[left, real_columns], picked[left, imag_columns]
                right_real, right_imag = picked[right, real_columns], picked[right, imag_columns]
                real_term = left_real * right_real + left_imag * right_imag
                imag_term = left_imag * right_real - left_real * right_imag
                real_sum = real_term if real_sum is None else real_sum + real_term
                imag_sum = imag_term if imag_sum is None else imag_sum + imag_term
            quarter_real = jnp.where(even, real_sum, -imag_sum) * flip_upper
            quarter_imag = jnp.where(even, imag_sum, real_sum) * flip_upper
            quarters = [
                (real_sum, imag_sum),
                (quarter_real, quarter_imag),
                (real_sum * flip_odd, imag_sum * flip_odd),
                (quarter_real * flip_odd, quarter_imag * flip_odd),
            ]
            position = 2 * step + half
            for quarter, (real_part, imag_part) in enumerate(quarters):
                first = quarter * residue_rows + position * pairs
                stacked_ref[first : first + pairs, :DBINS] = real_part.astype(jnp.bfloat16)
                stacked_ref[first : first + pairs, DBINS:] = imag_part.astype(jnp.bfloat16)

    turned_ref[...] = jnp.dot(stacked_ref[...], inner_ref[...], preferred_element_type=jnp.float32)

    for tile in range(SUB // 128):
        columns = slice(tile * 128, (tile + 1) * 128)
        for group in range(pairs // 8):
            real_of, imag_of = {}, {}
            for position, turn in enumerate(TURNS):
                first = tile * residue_rows + position * pairs + group * 8
                real_part, imag_part = turned_ref[first : first + 8, :DBINS], turned_ref[first : first + 8, DBINS:]
                cos_turn = outer_ref[2 * position : 2 * position + 1, columns]
                sin_turn = outer_ref[2 * position + 1 : 2 * position + 2, columns]
                real_of[turn] = real_part * cos_turn - imag_part * sin_turn
                if turn % STEPS:
                    imag_of[turn] = real_part * sin_turn + imag_part * cos_turn
            r0, r6 = real_of[0], real_of[6]
            re = [None] + [real_of[r] + real_of[RADIX - r] for r in range(1, STEPS)]
            im = [None] + [imag_of[r] - imag_of[RADIX - r] for r in range(1, STEPS)]
            even, odd = re[2] + re[4], re[1] + re[5]
            q_zero = (r0 + r6) + (even + odd + re[3])
            q_one_real = (r0 - r6) + 0.5 * (re[2] - re[4]) + ROOT3_2 * (re[1] - re[5])
            q_one_imag = 0.5 * (im[1] + im[5]) + ROOT3_2 * (im[2] + im[4]) + im[3]
            q_two_real = (r0 + r6) + 0.5 * (re[1] + re[5] - even) - re[3]
            q_two_imag = ROOT3_2 * (im[1] + im[2] - im[4] - im[5])
            periods = [q_two_real + q_two_imag, q_one_real + q_one_imag, q_zero, q_one_real - q_one_imag]
            for period, values in enumerate(periods):
                sums_ref[group * 8 : group * 8 + 8, period * SUB + tile * 128 : period * SUB + (tile + 1) * 128] = values

    rings = kept_ref.shape[0]
    share = kept_ref.shape[2]
    for offset in range(rings):
        ring = lax.rem(place_ref[0] + offset, rings)
        kept = pl.multiple_of((2 * ring + place_ref[1]) * share, share)
        sent = pl.multiple_of((2 * ring + 1 - place_ref[1]) * share, share)
        kept_ref[offset] = sums_ref[:, pl.ds(kept, share)]
        sent_ref[offset] = sums_ref[:, pl.ds(sent, share)].astype(sent_ref.dtype)


def lag_sums(place, places, received, parts, normalizer):
    ends = places.shape[0]
    slots = received.shape[0]
    pairs = ends // 2
    windows = slots // (32 * CAP)
    inner, outer = lag_tables(normalizer)
    share = 2 * LAG // parts
    vmem = pl.BlockSpec(memory_space=pltpu.VMEM)
    return pl.pallas_call(
        lag_kernel,
        out_shape=(
            jax.ShapeDtypeStruct((parts // 2, pairs, share), jnp.float32),
            jax.ShapeDtypeStruct((parts // 2, pairs, share), jnp.bfloat16),
        ),
        in_specs=[pl.BlockSpec(memory_space=pltpu.SMEM)] + [vmem] * 4,
        out_specs=(vmem, vmem),
        scratch_shapes=[
            pltpu.VMEM((windows * ends, slots), jnp.bfloat16),
            pltpu.VMEM((SUB // DBINS * RADIX * pairs, 2 * DBINS), jnp.bfloat16),
            pltpu.VMEM((SUB // DBINS * RADIX * pairs, 2 * DBINS), jnp.float32),
            pltpu.VMEM((pairs, 2 * LAG), jnp.float32),
        ],
        compiler_params=pltpu.CompilerParams(vmem_limit_bytes=32 << 20),
        cost_estimate=pl.CostEstimate(
            flops=2 * windows * ends * slots * 2 * F, bytes_accessed=5_000_000, transcendentals=0
        ),
        name="lag_sums",
    )(place, places, received, jnp.asarray(inner), jnp.asarray(outer))


def add_kernel(kept_ref, got_ref, own_ref, *sent_refs):
    own_ref[...] = kept_ref[0] + got_ref[0].astype(jnp.float32)
    for offset, sent_ref in enumerate(sent_refs, 1):
        sent_ref[...] = (kept_ref[offset] + got_ref[offset].astype(jnp.float32)).astype(sent_ref.dtype)


def total_kernel(own_ref, *rest):
    total = own_ref[...]
    for got_ref in rest[:-1]:
        total = total + got_ref[...].astype(jnp.float32)
    rest[-1][...] = total


def window_total(kept, sent):
    rings, pairs, share = kept.shape
    devices = range(2 * rings)
    got = lax.ppermute(sent, "tm", [(source, source ^ 1) for source in devices])
    params = pltpu.CompilerParams(vmem_limit_bytes=16 << 20)
    own, *onward = pl.pallas_call(
        add_kernel,
        out_shape=[jax.ShapeDtypeStruct((pairs, share), jnp.float32)]
        + [jax.ShapeDtypeStruct((pairs, share), jnp.bfloat16)] * (rings - 1),
        compiler_params=params,
        name="core_total",
    )(kept, got)
    arrived = []
    farthest_first = sorted(range(1, rings), key=lambda offset: -min(offset, rings - offset))
    for offset in farthest_first:
        targets = [(source, (source // 2 + offset) % rings * 2 + source % 2) for source in devices]
        arrived.append(lax.ppermute(onward[offset - 1], "tm", targets))
    return pl.pallas_call(
        total_kernel,
        out_shape=jax.ShapeDtypeStruct((pairs, share), jnp.float32),
        compiler_params=params,
        name="window_total",
    )(own, *arrived).T


def on_device(traces, station_slot, pair_stations):
    window_count, station_count, length = traces.shape
    blocks = lax.axis_size("pairs")
    lag_parts = lax.axis_size("tm")
    slots = blocks * window_count * CAP
    normalizer = 1.0 / math.sqrt(F * window_count * lag_parts)
    own = lax.axis_index("tm")
    wanted, places = requests(station_slot, pair_stations, blocks, window_count, station_count)
    wanted, own = lax.optimization_barrier((wanted, own))
    lists = lax.all_to_all(wanted[:, None, :], "pairs", split_axis=0, concat_axis=0, tiled=True)
    place = jnp.stack([own // 2, own % 2]).astype(jnp.int32)
    lists, place = lax.optimization_barrier((lists, place))
    whitened = whitened_spectra(traces.reshape(window_count * station_count, length))
    rows = gathered(lists.reshape(wanted.shape), whitened, window_count)
    received = lax.all_to_all(
        rows.reshape(blocks, window_count * CAP, 2 * F), "pairs", split_axis=0, concat_axis=0, tiled=True
    )
    kept, sent = lag_sums(place, places, received.reshape(slots, 2 * F), lag_parts, normalizer)
    return window_total(kept, sent)


def solution(mesh):
    in_specs = (P("tm", "pairs", None), P(), P("pairs", None))
    out_specs = P("tm", "pairs")
    return jax.shard_map(
        on_device, mesh=mesh, in_specs=in_specs, out_specs=out_specs, check_vma=False
    )
```

```python
import functools
import math

import jax
import jax.numpy as jnp
import ml_dtypes
import numpy as np
from jax import lax
from jax.experimental import pallas as pl
from jax.experimental.pallas import tpu as pltpu
from jax.sharding import PartitionSpec as P

F = 1536
FLO = 32
LAG = 1024
NS = 6144
RADIX = 12
SUB = NS // RADIX
DBINS = F // RADIX
STEPS = RADIX // 2
CAP = 8
ROOT3_2 = math.sqrt(3.0) / 2.0

TURNS = [0, 6] + [turn for step in range(1, STEPS) for turn in (step, RADIX - step)]
RESIDUES = [(turn - FLO) % RADIX for turn in TURNS]


def spectrum_tables():
    sub_times = np.arange(SUB, dtype=np.int64)[:, None]
    bins = np.arange(DBINS, dtype=np.int64)[None, :]
    angles = (sub_times * bins % SUB) * (2.0 * np.pi / SUB)
    cos_part, sin_part = np.cos(angles), np.sin(angles)
    inner = np.block([[cos_part, -sin_part], [sin_part, cos_part]]).astype(ml_dtypes.bfloat16)
    first_bins = FLO + np.array(RESIDUES, dtype=np.int64)[:, None]
    turn_angles = (first_bins * sub_times[:, 0][None, :] % NS) * (2.0 * np.pi / NS)
    turns = np.stack([np.cos(turn_angles), np.sin(turn_angles)], axis=1)
    return inner, turns.reshape(2 * RADIX, SUB).astype(np.float32)


def hann_window():
    times = np.arange(NS, dtype=np.float64)
    return (0.5 - 0.5 * np.cos((times + 0.5) * (2.0 * np.pi / NS))).astype(np.float32)[None, :]


def lag_tables(normalizer):
    bins = np.arange(DBINS, dtype=np.int64)[:, None]
    sub_lags = np.arange(SUB, dtype=np.int64)[None, :]
    angles = (bins * sub_lags % SUB)[:, :DBINS] * (2.0 * np.pi / SUB)
    cos_part, sin_part = np.cos(angles), np.sin(angles)
    inner = np.block([[cos_part, sin_part], [-sin_part, cos_part]]).astype(ml_dtypes.bfloat16)
    first_bins = FLO + np.array(RESIDUES, dtype=np.int64)[:, None]
    outer_angles = (first_bins * sub_lags % NS) * (2.0 * np.pi / NS)
    outer = np.stack([np.cos(outer_angles), np.sin(outer_angles)], axis=1) * normalizer
    return inner, outer.reshape(2 * RADIX, SUB).astype(np.float32)


def request_kernel(windows, stations, slots_ref, pairs_ref, wanted_ref, places_ref):
    ends = 2 * pairs_ref.shape[1]
    owners_count = wanted_ref.shape[0]
    sublane = lax.broadcasted_iota(jnp.int32, (ends, ends), 0)
    lane = lax.broadcasted_iota(jnp.int32, (ends, ends), 1)

    def to_column(row):
        square = jnp.broadcast_to(row, (ends, ends))
        return jnp.sum(jnp.where(sublane == lane, square, 0).astype(jnp.float32), axis=1, keepdims=True)

    end_row = jnp.concatenate([pairs_ref[0:1, :], pairs_ref[1:2, :]], axis=1)
    end_column = to_column(end_row).astype(jnp.int32)
    lanes = lax.broadcasted_iota(jnp.int32, (ends, 128), 1)
    found = jnp.zeros((ends, 128), jnp.int32)
    for row in range(slots_ref.shape[0]):
        found = found + jnp.where(end_column == lanes + row * 128, slots_ref[row : row + 1, :], 0)
    slot_column = jnp.sum(found.astype(jnp.float32), axis=1, keepdims=True).astype(jnp.int32)
    slot_square = jnp.broadcast_to(slot_column, (ends, ends))
    slot_row = jnp.sum(
        jnp.where(sublane == lane, slot_square, 0).astype(jnp.float32), axis=0, keepdims=True
    ).astype(jnp.int32)
    owner_column = slot_column // stations
    owner_row = slot_row // stations
    same_owner = owner_column == owner_row
    rank_column = jnp.sum(
        jnp.where(same_owner & (lane < sublane), 1.0, 0.0), axis=1, keepdims=True
    ).astype(jnp.int32)
    places_ref[...] = jnp.broadcast_to(owner_column * (windows * CAP) + rank_column, places_ref.shape)
    local_column = (slot_column - owner_column * stations).astype(jnp.float32)
    owned = lax.broadcasted_iota(jnp.int32, (owners_count, ends), 0) == owner_row
    ranked = jnp.where(lane == rank_column, jnp.broadcast_to(local_column, (ends, ends)), 0.0)
    wanted_ref[...] = jnp.dot(
        jnp.where(owned, 1.0, 0.0).astype(jnp.bfloat16),
        ranked.astype(jnp.bfloat16),
        preferred_element_type=jnp.float32,
    )


def requests(station_slot, pair_stations, blocks, windows, stations):
    pair_count = pair_stations.shape[0]
    return pl.pallas_call(
        functools.partial(request_kernel, windows, stations),
        out_shape=(
            jax.ShapeDtypeStruct((blocks, 128), jnp.float32),
            jax.ShapeDtypeStruct((2 * pair_count, 128), jnp.int32),
        ),
        name="requests",
    )(station_slot.reshape(-1, 128), pair_stations.T)


def spectrum_kernel(traces_ref, hann_ref, turns_ref, table_ref, out_ref, *scratch):
    count = len(scratch) // 2
    row_count = traces_ref.shape[0] // count
    tables = (hann_ref, turns_ref, table_ref)
    for part in range(count):
        transform_rows(part * row_count, row_count, traces_ref, *tables, out_ref, *scratch[2 * part : 2 * part + 2])


def transform_rows(
    base_row, row_count, traces_ref, hann_ref, turns_ref, table_ref, out_ref, parts_ref, spectrum_ref
):

    def one_group(group):
        first = group * 16
        rows = pl.ds(base_row + first, 16)
        partial_sum = traces_ref[rows, 0:128]
        for tile in range(1, NS // 128):
            partial_sum = partial_sum + traces_ref[rows, tile * 128 : (tile + 1) * 128]
        mean = jnp.sum(partial_sum, axis=1, keepdims=True) * (1.0 / NS)
        for tile in range(SUB // 128):
            x = []
            for block in range(RADIX):
                columns = slice(block * SUB + tile * 128, block * SUB + (tile + 1) * 128)
                x.append((traces_ref[rows, columns] - mean) * hann_ref[:, columns])
            u = [None] + [x[a] + x[RADIX - a] for a in range(1, 6)]
            v = [None] + [x[a] - x[RADIX - a] for a in range(1, 6)]
            e0, o0 = x[0] + x[6], x[0] - x[6]
            p, q = u[1] + u[5], u[2] + u[4]
            pd, qd = u[1] - u[5], u[2] - u[4]
            m, n = v[1] - v[5], v[2] - v[4]
            ms, ns = v[1] + v[5], v[2] + v[4]
            half_pq, half_diff = 0.5 * (p + q), 0.5 * (p - q)
            e_plus, e_minus = e0 + u[3], e0 - u[3]
            base = o0 + 0.5 * qd
            side = ROOT3_2 * pd
            imag_base = 0.5 * ms + v[3]
            imag_side = ROOT3_2 * ns
            real_parts = [
                e_plus + (p + q),
                base + side,
                e_minus + half_diff,
                o0 - qd,
                e_plus - half_pq,
                base - side,
                e_minus - (p - q),
            ]
            imag_parts = [
                None,
                -(imag_base + imag_side),
                -ROOT3_2 * (m + n),
                v[3] - ms,
                -ROOT3_2 * (m - n),
                imag_side - imag_base,
                None,
            ]
            lanes = slice(tile * 128, (tile + 1) * 128)
            imag_lanes = slice(SUB + tile * 128, SUB + (tile + 1) * 128)
            for position, turn in enumerate(TURNS):
                index = min(turn, RADIX - turn)
                real_part, imag_part = real_parts[index], imag_parts[index]
                cos_turn = turns_ref[2 * position : 2 * position + 1, lanes]
                sin_turn = turns_ref[2 * position + 1 : 2 * position + 2, lanes]
                if imag_part is None:
                    turned_real = real_part * cos_turn
                    turned_imag = -(real_part * sin_turn)
                elif index == turn:
                    turned_real = real_part * cos_turn + imag_part * sin_turn
                    turned_imag = imag_part * cos_turn - real_part * sin_turn
                else:
                    turned_real = real_part * cos_turn - imag_part * sin_turn
                    turned_imag = -(imag_part * cos_turn + real_part * sin_turn)
                target = pl.ds(position * row_count + first, 16)
                parts_ref[target, lanes] = turned_real.astype(jnp.bfloat16)
                parts_ref[target, imag_lanes] = turned_imag.astype(jnp.bfloat16)

    for group in range(row_count // 16):
        one_group(group)
    spectrum_ref[...] = jnp.dot(parts_ref[...], table_ref[...], preferred_element_type=jnp.float32)

    def whiten_group(group):
        first = group * 16
        rows = pl.ds(base_row + first, 16)
        total = jnp.zeros((16, DBINS), jnp.float32)
        for position in range(RADIX):
            source = pl.ds(position * row_count + first, 16)
            real_part, imag_part = spectrum_ref[source, :DBINS], spectrum_ref[source, DBINS:]
            total = total + (real_part * real_part + imag_part * imag_part)
        water_level = jnp.sum(total, axis=1, keepdims=True) * (1.0 / F)
        floor = 0.1 * water_level + 1e-06
        for position in range(RADIX):
            source = pl.ds(position * row_count + first, 16)
            real_part, imag_part = spectrum_ref[source, :DBINS], spectrum_ref[source, DBINS:]
            scaling = lax.rsqrt(real_part * real_part + imag_part * imag_part + floor)
            start = position * 2 * DBINS
            out_ref[rows, start : start + DBINS] = (real_part * scaling).astype(jnp.bfloat16)
            out_ref[rows, start + DBINS : start + 2 * DBINS] = (imag_part * scaling).astype(jnp.bfloat16)

    for group in range(row_count // 16):
        whiten_group(group)


def in_hbm(*arrays):
    return [pltpu.with_memory_space_constraint(array, pltpu.HBM) for array in arrays]


def gather_kernel(windows, wanted_ref, whitened_ref, rows_ref):
    slots = rows_ref.shape[0]
    owners, lanes_count = wanted_ref.shape
    stations = whitened_ref.shape[0] // windows
    owner_of = lax.broadcasted_iota(jnp.int32, (slots, owners), 0) // (windows * CAP)
    spread = jnp.where(owner_of == lax.broadcasted_iota(jnp.int32, (slots, owners), 1), 1.0, 0.0)
    lists = jnp.dot(
        spread.astype(jnp.bfloat16), wanted_ref[...].astype(jnp.bfloat16), preferred_element_type=jnp.float32
    )
    slot_ids = lax.broadcasted_iota(jnp.int32, (slots, lanes_count), 0)
    lanes = lax.broadcasted_iota(jnp.int32, (slots, lanes_count), 1)
    row_wanted = jnp.sum(jnp.where(lanes == slot_ids % CAP, lists, 0.0), axis=1, keepdims=True)
    source = row_wanted.astype(jnp.int32) + slot_ids // CAP % windows * stations
    picks = jnp.where(lanes == source, 1.0, 0.0).astype(whitened_ref.dtype)
    for start in range(0, rows_ref.shape[1], GATHER_COLUMNS):
        columns = slice(start, start + GATHER_COLUMNS)
        rows_ref[:, columns] = jnp.dot(
            picks, whitened_ref[:, columns], preferred_element_type=jnp.float32
        ).astype(rows_ref.dtype)


GATHER_COLUMNS = 512


def gathered(wanted, whitened, windows):
    slots = wanted.shape[0] * windows * CAP
    shape = (slots, whitened.shape[1])
    vmem = pl.BlockSpec(memory_space=pltpu.VMEM)
    return pl.pallas_call(
        functools.partial(gather_kernel, windows),
        out_shape=jax.ShapeDtypeStruct(shape, whitened.dtype),
        in_specs=[vmem, vmem],
        out_specs=vmem,
        compiler_params=pltpu.CompilerParams(vmem_limit_bytes=16 << 20),
        name="gathered",
    )(wanted, whitened)


PART_ROWS = 32
STEP_PARTS = 2


def whitened_spectra(traces):
    total = traces.shape[0]
    rows = PART_ROWS * STEP_PARTS
    table, turns = spectrum_tables()
    scratch = [
        pltpu.VMEM((RADIX * PART_ROWS, 2 * SUB), jnp.bfloat16),
        pltpu.VMEM((RADIX * PART_ROWS, 2 * DBINS), jnp.float32),
    ]
    return pl.pallas_call(
        spectrum_kernel,
        out_shape=jax.ShapeDtypeStruct((total, 2 * F), jnp.bfloat16),
        grid_spec=pltpu.PrefetchScalarGridSpec(
            num_scalar_prefetch=0,
            grid=(total // rows,),
            in_specs=[
                pl.BlockSpec((rows, NS), lambda s: (s, 0)),
                pl.BlockSpec((1, NS), lambda s: (0, 0)),
                pl.BlockSpec((2 * RADIX, SUB), lambda s: (0, 0)),
                pl.BlockSpec((2 * SUB, 2 * DBINS), lambda s: (0, 0)),
            ],
            out_specs=pl.BlockSpec((rows, 2 * F), lambda s: (s, 0)),
            scratch_shapes=scratch * STEP_PARTS,
        ),
        compiler_params=pltpu.CompilerParams(
            dimension_semantics=("arbitrary",), vmem_limit_bytes=24 << 20
        ),
        cost_estimate=pl.CostEstimate(
            flops=2 * total * RADIX * 2 * SUB * 2 * DBINS,
            bytes_accessed=5_000_000,
            transcendentals=total * F,
        ),
        name="whitened_spectra",
    )(*in_hbm(traces, jnp.asarray(hann_window()), jnp.asarray(turns), jnp.asarray(table)))


def lag_kernel(
    place_ref, places_ref, received_ref, inner_ref, outer_ref, kept_ref, sent_ref,
    select_ref, stacked_ref, turned_ref, sums_ref,
):
    slots = received_ref.shape[0]
    ends = places_ref.shape[0]
    pairs = ends // 2
    windows = select_ref.shape[0] // ends
    lanes = lax.broadcasted_iota(jnp.int32, (ends, 128), 1)
    places = places_ref[...]
    for window in range(windows):
        for tile in range(slots // 128):
            hit = jnp.where(places + window * CAP == lanes + tile * 128, 1.0, 0.0)
            rows = slice(window * ends, (window + 1) * ends)
            select_ref[rows, tile * 128 : (tile + 1) * 128] = hit.astype(jnp.bfloat16)

    bins = lax.broadcasted_iota(jnp.int32, (1, DBINS), 1)
    even = bins % 2 == 0
    flip_odd = jnp.where(even, 1.0, -1.0)
    flip_upper = jnp.where(bins % 4 < 2, 1.0, -1.0)
    residue_rows = RADIX * pairs
    for step in range(STEPS):
        columns = slice(step * 4 * DBINS, (step + 1) * 4 * DBINS)
        picked = jnp.dot(select_ref[...], received_ref[:, columns], preferred_element_type=jnp.float32)
        for half in range(2):
            real_columns = slice(half * 2 * DBINS, half * 2 * DBINS + DBINS)
            imag_columns = slice(half * 2 * DBINS + DBINS, (half + 1) * 2 * DBINS)
            real_sum = imag_sum = None
            for window in range(windows):
                left = slice(window * ends, window * ends + pairs)
                right = slice(window * ends + pairs, (window + 1) * ends)
                left_real, left_imag = picked[left, real_columns], picked[left, imag_columns]
                right_real, right_imag = picked[right, real_columns], picked[right, imag_columns]
                real_term = left_real * right_real + left_imag * right_imag
                imag_term = left_imag * right_real - left_real * right_imag
                real_sum = real_term if real_sum is None else real_sum + real_term
                imag_sum = imag_term if imag_sum is None else imag_sum + imag_term
            quarter_real = jnp.where(even, real_sum, -imag_sum) * flip_upper
            quarter_imag = jnp.where(even, imag_sum, real_sum) * flip_upper
            quarters = [
                (real_sum, imag_sum),
                (quarter_real, quarter_imag),
                (real_sum * flip_odd, imag_sum * flip_odd),
                (quarter_real * flip_odd, quarter_imag * flip_odd),
            ]
            position = 2 * step + half
            for quarter, (real_part, imag_part) in enumerate(quarters):
                first = quarter * residue_rows + position * pairs
                stacked_ref[first : first + pairs, :DBINS] = real_part.astype(jnp.bfloat16)
                stacked_ref[first : first + pairs, DBINS:] = imag_part.astype(jnp.bfloat16)

    turned_ref[...] = jnp.dot(stacked_ref[...], inner_ref[...], preferred_element_type=jnp.float32)

    for tile in range(SUB // 128):
        columns = slice(tile * 128, (tile + 1) * 128)
        for group in range(pairs // 8):
            real_of, imag_of = {}, {}
            for position, turn in enumerate(TURNS):
                first = tile * residue_rows + position * pairs + group * 8
                real_part, imag_part = turned_ref[first : first + 8, :DBINS], turned_ref[first : first + 8, DBINS:]
                cos_turn = outer_ref[2 * position : 2 * position + 1, columns]
                sin_turn = outer_ref[2 * position + 1 : 2 * position + 2, columns]
                real_of[turn] = real_part * cos_turn - imag_part * sin_turn
                if turn % STEPS:
                    imag_of[turn] = real_part * sin_turn + imag_part * cos_turn
            r0, r6 = real_of[0], real_of[6]
            re = [None] + [real_of[r] + real_of[RADIX - r] for r in range(1, STEPS)]
            im = [None] + [imag_of[r] - imag_of[RADIX - r] for r in range(1, STEPS)]
            even, odd = re[2] + re[4], re[1] + re[5]
            q_zero = (r0 + r6) + (even + odd + re[3])
            q_one_real = (r0 - r6) + 0.5 * (re[2] - re[4]) + ROOT3_2 * (re[1] - re[5])
            q_one_imag = 0.5 * (im[1] + im[5]) + ROOT3_2 * (im[2] + im[4]) + im[3]
            q_two_real = (r0 + r6) + 0.5 * (re[1] + re[5] - even) - re[3]
            q_two_imag = ROOT3_2 * (im[1] + im[2] - im[4] - im[5])
            periods = [q_two_real + q_two_imag, q_one_real + q_one_imag, q_zero, q_one_real - q_one_imag]
            for period, values in enumerate(periods):
                sums_ref[group * 8 : group * 8 + 8, period * SUB + tile * 128 : period * SUB + (tile + 1) * 128] = values

    rings = kept_ref.shape[0]
    share = kept_ref.shape[2]
    for offset in range(rings):
        ring = lax.rem(place_ref[0] + offset, rings)
        kept = pl.multiple_of((2 * ring + place_ref[1]) * share, share)
        sent = pl.multiple_of((2 * ring + 1 - place_ref[1]) * share, share)
        kept_ref[offset] = sums_ref[:, pl.ds(kept, share)]
        sent_ref[offset] = sums_ref[:, pl.ds(sent, share)].astype(sent_ref.dtype)


def lag_sums(place, places, received, parts, normalizer):
    ends = places.shape[0]
    slots = received.shape[0]
    pairs = ends // 2
    windows = slots // (32 * CAP)
    inner, outer = lag_tables(normalizer)
    share = 2 * LAG // parts
    vmem = pl.BlockSpec(memory_space=pltpu.VMEM)
    return pl.pallas_call(
        lag_kernel,
        out_shape=(
            jax.ShapeDtypeStruct((parts // 2, pairs, share), jnp.float32),
            jax.ShapeDtypeStruct((parts // 2, pairs, share), jnp.bfloat16),
        ),
        in_specs=[pl.BlockSpec(memory_space=pltpu.SMEM)] + [vmem] * 4,
        out_specs=(vmem, vmem),
        scratch_shapes=[
            pltpu.VMEM((windows * ends, slots), jnp.bfloat16),
            pltpu.VMEM((SUB // DBINS * RADIX * pairs, 2 * DBINS), jnp.bfloat16),
            pltpu.VMEM((SUB // DBINS * RADIX * pairs, 2 * DBINS), jnp.float32),
            pltpu.VMEM((pairs, 2 * LAG), jnp.float32),
        ],
        compiler_params=pltpu.CompilerParams(vmem_limit_bytes=32 << 20),
        cost_estimate=pl.CostEstimate(
            flops=2 * windows * ends * slots * 2 * F, bytes_accessed=5_000_000, transcendentals=0
        ),
        name="lag_sums",
    )(place, places, received, jnp.asarray(inner), jnp.asarray(outer))


def add_kernel(kept_ref, got_ref, own_ref, *sent_refs):
    own_ref[...] = kept_ref[0] + got_ref[0].astype(jnp.float32)
    for offset, sent_ref in enumerate(sent_refs, 1):
        sent_ref[...] = (kept_ref[offset] + got_ref[offset].astype(jnp.float32)).astype(sent_ref.dtype)


def total_kernel(own_ref, *rest):
    total = own_ref[...]
    for got_ref in rest[:-1]:
        total = total + got_ref[...].astype(jnp.float32)
    rest[-1][...] = total


def window_total(kept, sent):
    rings, pairs, share = kept.shape
    devices = range(2 * rings)
    got = lax.ppermute(sent, "tm", [(source, source ^ 1) for source in devices])
    params = pltpu.CompilerParams(vmem_limit_bytes=16 << 20)
    own, *onward = pl.pallas_call(
        add_kernel,
        out_shape=[jax.ShapeDtypeStruct((pairs, share), jnp.float32)]
        + [jax.ShapeDtypeStruct((pairs, share), jnp.bfloat16)] * (rings - 1),
        compiler_params=params,
        name="core_total",
    )(kept, got)
    arrived = []
    nearest_first = sorted(range(1, rings), key=lambda offset: min(offset, rings - offset))
    for offset in nearest_first:
        targets = [(source, (source // 2 + offset) % rings * 2 + source % 2) for source in devices]
        arrived.append(lax.ppermute(onward[offset - 1], "tm", targets))
    return pl.pallas_call(
        total_kernel,
        out_shape=jax.ShapeDtypeStruct((pairs, share), jnp.float32),
        compiler_params=params,
        name="window_total",
    )(own, *arrived).T


def on_device(traces, station_slot, pair_stations):
    window_count, station_count, length = traces.shape
    blocks = lax.axis_size("pairs")
    lag_parts = lax.axis_size("tm")
    slots = blocks * window_count * CAP
    normalizer = 1.0 / math.sqrt(F * window_count * lag_parts)
    own = lax.axis_index("tm")
    wanted, places = requests(station_slot, pair_stations, blocks, window_count, station_count)
    wanted, own = lax.optimization_barrier((wanted, own))
    lists = lax.all_to_all(wanted[:, None, :], "pairs", split_axis=0, concat_axis=0, tiled=True)
    place = jnp.stack([own // 2, own % 2]).astype(jnp.int32)
    lists, place = lax.optimization_barrier((lists, place))
    whitened = whitened_spectra(traces.reshape(window_count * station_count, length))
    rows = gathered(lists.reshape(wanted.shape), whitened, window_count)
    received = lax.all_to_all(
        rows.reshape(blocks, window_count * CAP, 2 * F), "pairs", split_axis=0, concat_axis=0, tiled=True
    )
    kept, sent = lag_sums(place, places, received.reshape(slots, 2 * F), lag_parts, normalizer)
    return window_total(kept, sent)


def solution(mesh):
    in_specs = (P("tm", "pairs", None), P(), P("pairs", None))
    out_specs = P("tm", "pairs")
    return jax.shard_map(
        on_device, mesh=mesh, in_specs=in_specs, out_specs=out_specs, check_vma=False
    )
```

```python
import functools
import math

import jax
import jax.numpy as jnp
import ml_dtypes
import numpy as np
from jax import lax
from jax.experimental import pallas as pl
from jax.experimental.pallas import tpu as pltpu
from jax.sharding import PartitionSpec as P

F = 1536
FLO = 32
LAG = 1024
NS = 6144
RADIX = 12
SUB = NS // RADIX
DBINS = F // RADIX
STEPS = RADIX // 2
CAP = 8
ROOT3_2 = math.sqrt(3.0) / 2.0

TURNS = [0, 6] + [turn for step in range(1, STEPS) for turn in (step, RADIX - step)]
RESIDUES = [(turn - FLO) % RADIX for turn in TURNS]


def spectrum_tables():
    sub_times = np.arange(SUB, dtype=np.int64)[:, None]
    bins = np.arange(DBINS, dtype=np.int64)[None, :]
    angles = (sub_times * bins % SUB) * (2.0 * np.pi / SUB)
    cos_part, sin_part = np.cos(angles), np.sin(angles)
    inner = np.block([[cos_part, -sin_part], [sin_part, cos_part]]).astype(ml_dtypes.bfloat16)
    first_bins = FLO + np.array(RESIDUES, dtype=np.int64)[:, None]
    turn_angles = (first_bins * sub_times[:, 0][None, :] % NS) * (2.0 * np.pi / NS)
    turns = np.stack([np.cos(turn_angles), np.sin(turn_angles)], axis=1)
    return inner, turns.reshape(2 * RADIX, SUB).astype(np.float32)


def hann_window():
    times = np.arange(NS, dtype=np.float64)
    return (0.5 - 0.5 * np.cos((times + 0.5) * (2.0 * np.pi / NS))).astype(np.float32)[None, :]


def lag_tables(normalizer):
    bins = np.arange(DBINS, dtype=np.int64)[:, None]
    sub_lags = np.arange(SUB, dtype=np.int64)[None, :]
    angles = (bins * sub_lags % SUB)[:, :DBINS] * (2.0 * np.pi / SUB)
    cos_part, sin_part = np.cos(angles), np.sin(angles)
    inner = np.block([[cos_part, sin_part], [-sin_part, cos_part]]).astype(ml_dtypes.bfloat16)
    first_bins = FLO + np.array(RESIDUES, dtype=np.int64)[:, None]
    outer_angles = (first_bins * sub_lags % NS) * (2.0 * np.pi / NS)
    outer = np.stack([np.cos(outer_angles), np.sin(outer_angles)], axis=1) * normalizer
    return inner, outer.reshape(2 * RADIX, SUB).astype(np.float32)


def request_kernel(windows, stations, slots_ref, pairs_ref, wanted_ref, places_ref):
    ends = 2 * pairs_ref.shape[1]
    owners_count = wanted_ref.shape[0]
    table_rows, width = slots_ref.shape
    sublane = lax.broadcasted_iota(jnp.int32, (ends, ends), 0)
    lane = lax.broadcasted_iota(jnp.int32, (ends, ends), 1)

    end_row = jnp.concatenate([pairs_ref[0:1, :], pairs_ref[1:2, :]], axis=1)
    high_row = end_row // width
    low_row = end_row - high_row * width
    owner_table = slots_ref[...] // stations
    local_table = slots_ref[...] - owner_table * stations
    both = jnp.concatenate([owner_table, local_table], axis=0).astype(jnp.float32).astype(jnp.bfloat16)
    at_low = jnp.where(lax.broadcasted_iota(jnp.int32, (width, ends), 0) == low_row, 1.0, 0.0)
    found = jnp.dot(both, at_low.astype(jnp.bfloat16), preferred_element_type=jnp.float32)
    at_high = lax.broadcasted_iota(jnp.int32, (table_rows, ends), 0) == high_row
    owner_row = jnp.sum(jnp.where(at_high, found[:table_rows], 0.0), axis=0, keepdims=True)
    local_row = jnp.sum(jnp.where(at_high, found[table_rows:], 0.0), axis=0, keepdims=True)
    owner_square = jnp.broadcast_to(owner_row, (ends, ends))
    earlier = (owner_square.T == owner_square) & (sublane < lane)
    rank_row = jnp.sum(jnp.where(earlier, 1.0, 0.0), axis=0, keepdims=True)
    owned = lax.broadcasted_iota(jnp.int32, (owners_count, ends), 0) == owner_row.astype(jnp.int32)
    ranked = jnp.where(sublane == rank_row.astype(jnp.int32), jnp.broadcast_to(local_row, (ends, ends)), 0.0)
    wanted_ref[...] = lax.dot_general(
        jnp.where(owned, 1.0, 0.0).astype(jnp.bfloat16),
        ranked.astype(jnp.bfloat16),
        (((1,), (1,)), ((), ())),
        preferred_element_type=jnp.float32,
    )
    place_row = owner_row * (windows * CAP) + rank_row
    places_ref[...] = jnp.broadcast_to(place_row, (ends, ends)).T.astype(jnp.int32)


def requests(station_slot, pair_stations, blocks, windows, stations):
    pair_count = pair_stations.shape[0]
    return pl.pallas_call(
        functools.partial(request_kernel, windows, stations),
        out_shape=(
            jax.ShapeDtypeStruct((blocks, 128), jnp.float32),
            jax.ShapeDtypeStruct((2 * pair_count, 128), jnp.int32),
        ),
        name="requests",
    )(station_slot.reshape(-1, 128), pair_stations.T)


def spectrum_kernel(traces_ref, hann_ref, turns_ref, table_ref, out_ref, *scratch):
    count = len(scratch) // 2
    row_count = traces_ref.shape[0] // count
    tables = (hann_ref, turns_ref, table_ref)
    for part in range(count):
        transform_rows(part * row_count, row_count, traces_ref, *tables, out_ref, *scratch[2 * part : 2 * part + 2])


def transform_rows(
    base_row, row_count, traces_ref, hann_ref, turns_ref, table_ref, out_ref, parts_ref, spectrum_ref
):

    def one_group(group):
        first = group * 16
        rows = pl.ds(base_row + first, 16)
        partial_sum = traces_ref[rows, 0:128]
        for tile in range(1, NS // 128):
            partial_sum = partial_sum + traces_ref[rows, tile * 128 : (tile + 1) * 128]
        mean = jnp.sum(partial_sum, axis=1, keepdims=True) * (1.0 / NS)
        for tile in range(SUB // 128):
            x = []
            for block in range(RADIX):
                columns = slice(block * SUB + tile * 128, block * SUB + (tile + 1) * 128)
                x.append((traces_ref[rows, columns] - mean) * hann_ref[:, columns])
            u = [None] + [x[a] + x[RADIX - a] for a in range(1, 6)]
            v = [None] + [x[a] - x[RADIX - a] for a in range(1, 6)]
            e0, o0 = x[0] + x[6], x[0] - x[6]
            p, q = u[1] + u[5], u[2] + u[4]
            pd, qd = u[1] - u[5], u[2] - u[4]
            m, n = v[1] - v[5], v[2] - v[4]
            ms, ns = v[1] + v[5], v[2] + v[4]
            half_pq, half_diff = 0.5 * (p + q), 0.5 * (p - q)
            e_plus, e_minus = e0 + u[3], e0 - u[3]
            base = o0 + 0.5 * qd
            side = ROOT3_2 * pd
            imag_base = 0.5 * ms + v[3]
            imag_side = ROOT3_2 * ns
            real_parts = [
                e_plus + (p + q),
                base + side,
                e_minus + half_diff,
                o0 - qd,
                e_plus - half_pq,
                base - side,
                e_minus - (p - q),
            ]
            imag_parts = [
                None,
                -(imag_base + imag_side),
                -ROOT3_2 * (m + n),
                v[3] - ms,
                -ROOT3_2 * (m - n),
                imag_side - imag_base,
                None,
            ]
            lanes = slice(tile * 128, (tile + 1) * 128)
            imag_lanes = slice(SUB + tile * 128, SUB + (tile + 1) * 128)
            for position, turn in enumerate(TURNS):
                index = min(turn, RADIX - turn)
                real_part, imag_part = real_parts[index], imag_parts[index]
                cos_turn = turns_ref[2 * position : 2 * position + 1, lanes]
                sin_turn = turns_ref[2 * position + 1 : 2 * position + 2, lanes]
                if imag_part is None:
                    turned_real = real_part * cos_turn
                    turned_imag = -(real_part * sin_turn)
                elif index == turn:
                    turned_real = real_part * cos_turn + imag_part * sin_turn
                    turned_imag = imag_part * cos_turn - real_part * sin_turn
                else:
                    turned_real = real_part * cos_turn - imag_part * sin_turn
                    turned_imag = -(imag_part * cos_turn + real_part * sin_turn)
                target = pl.ds(position * row_count + first, 16)
                parts_ref[target, lanes] = turned_real.astype(jnp.bfloat16)
                parts_ref[target, imag_lanes] = turned_imag.astype(jnp.bfloat16)

    for group in range(row_count // 16):
        one_group(group)
    spectrum_ref[...] = jnp.dot(parts_ref[...], table_ref[...], preferred_element_type=jnp.float32)

    def whiten_group(group):
        first = group * 16
        rows = pl.ds(base_row + first, 16)
        total = jnp.zeros((16, DBINS), jnp.float32)
        for position in range(RADIX):
            source = pl.ds(position * row_count + first, 16)
            real_part, imag_part = spectrum_ref[source, :DBINS], spectrum_ref[source, DBINS:]
            total = total + (real_part * real_part + imag_part * imag_part)
        water_level = jnp.sum(total, axis=1, keepdims=True) * (1.0 / F)
        floor = 0.1 * water_level + 1e-06
        for position in range(RADIX):
            source = pl.ds(position * row_count + first, 16)
            real_part, imag_part = spectrum_ref[source, :DBINS], spectrum_ref[source, DBINS:]
            scaling = lax.rsqrt(real_part * real_part + imag_part * imag_part + floor)
            start = position * 2 * DBINS
            out_ref[rows, start : start + DBINS] = (real_part * scaling).astype(jnp.bfloat16)
            out_ref[rows, start + DBINS : start + 2 * DBINS] = (imag_part * scaling).astype(jnp.bfloat16)

    for group in range(row_count // 16):
        whiten_group(group)


def in_hbm(*arrays):
    return [pltpu.with_memory_space_constraint(array, pltpu.HBM) for array in arrays]


def gather_kernel(windows, wanted_ref, whitened_ref, rows_ref):
    slots = rows_ref.shape[0]
    owners, lanes_count = wanted_ref.shape
    stations = whitened_ref.shape[0] // windows
    owner_of = lax.broadcasted_iota(jnp.int32, (slots, owners), 0) // (windows * CAP)
    spread = jnp.where(owner_of == lax.broadcasted_iota(jnp.int32, (slots, owners), 1), 1.0, 0.0)
    lists = jnp.dot(
        spread.astype(jnp.bfloat16), wanted_ref[...].astype(jnp.bfloat16), preferred_element_type=jnp.float32
    )
    slot_ids = lax.broadcasted_iota(jnp.int32, (slots, lanes_count), 0)
    lanes = lax.broadcasted_iota(jnp.int32, (slots, lanes_count), 1)
    row_wanted = jnp.sum(jnp.where(lanes == slot_ids % CAP, lists, 0.0), axis=1, keepdims=True)
    source = row_wanted.astype(jnp.int32) + slot_ids // CAP % windows * stations
    picks = jnp.where(lanes == source, 1.0, 0.0).astype(whitened_ref.dtype)
    for start in range(0, rows_ref.shape[1], GATHER_COLUMNS):
        columns = slice(start, start + GATHER_COLUMNS)
        rows_ref[:, columns] = jnp.dot(
            picks, whitened_ref[:, columns], preferred_element_type=jnp.float32
        ).astype(rows_ref.dtype)


GATHER_COLUMNS = 512


def gathered(wanted, whitened, windows):
    slots = wanted.shape[0] * windows * CAP
    shape = (slots, whitened.shape[1])
    vmem = pl.BlockSpec(memory_space=pltpu.VMEM)
    return pl.pallas_call(
        functools.partial(gather_kernel, windows),
        out_shape=jax.ShapeDtypeStruct(shape, whitened.dtype),
        in_specs=[vmem, vmem],
        out_specs=vmem,
        compiler_params=pltpu.CompilerParams(vmem_limit_bytes=16 << 20),
        name="gathered",
    )(wanted, whitened)


PART_ROWS = 32
STEP_PARTS = 2


def whitened_spectra(traces):
    total = traces.shape[0]
    rows = PART_ROWS * STEP_PARTS
    table, turns = spectrum_tables()
    scratch = [
        pltpu.VMEM((RADIX * PART_ROWS, 2 * SUB), jnp.bfloat16),
        pltpu.VMEM((RADIX * PART_ROWS, 2 * DBINS), jnp.float32),
    ]
    return pl.pallas_call(
        spectrum_kernel,
        out_shape=jax.ShapeDtypeStruct((total, 2 * F), jnp.bfloat16),
        grid_spec=pltpu.PrefetchScalarGridSpec(
            num_scalar_prefetch=0,
            grid=(total // rows,),
            in_specs=[
                pl.BlockSpec((rows, NS), lambda s: (s, 0)),
                pl.BlockSpec((1, NS), lambda s: (0, 0)),
                pl.BlockSpec((2 * RADIX, SUB), lambda s: (0, 0)),
                pl.BlockSpec((2 * SUB, 2 * DBINS), lambda s: (0, 0)),
            ],
            out_specs=pl.BlockSpec((rows, 2 * F), lambda s: (s, 0)),
            scratch_shapes=scratch * STEP_PARTS,
        ),
        compiler_params=pltpu.CompilerParams(
            dimension_semantics=("arbitrary",), vmem_limit_bytes=24 << 20
        ),
        cost_estimate=pl.CostEstimate(
            flops=2 * total * RADIX * 2 * SUB * 2 * DBINS,
            bytes_accessed=5_000_000,
            transcendentals=total * F,
        ),
        name="whitened_spectra",
    )(*in_hbm(traces, jnp.asarray(hann_window()), jnp.asarray(turns), jnp.asarray(table)))


def lag_kernel(
    place_ref, places_ref, received_ref, inner_ref, outer_ref, kept_ref, sent_ref,
    select_ref, stacked_ref, turned_ref, sums_ref,
):
    slots = received_ref.shape[0]
    ends = places_ref.shape[0]
    pairs = ends // 2
    windows = select_ref.shape[0] // ends
    lanes = lax.broadcasted_iota(jnp.int32, (ends, 128), 1)
    places = places_ref[...]
    for window in range(windows):
        for tile in range(slots // 128):
            hit = jnp.where(places + window * CAP == lanes + tile * 128, 1.0, 0.0)
            rows = slice(window * ends, (window + 1) * ends)
            select_ref[rows, tile * 128 : (tile + 1) * 128] = hit.astype(jnp.bfloat16)

    bins = lax.broadcasted_iota(jnp.int32, (1, DBINS), 1)
    even = bins % 2 == 0
    flip_odd = jnp.where(even, 1.0, -1.0)
    flip_upper = jnp.where(bins % 4 < 2, 1.0, -1.0)
    residue_rows = RADIX * pairs
    for step in range(STEPS):
        columns = slice(step * 4 * DBINS, (step + 1) * 4 * DBINS)
        picked = jnp.dot(select_ref[...], received_ref[:, columns], preferred_element_type=jnp.float32)
        for half in range(2):
            real_columns = slice(half * 2 * DBINS, half * 2 * DBINS + DBINS)
            imag_columns = slice(half * 2 * DBINS + DBINS, (half + 1) * 2 * DBINS)
            real_sum = imag_sum = None
            for window in range(windows):
                left = slice(window * ends, window * ends + pairs)
                right = slice(window * ends + pairs, (window + 1) * ends)
                left_real, left_imag = picked[left, real_columns], picked[left, imag_columns]
                right_real, right_imag = picked[right, real_columns], picked[right, imag_columns]
                real_term = left_real * right_real + left_imag * right_imag
                imag_term = left_imag * right_real - left_real * right_imag
                real_sum = real_term if real_sum is None else real_sum + real_term
                imag_sum = imag_term if imag_sum is None else imag_sum + imag_term
            quarter_real = jnp.where(even, real_sum, -imag_sum) * flip_upper
            quarter_imag = jnp.where(even, imag_sum, real_sum) * flip_upper
            quarters = [
                (real_sum, imag_sum),
                (quarter_real, quarter_imag),
                (real_sum * flip_odd, imag_sum * flip_odd),
                (quarter_real * flip_odd, quarter_imag * flip_odd),
            ]
            position = 2 * step + half
            for quarter, (real_part, imag_part) in enumerate(quarters):
                first = quarter * residue_rows + position * pairs
                stacked_ref[first : first + pairs, :DBINS] = real_part.astype(jnp.bfloat16)
                stacked_ref[first : first + pairs, DBINS:] = imag_part.astype(jnp.bfloat16)

    turned_ref[...] = jnp.dot(stacked_ref[...], inner_ref[...], preferred_element_type=jnp.float32)

    for tile in range(SUB // 128):
        columns = slice(tile * 128, (tile + 1) * 128)
        for group in range(pairs // 8):
            real_of, imag_of = {}, {}
            for position, turn in enumerate(TURNS):
                first = tile * residue_rows + position * pairs + group * 8
                real_part, imag_part = turned_ref[first : first + 8, :DBINS], turned_ref[first : first + 8, DBINS:]
                cos_turn = outer_ref[2 * position : 2 * position + 1, columns]
                sin_turn = outer_ref[2 * position + 1 : 2 * position + 2, columns]
                real_of[turn] = real_part * cos_turn - imag_part * sin_turn
                if turn % STEPS:
                    imag_of[turn] = real_part * sin_turn + imag_part * cos_turn
            r0, r6 = real_of[0], real_of[6]
            re = [None] + [real_of[r] + real_of[RADIX - r] for r in range(1, STEPS)]
            im = [None] + [imag_of[r] - imag_of[RADIX - r] for r in range(1, STEPS)]
            even, odd = re[2] + re[4], re[1] + re[5]
            q_zero = (r0 + r6) + (even + odd + re[3])
            q_one_real = (r0 - r6) + 0.5 * (re[2] - re[4]) + ROOT3_2 * (re[1] - re[5])
            q_one_imag = 0.5 * (im[1] + im[5]) + ROOT3_2 * (im[2] + im[4]) + im[3]
            q_two_real = (r0 + r6) + 0.5 * (re[1] + re[5] - even) - re[3]
            q_two_imag = ROOT3_2 * (im[1] + im[2] - im[4] - im[5])
            periods = [q_two_real + q_two_imag, q_one_real + q_one_imag, q_zero, q_one_real - q_one_imag]
            for period, values in enumerate(periods):
                sums_ref[group * 8 : group * 8 + 8, period * SUB + tile * 128 : period * SUB + (tile + 1) * 128] = values

    rings = kept_ref.shape[0]
    share = kept_ref.shape[2]
    for offset in range(rings):
        ring = lax.rem(place_ref[0] + offset, rings)
        kept = pl.multiple_of((2 * ring + place_ref[1]) * share, share)
        sent = pl.multiple_of((2 * ring + 1 - place_ref[1]) * share, share)
        kept_ref[offset] = sums_ref[:, pl.ds(kept, share)]
        sent_ref[offset] = sums_ref[:, pl.ds(sent, share)].astype(sent_ref.dtype)


def lag_sums(place, places, received, parts, normalizer):
    ends = places.shape[0]
    slots = received.shape[0]
    pairs = ends // 2
    windows = slots // (32 * CAP)
    inner, outer = lag_tables(normalizer)
    share = 2 * LAG // parts
    vmem = pl.BlockSpec(memory_space=pltpu.VMEM)
    return pl.pallas_call(
        lag_kernel,
        out_shape=(
            jax.ShapeDtypeStruct((parts // 2, pairs, share), jnp.float32),
            jax.ShapeDtypeStruct((parts // 2, pairs, share), jnp.bfloat16),
        ),
        in_specs=[pl.BlockSpec(memory_space=pltpu.SMEM)] + [vmem] * 4,
        out_specs=(vmem, vmem),
        scratch_shapes=[
            pltpu.VMEM((windows * ends, slots), jnp.bfloat16),
            pltpu.VMEM((SUB // DBINS * RADIX * pairs, 2 * DBINS), jnp.bfloat16),
            pltpu.VMEM((SUB // DBINS * RADIX * pairs, 2 * DBINS), jnp.float32),
            pltpu.VMEM((pairs, 2 * LAG), jnp.float32),
        ],
        compiler_params=pltpu.CompilerParams(vmem_limit_bytes=32 << 20),
        cost_estimate=pl.CostEstimate(
            flops=2 * windows * ends * slots * 2 * F, bytes_accessed=5_000_000, transcendentals=0
        ),
        name="lag_sums",
    )(place, places, received, jnp.asarray(inner), jnp.asarray(outer))


def add_kernel(kept_ref, got_ref, own_ref, *sent_refs):
    own_ref[...] = kept_ref[0] + got_ref[0].astype(jnp.float32)
    for offset, sent_ref in enumerate(sent_refs, 1):
        sent_ref[...] = (kept_ref[offset] + got_ref[offset].astype(jnp.float32)).astype(sent_ref.dtype)


def total_kernel(own_ref, *rest):
    total = own_ref[...]
    for got_ref in rest[:-1]:
        total = total + got_ref[...].astype(jnp.float32)
    rest[-1][...] = total


def window_total(kept, sent):
    rings, pairs, share = kept.shape
    devices = range(2 * rings)
    got = lax.ppermute(sent, "tm", [(source, source ^ 1) for source in devices])
    params = pltpu.CompilerParams(vmem_limit_bytes=16 << 20)
    own, *onward = pl.pallas_call(
        add_kernel,
        out_shape=[jax.ShapeDtypeStruct((pairs, share), jnp.float32)]
        + [jax.ShapeDtypeStruct((pairs, share), jnp.bfloat16)] * (rings - 1),
        compiler_params=params,
        name="core_total",
    )(kept, got)
    arrived = []
    for offset, values in enumerate(onward, 1):
        targets = [(source, (source // 2 + offset) % rings * 2 + source % 2) for source in devices]
        arrived.append(lax.ppermute(values, "tm", targets))
    return pl.pallas_call(
        total_kernel,
        out_shape=jax.ShapeDtypeStruct((pairs, share), jnp.float32),
        compiler_params=params,
        name="window_total",
    )(own, *arrived).T


def on_device(traces, station_slot, pair_stations):
    window_count, station_count, length = traces.shape
    blocks = lax.axis_size("pairs")
    lag_parts = lax.axis_size("tm")
    slots = blocks * window_count * CAP
    normalizer = 1.0 / math.sqrt(F * window_count * lag_parts)
    own = lax.axis_index("tm")
    wanted, places = requests(station_slot, pair_stations, blocks, window_count, station_count)
    wanted, own = lax.optimization_barrier((wanted, own))
    lists = lax.all_to_all(wanted[:, None, :], "pairs", split_axis=0, concat_axis=0, tiled=True)
    place = jnp.stack([own // 2, own % 2]).astype(jnp.int32)
    lists, place = lax.optimization_barrier((lists, place))
    whitened = whitened_spectra(traces.reshape(window_count * station_count, length))
    rows = gathered(lists.reshape(wanted.shape), whitened, window_count)
    received = lax.all_to_all(
        rows.reshape(blocks, window_count * CAP, 2 * F), "pairs", split_axis=0, concat_axis=0, tiled=True
    )
    kept, sent = lag_sums(place, places, received.reshape(slots, 2 * F), lag_parts, normalizer)
    return window_total(kept, sent)


def solution(mesh):
    in_specs = (P("tm", "pairs", None), P(), P("pairs", None))
    out_specs = P("tm", "pairs")
    return jax.shard_map(
        on_device, mesh=mesh, in_specs=in_specs, out_specs=out_specs, check_vma=False
    )
```
